32 devices in a mesh: batch: 8 (over z, y), tensor: 4 (over x, core).
Axes of the slice: x: 2, y: 2, z: 4, core: 2. Of those that a mesh axis runs over, the one named last changes fastest.
Arguments:
- tokens: bfloat16 [12288, 768], P('batch'), may hold values from -6 to 6
- lengths: int32 [8], P('batch'), may hold values from 1024 to 1536, as said below
- w_query: bfloat16 [768, 768], P('batch', 'tensor'), may hold values from -0.4375 to 0.4375
- w_key: bfloat16 [768, 768], P('batch', 'tensor'), may hold values from -0.21875 to 0.21875
- w_value: bfloat16 [768, 768], P('batch', 'tensor'), may hold values from -0.21875 to 0.21875
- w_out: bfloat16 [768, 768], P('tensor', 'batch'), may hold values from -0.875 to 0.875
- w_up: bfloat16 [768, 3072], P('batch', 'tensor'), may hold values from -0.21875 to 0.21875
- w_down: bfloat16 [3072, 768], P('tensor', 'batch'), may hold values from -0.109375 to 0.109375
- norm_gain: bfloat16 [2, 768], P(None, 'batch'), may hold values from 0.099609375 to 1.8984375
- norm_shift: bfloat16 [2, 768], P(None, 'batch'), may hold values from -3 to 3
- out_grad: bfloat16 [12288, 768], P('batch'), may hold values from -6 to 6
Outputs:
- layer_out: bfloat16 [12288, 768], P('batch')
- grad_input: bfloat16 [12288, 768], P('batch')
- grad_query: float32 [768, 768], P('batch', 'tensor')
- grad_key: float32 [768, 768], P('batch', 'tensor')
- grad_value: float32 [768, 768], P('batch', 'tensor')
- grad_out: float32 [768, 768], P('tensor', 'batch')
- grad_up: float32 [768, 3072], P('batch', 'tensor')
- grad_down: float32 [3072, 768], P('tensor', 'batch')
- grad_gain: float32 [2, 768], P(None, 'batch')
- grad_shift: float32 [2, 768], P(None, 'batch')
The draws below stay inside these ranges and needn't reach their ends.
Inputs may be any that keep to these rules, and one draw needn't show every extreme that they name: `lengths`: each sequence's valid tokens; some sequence fills all 1536 slots.
All inputs are finite; a program needn't handle non-finite values.
Results may differ from the reference program's by a relative error of at most 0.017.
Values may be sent and summed in bfloat16 or wider, within the bound.
No kernel may reach another device: no remote copies, remote signals or barrier semaphores. Data moves between devices by JAX's collectives and lax.ppermute only.
A program may use at most 192 MiB of HBM per device.

```python
import jax
import jax.numpy as jnp
from jax import lax

D = 768
HD = 64
FF = 3072
LEN = 1536
SEQS = 8
TOKENS = 12288


def draw_lengths(key, part):
    sampled = jax.random.randint(jax.random.fold_in(key, 11), (SEQS,), LEN * 2 // 3, LEN + 1)
    chosen = jax.random.randint(jax.random.fold_in(key, 12), (), 0, SEQS)
    return jnp.where(jnp.arange(SEQS) == chosen, LEN, sampled).astype(jnp.int32)


def block_scale(stream_key, shape, split, least, largest):
    level = 1.0
    for dim, blocks in split:
        steps = jax.random.uniform(jax.random.fold_in(jax.random.fold_in(stream_key, 6), dim), (blocks,), jnp.float32, least / len(split), largest / len(split))
        level = level * jnp.repeat(jnp.exp(steps), shape[dim] // blocks).reshape((-1,) + (1,) * (len(shape) - 1 - dim))
    return level


def scatter_about(rng, shape, scale, bound, cuts=(), kind=jnp.bfloat16):
    drawn = jax.random.normal(rng, shape, jnp.float32) * scale
    if len(cuts) > 0:
        drawn = block_scale(rng, shape, cuts, -0.22, 0.18) * drawn
    return jnp.clip(drawn, min=-bound, max=bound).astype(kind)


def setup_inputs(seed: int = 0) -> dict:
    splits = jax.random.split(jax.random.key(seed), 12)
    tokens = scatter_about(splits[0], (TOKENS, D), 1.0, 6.0, ((0, 8),))
    lengths = draw_lengths(jax.random.fold_in(splits[11], 71), 0)
    w_query = scatter_about(splits[2], (D, D), (D // 4) ** -0.5, 0.4375, ((0, 8), (1, 4)))
    w_key = scatter_about(splits[3], (D, D), D ** -0.5, 0.21875, ((0, 8), (1, 4)))
    w_value = scatter_about(splits[4], (D, D), D ** -0.5, 0.21875, ((0, 8), (1, 4)))
    w_out = scatter_about(splits[5], (D, D), (D // 16) ** -0.5, 0.875, ((0, 4), (1, 8)))
    w_up = scatter_about(splits[6], (D, FF), D ** -0.5, 0.21875, ((0, 8), (1, 4)))
    w_down = scatter_about(splits[7], (FF, D), FF ** -0.5, 0.109375, ((0, 4), (1, 8)))
    norm_gain = jnp.clip(1.0 + 0.18 * jax.random.normal(splits[8], (2, D), jnp.float32), 0.099609375, 1.8984375).astype(jnp.bfloat16)
    norm_shift = scatter_about(splits[9], (2, D), 0.3, 3.0, ((1, 8),))
    out_grad = scatter_about(splits[10], (TOKENS, D), 1.0, 6.0, ((0, 8),))
    return dict(tokens=tokens, lengths=lengths, w_query=w_query, w_key=w_key, w_value=w_value, w_out=w_out, w_up=w_up, w_down=w_down, norm_gain=norm_gain, norm_shift=norm_shift, out_grad=out_grad)


epsilon = 1e-05
highest = lax.Precision.HIGHEST

@jax.custom_vjp
def low(v):
    return lax.optimization_barrier(v.astype(jnp.bfloat16)).astype(jnp.float32)

@jax.custom_vjp
def low_back(v):
    return v

def low_keep(v):
    return (low(v), None)

def low_pass(kept, grad):
    return (grad,)

def back_keep(v):
    return (v, None)

def back_low(kept, grad):
    return (low(grad),)
low.defvjp(low_keep, low_pass)
low_back.defvjp(back_keep, back_low)

def normalize(values, gain_row, shift_row):
    middle = lax.optimization_barrier(jnp.mean(values, axis=-1, keepdims=True))
    centred = values - middle
    spread = lax.optimization_barrier(jnp.mean(centred * centred, axis=-1, keepdims=True))
    return centred * lax.rsqrt(spread + epsilon) * gain_row + shift_row

def product(left_mat, right_mat):
    return jnp.dot(left_mat, right_mat, precision=highest)

def sequence_layer(inputs, length, params):
    w_query, w_key, w_value, w_out, w_up, w_down, gain_rows, shift_rows = params
    seq_rows = inputs.shape[0]
    head_count = w_query.shape[1] // HD
    position = jnp.arange(seq_rows, dtype=jnp.int32)
    is_valid = (position < length).astype(jnp.float32)
    normed = low(normalize(inputs, gain_rows[0], shift_rows[0]))
    queries = low_back(low(product(normed, w_query))).reshape(seq_rows, head_count, HD)
    key_rows = low_back(low(product(normed, w_key))).reshape(seq_rows, head_count, HD)
    value_rows = low_back(low(product(normed, w_value))).reshape(seq_rows, head_count, HD)
    raw_scores = low_back(jnp.einsum('qhd,khd->hqk', queries, key_rows, precision=highest))
    scores = raw_scores * float(HD) ** (-0.5)
    allowed = (position[None, :] <= position[:, None]) & (position[None, :] < length)
    magnitude = jnp.where(allowed[None], jnp.abs(scores), -1e+30)
    weights = low(jnp.sign(scores) * jax.nn.softmax(magnitude, axis=-1))
    mixed_heads = jnp.einsum('hqk,khd->qhd', weights, value_rows, precision=highest).reshape(seq_rows, -1)
    mixed_heads = low_back(low(mixed_heads))
    hidden = inputs + low_back(product(mixed_heads, w_out))
    normed_two = low(normalize(hidden, gain_rows[1], shift_rows[1]))
    up_proj = low_back(product(normed_two, w_up))
    active = low(jax.nn.gelu(up_proj, approximate=True))
    branch = low_back(product(active, w_down))
    return (hidden + branch) * is_valid[:, None]

def reference(tokens, lengths, w_query, w_key, w_value, w_out, w_up, w_down, norm_gain, norm_shift, out_grad):
    params = tuple((weight_arg.astype(jnp.float32) for weight_arg in (w_query, w_key, w_value, w_out, w_up, w_down, norm_gain, norm_shift)))
    inputs = tokens.astype(jnp.float32).reshape(SEQS, LEN, D)
    cotangent = out_grad.astype(jnp.float32).reshape(SEQS, LEN, D)

    def forward(inputs, params):

        def single(seq_pair):
            return jax.checkpoint(sequence_layer)(seq_pair[0], seq_pair[1], params)
        return lax.map(single, (inputs, lengths))
    outputs, pullback = jax.vjp(forward, inputs, params)
    grad_inputs, grad_params = pullback(cotangent)
    return (outputs.reshape(TOKENS, D).astype(jnp.bfloat16), grad_inputs.reshape(TOKENS, D).astype(jnp.bfloat16), grad_params[0], grad_params[1], grad_params[2], grad_params[3], grad_params[4], grad_params[5], grad_params[6], grad_params[7])
```

```python
import functools

import jax
import jax.numpy as jnp
from jax import lax
from jax.experimental import pallas as pl
from jax.experimental.pallas import tpu as pltpu
from jax.sharding import PartitionSpec as P

HD = 64
EPSILON = 1e-05
LOG2E = 1.4426950408889634
HUGE = 3e38
FAR = -1e30
LOW = jnp.bfloat16
WIDE = jnp.float32
LANES = 128


def multiply(left, right):
    return lax.dot_general(left, right, (((1,), (0,)), ((), ())), preferred_element_type=WIDE)


def outer_cols(left, right):
    return lax.dot_general(left, right, (((1,), (1,)), ((), ())), preferred_element_type=WIDE)


def inner_rows(left, right):
    return lax.dot_general(left, right, (((0,), (0,)), ((), ())), preferred_element_type=WIDE)


def whole():
    return pl.BlockSpec(memory_space=pltpu.VMEM)


def scalars():
    return pl.BlockSpec(memory_space=pltpu.SMEM)


def struct(shape, dtype):
    return jax.ShapeDtypeStruct(shape, dtype)


def swap(value, axis, bits):
    size = lax.axis_size(axis)
    return lax.ppermute(value, axis, [(i, i ^ bits) for i in range(size)])


def gather_batch(shard):
    size = lax.axis_size("batch")
    if size != 8:
        return lax.all_gather(shard, "batch", axis=0, tiled=True)
    rows = shard.shape[0]
    me = lax.axis_index("batch")
    pieces = {0: shard}
    for bits in (2, 4, 6):
        pieces[bits] = swap(shard, "batch", bits)
    for bits in (0, 2, 4, 6):
        pieces[bits + 1] = swap(pieces[bits], "batch", 1)
    full = jnp.zeros((size * rows, shard.shape[1]), shard.dtype)
    for bits, piece in pieces.items():
        full = lax.dynamic_update_slice(full, piece, ((me ^ bits) * rows, 0))
    return full


def scatter_batch(value):
    size = lax.axis_size("batch")
    parts = value.reshape(size, value.shape[0] // size, value.shape[1])
    parts = lax.all_to_all(parts, "batch", 0, 0, tiled=True)
    return jnp.sum(parts.astype(WIDE), axis=0)


def gather_tensor(piece):
    across = swap(piece, "tensor", 2)
    beside = swap(piece, "tensor", 1)
    both = swap(across, "tensor", 1)
    return piece, across, beside, both


def pair_sum(keep, send):
    mine = (keep.astype(WIDE) + swap(send, "tensor", 1).astype(WIDE)).astype(LOW)
    return mine, swap(mine, "tensor", 2)


def standardize(values):
    middle = jnp.mean(values, axis=-1, keepdims=True)
    centred = values - middle
    spread = jnp.mean(centred * centred, axis=-1, keepdims=True)
    inverse = lax.rsqrt(spread + EPSILON)
    return centred * inverse, inverse


def standardize_back(grad, scaled, inverse, gain):
    grad = grad * gain
    mean_grad = jnp.mean(grad, axis=-1, keepdims=True)
    mean_cross = jnp.mean(grad * scaled, axis=-1, keepdims=True)
    return inverse * (grad - mean_grad - scaled * mean_cross)


def project_kernel(tokens_ref, weights_ref, normed_ref, queries_ref, keys_ref, values_ref, rows_ref, *, width):
    first = (3 * width) // LANES * LANES
    offset = 3 * width - first

    @pl.when(pl.program_id(0) == 0)
    def _():
        columns = weights_ref[:, first : first + LANES].astype(WIDE)
        rows_ref[...] = jnp.transpose(columns)[offset : offset + 8, :]

    scaled, _ = standardize(tokens_ref[...].astype(WIDE))
    normed = (scaled * rows_ref[0:1, :] + rows_ref[2:3, :]).astype(LOW)
    normed_ref[...] = normed
    projected = multiply(normed, weights_ref[:, : 3 * width]).astype(LOW)
    queries_ref[...] = projected[:, :width]
    keys_ref[...] = projected[:, width : 2 * width]
    values_ref[...] = projected[:, 2 * width :]


def project(tokens, weights, width, block):
    count, depth = tokens.shape
    return pl.pallas_call(
        functools.partial(project_kernel, width=width),
        grid=(count // block,),
        in_specs=[pl.BlockSpec((block, depth), lambda i: (i, 0)), whole()],
        out_specs=(
            pl.BlockSpec((block, depth), lambda i: (i, 0)),
            pl.BlockSpec((block, width), lambda i: (i, 0)),
            pl.BlockSpec((block, width), lambda i: (i, 0)),
            pl.BlockSpec((block, width), lambda i: (i, 0)),
            pl.BlockSpec((8, depth), lambda i: (0, 0)),
        ),
        out_shape=(
            struct((count, depth), LOW),
            struct((count, width), LOW),
            struct((count, width), LOW),
            struct((count, width), LOW),
            struct((8, depth), WIDE),
        ),
        compiler_params=pltpu.CompilerParams(vmem_limit_bytes=24 << 20),
        name="project",
    )(tokens, weights)


def sign_of(scores):
    return jnp.minimum(jnp.maximum(scores * HUGE, -1.0), 1.0)


def attend_kernel(length_ref, q_ref, k_ref, v_ref, mixed_ref, sums_ref, *, begin, rows, block, heads, sure):
    length = length_ref[0]
    factor = LOG2E * HD**-0.5
    for i in range(rows // block):
        row0 = begin + i * block
        outs = []
        sums = []
        for h in range(heads):
            cols = slice(h * HD, (h + 1) * HD)
            q = q_ref[i * block : (i + 1) * block, cols]
            row = lax.broadcasted_iota(jnp.int32, (block, 1), 0) + row0
            key = lax.broadcasted_iota(jnp.int32, (block, block), 1) + row0
            near = outer_cols(q, k_ref[row0 : row0 + block, cols])
            near_size = jnp.where(key <= jnp.minimum(row, length - 1), jnp.abs(near) * factor, FAR)
            top = jnp.max(near_size, axis=1, keepdims=True)
            if row0 > 0:
                past = outer_cols(q, k_ref[:row0, cols])
                past_size = jnp.abs(past) * factor
                if row0 > sure:
                    past_key = lax.broadcasted_iota(jnp.int32, (block, row0), 1)
                    past_size = jnp.where(past_key < length, past_size, FAR)
                top = jnp.maximum(top, jnp.max(past_size, axis=1, keepdims=True))
                past_prob = jnp.exp2(past_size - top)
            near_prob = jnp.exp2(near_size - top)
            total = jnp.sum(near_prob, axis=1, keepdims=True)
            mixed = multiply((near_prob * sign_of(near)).astype(LOW), v_ref[row0 : row0 + block, cols])
            if row0 > 0:
                total = total + jnp.sum(past_prob, axis=1, keepdims=True)
                mixed = mixed + multiply((past_prob * sign_of(past)).astype(LOW), v_ref[:row0, cols])
            outs.append((mixed / total).astype(LOW))
            sums.append(top + jnp.log2(total))
        mixed_ref[i * block : (i + 1) * block, :] = jnp.concatenate(outs, axis=1)
        blank = jnp.zeros((block, LANES - heads), WIDE)
        sums_ref[i] = jnp.transpose(jnp.concatenate(sums + [blank], axis=1))[:8, :]


def attend(queries, keys, values, lengths, begin, rows, block, sure):
    width = keys.shape[1]
    heads = width // HD
    return pl.pallas_call(
        functools.partial(attend_kernel, begin=begin, rows=rows, block=block, heads=heads, sure=sure),
        in_specs=[scalars(), whole(), whole(), whole()],
        out_specs=(whole(), whole()),
        out_shape=(struct((rows, width), LOW), struct((rows // block, 8, block), WIDE)),
        compiler_params=pltpu.CompilerParams(vmem_limit_bytes=32 << 20),
        name="attend_forward",
    )(lengths, queries, keys, values)


def attend_back_kernel(
    length_ref, q_ref, k_ref, v_ref, g_ref, mixed_ref, sums_ref, dq_ref, dk_ref, dv_ref, delta, dq_turned, *, rows, block, heads, sure
):
    length = length_ref[0]
    scaling = HD**-0.5
    factor = LOG2E * scaling
    blocks = rows // block
    for i in range(blocks):
        part = slice(i * block, (i + 1) * block)
        both = g_ref[part, :].astype(WIDE) * mixed_ref[part, :].astype(WIDE)
        cols = [jnp.sum(both[:, h * HD : (h + 1) * HD], axis=1, keepdims=True) for h in range(heads)]
        blank = jnp.zeros((block, LANES - heads), WIDE)
        delta[i] = jnp.transpose(jnp.concatenate(cols + [blank], axis=1))[:8, :]
    dq_turned[...] = jnp.zeros_like(dq_turned)
    for j in range(blocks):
        key0 = j * block

        def body(i, carry, near):
            row0 = i * block if near else pl.multiple_of(i * block, block)
            dks, dvs = [], []
            for h in range(heads):
                cols = slice(h * HD, (h + 1) * HD)
                q = q_ref[pl.ds(row0, block), cols]
                g = g_ref[pl.ds(row0, block), cols]
                k = k_ref[key0 : key0 + block, cols]
                v = v_ref[key0 : key0 + block, cols]
                scores = outer_cols(k, q)
                grad_weights = outer_cols(v, g)
                size = jnp.abs(scores) * factor - sums_ref[i, h : h + 1, :]
                key = lax.broadcasted_iota(jnp.int32, (block, block), 0) + key0
                if near:
                    row = lax.broadcasted_iota(jnp.int32, (1, block), 1) + row0
                    size = jnp.where(key <= jnp.minimum(row, length - 1), size, FAR)
                elif key0 + block > sure:
                    size = jnp.where(key < length, size, FAR)
                sign = sign_of(scores)
                weights = jnp.exp2(size) * sign
                raw = (weights * (sign * grad_weights - delta[i, h : h + 1, :])).astype(LOW)
                dvs.append(carry[1][h] + multiply(weights.astype(LOW), g))
                dks.append(carry[0][h] + multiply(raw, q))
                dq_turned[cols, pl.ds(row0, block)] += inner_rows(k, raw)
            return tuple(dks), tuple(dvs)

        blank = tuple(jnp.zeros((block, HD), WIDE) for _ in range(heads))
        carry = body(j, (blank, blank), True)
        if j + 1 < blocks:
            carry = lax.fori_loop(j + 1, blocks, lambda i, kept: body(i, kept, False), carry)
        dks, dvs = carry
        part = slice(key0, key0 + block)
        dk_ref[part, :] = jnp.concatenate([dk * scaling for dk in dks], axis=1).astype(LOW)
        dv_ref[part, :] = jnp.concatenate(dvs, axis=1).astype(LOW)
    for i in range(blocks):
        part = slice(i * block, (i + 1) * block)
        dq_ref[part, :] = (jnp.transpose(dq_turned[:, part]) * scaling).astype(LOW)


def attend_back(queries, keys, values, grad_mixed, mixed, sums, lengths, block, sure):
    rows, width = keys.shape
    heads = width // HD
    return pl.pallas_call(
        functools.partial(attend_back_kernel, rows=rows, block=block, heads=heads, sure=sure),
        in_specs=[scalars()] + [whole()] * 6,
        out_specs=(whole(),) * 3,
        out_shape=(struct((rows, width), LOW),) * 3,
        scratch_shapes=[pltpu.VMEM((rows // block, 8, block), WIDE), pltpu.VMEM((width, rows), WIDE)],
        compiler_params=pltpu.CompilerParams(vmem_limit_bytes=32 << 20),
        name="attend_backward",
    )(lengths, queries, keys, values, grad_mixed, mixed, sums)


def gelu_pair(up):
    root = 0.7978845608028654
    square = up * up
    bent = jnp.tanh(root * up * (1.0 + 0.044715 * square))
    half = 0.5 * (1.0 + bent)
    slope = half + 0.5 * up * (1.0 - bent * bent) * (root * (1.0 + 3 * 0.044715 * square))
    return up * half, slope


def feed_kernel(
    scalar_ref, tokens_ref, grad_ref, m0, m1, m2, m3, o0, o1, o2, o3, up_ref, down_ref, rows_ref,
    keep_ref, send_ref, hidden_ref, normed_ref, active_ref, upper_ref, sums_ref, mixed_ref, *, block, blocks,
):
    i = pl.program_id(0)
    half = blocks // 2
    core = scalar_ref[0]
    row0 = lax.rem(i + (1 - core) * half, blocks) * block
    row = lax.broadcasted_iota(jnp.int32, (block, 1), 0) + row0
    @pl.when(scalar_ref[2] == 0)
    def _():
        across = outer_cols(m0[...], o0[...]) + outer_cols(m1[...], o1[...])
        mixed_ref[...] = across + outer_cols(m2[...], o2[...]) + outer_cols(m3[...], o3[...])

    @pl.when(scalar_ref[2] != 0)
    def _():
        across = outer_cols(m1[...], o1[...]) + outer_cols(m0[...], o0[...])
        mixed_ref[...] = across + outer_cols(m3[...], o3[...]) + outer_cols(m2[...], o2[...])

    hidden = tokens_ref[...].astype(WIDE) + mixed_ref[...]
    scaled, _ = standardize(hidden)
    normed = (scaled * rows_ref[1:2, :] + rows_ref[3:4, :]).astype(LOW)
    normed_ref[...] = normed
    grad = jnp.where(row < scalar_ref[1], grad_ref[...].astype(WIDE), 0.0).astype(LOW)
    active, slope = gelu_pair(multiply(normed, up_ref[...]))
    active_ref[...] = active.astype(LOW)
    upper = (multiply(grad, down_ref[...]) * slope).astype(LOW)
    upper_ref[...] = upper
    back = outer_cols(upper, up_ref[...])

    @pl.when(i == 0)
    def _():
        sums_ref[...] = jnp.zeros_like(sums_ref)

    sums_ref[0:1, :] += jnp.sum(back * scaled, axis=0, keepdims=True)
    sums_ref[1:2, :] += jnp.sum(back, axis=0, keepdims=True)

    @pl.when(i < half)
    def _():
        send_ref[...] = back.astype(LOW)

    @pl.when(i >= half)
    def _():
        keep_ref[...] = back.astype(LOW)
        hidden_ref[...] = hidden


def feed(pair, tokens, out_grad, mixed, outs, up, down, rows, block):
    count, depth = tokens.shape
    hidden_units = up.shape[1]
    width = mixed[0].shape[1]
    blocks = count // block
    half = blocks // 2

    def turned(i, scalar_ref):
        return (lax.rem(i + (1 - scalar_ref[0]) * half, blocks), 0)

    def fixed(i, scalar_ref):
        return (0, 0)

    def row_block(columns):
        return pl.BlockSpec((block, columns), turned)

    def kept(i, scalar_ref):
        return (jnp.maximum(i - half, 0), 0)

    def sent(i, scalar_ref):
        return (jnp.minimum(i, half - 1), 0)

    return pl.pallas_call(
        functools.partial(feed_kernel, block=block, blocks=blocks),
        grid_spec=pltpu.PrefetchScalarGridSpec(
            num_scalar_prefetch=1,
            grid=(blocks,),
            in_specs=[row_block(depth), row_block(depth)]
            + [row_block(width)] * 4
            + [whole()] * 7,
            out_specs=(
                pl.BlockSpec((block, depth), kept),
                pl.BlockSpec((block, depth), sent),
                pl.BlockSpec((block, depth), kept),
                row_block(depth),
                row_block(hidden_units),
                row_block(hidden_units),
                pl.BlockSpec((8, depth), fixed),
            ),
            scratch_shapes=[pltpu.VMEM((block, depth), WIDE)],
        ),
        out_shape=(
            struct((count // 2, depth), LOW),
            struct((count // 2, depth), LOW),
            struct((count // 2, depth), WIDE),
            struct((count, depth), LOW),
            struct((count, hidden_units), LOW),
            struct((count, hidden_units), LOW),
            struct((8, depth), WIDE),
        ),
        compiler_params=pltpu.CompilerParams(vmem_limit_bytes=40 << 20),
        name="feed_forward",
    )(pair, tokens, out_grad, *mixed, *outs, up, down, rows)


def second_back_kernel(scalar_ref, mine_ref, other_ref, hidden_ref, grad_ref, rows_ref, wide_ref, low_ref, *, block, blocks):
    row0 = (pl.program_id(0) + scalar_ref[0] * blocks) * block
    row = lax.broadcasted_iota(jnp.int32, (block, 1), 0) + row0
    grad_normed = mine_ref[...].astype(WIDE) + other_ref[...].astype(WIDE)
    scaled, inverse = standardize(hidden_ref[...])
    grad = jnp.where(row < scalar_ref[1], grad_ref[...].astype(WIDE), 0.0)
    grad = grad + standardize_back(grad_normed, scaled, inverse, rows_ref[1:2, :])
    wide_ref[...] = grad
    low_ref[...] = grad.astype(LOW)


def second_back(pair, mine, other, hidden, out_grad, rows, block):
    count, depth = hidden.shape
    blocks = count // block

    def own(i, scalar_ref):
        return (i, 0)

    def placed(i, scalar_ref):
        return (i + scalar_ref[0] * blocks, 0)

    return pl.pallas_call(
        functools.partial(second_back_kernel, block=block, blocks=blocks),
        grid_spec=pltpu.PrefetchScalarGridSpec(
            num_scalar_prefetch=1,
            grid=(blocks,),
            in_specs=[pl.BlockSpec((block, depth), own)] * 3 + [pl.BlockSpec((block, depth), placed), whole()],
            out_specs=(pl.BlockSpec((block, depth), own),) * 2,
        ),
        out_shape=(struct((count, depth), WIDE), struct((count, depth), LOW)),
        compiler_params=pltpu.CompilerParams(vmem_limit_bytes=24 << 20),
        name="second_norm_backward",
    )(pair, mine, other, hidden, out_grad, rows)


def inward_kernel(scalar_ref, dq_ref, dk_ref, dv_ref, tokens_ref, weights_ref, keep_ref, send_ref, sums_ref, *, blocks, width):
    i = pl.program_id(0)
    half = blocks // 2
    back = outer_cols(dq_ref[...], weights_ref[:, :width])
    back = back + outer_cols(dk_ref[...], weights_ref[:, width : 2 * width])
    back = back + outer_cols(dv_ref[...], weights_ref[:, 2 * width : 3 * width])
    scaled, _ = standardize(tokens_ref[...].astype(WIDE))

    @pl.when(i == 0)
    def _():
        sums_ref[...] = jnp.zeros_like(sums_ref)

    sums_ref[0:1, :] += jnp.sum(back * scaled, axis=0, keepdims=True)
    sums_ref[1:2, :] += jnp.sum(back, axis=0, keepdims=True)

    @pl.when(i < half)
    def _():
        send_ref[...] = back.astype(LOW)

    @pl.when(i >= half)
    def _():
        keep_ref[...] = back.astype(LOW)


def inward(pair, dq, dk, dv, tokens, weights, block):
    count, depth = tokens.shape
    width = dq.shape[1]
    blocks = count // block
    half = blocks // 2

    def turned(i, scalar_ref):
        return (lax.rem(i + (1 - scalar_ref[0]) * half, blocks), 0)

    def kept(i, scalar_ref):
        return (jnp.maximum(i - half, 0), 0)

    def sent(i, scalar_ref):
        return (jnp.minimum(i, half - 1), 0)

    return pl.pallas_call(
        functools.partial(inward_kernel, blocks=blocks, width=width),
        grid_spec=pltpu.PrefetchScalarGridSpec(
            num_scalar_prefetch=1,
            grid=(blocks,),
            in_specs=[pl.BlockSpec((block, width), turned)] * 3 + [pl.BlockSpec((block, depth), turned), whole()],
            out_specs=(
                pl.BlockSpec((block, depth), kept),
                pl.BlockSpec((block, depth), sent),
                pl.BlockSpec((8, depth), lambda i, scalar_ref: (0, 0)),
            ),
        ),
        out_shape=(
            struct((count // 2, depth), LOW),
            struct((count // 2, depth), LOW),
            struct((8, depth), WIDE),
        ),
        compiler_params=pltpu.CompilerParams(vmem_limit_bytes=24 << 20),
        name="grad_normed",
    )(pair, dq, dk, dv, tokens, weights)


def first_back_kernel(scalar_ref, mine_ref, other_ref, tokens_ref, grad_ref, rows_ref, own_ref, full_ref):
    grad_normed = mine_ref[...].astype(WIDE) + other_ref[...].astype(WIDE)
    scaled, inverse = standardize(tokens_ref[...].astype(WIDE))
    grad = grad_ref[...] + standardize_back(grad_normed, scaled, inverse, rows_ref[0:1, :])
    low = grad.astype(LOW)
    own_ref[...] = low
    full_ref[...] = low


def first_back(pair, mine, other, tokens, grad_hidden, rows, block):
    count, depth = grad_hidden.shape
    blocks = count // block

    def own(i, scalar_ref):
        return (i, 0)

    def placed(i, scalar_ref):
        return (i + scalar_ref[0] * blocks, 0)

    return pl.pallas_call(
        first_back_kernel,
        grid_spec=pltpu.PrefetchScalarGridSpec(
            num_scalar_prefetch=1,
            grid=(blocks,),
            in_specs=[
                pl.BlockSpec((block, depth), own),
                pl.BlockSpec((block, depth), own),
                pl.BlockSpec((block, depth), placed),
                pl.BlockSpec((block, depth), own),
                whole(),
            ],
            out_specs=(pl.BlockSpec((block, depth), own), pl.BlockSpec((block, depth), placed)),
        ),
        out_shape=(struct((count, depth), LOW), struct((2 * count, depth), LOW)),
        compiler_params=pltpu.CompilerParams(vmem_limit_bytes=24 << 20),
        name="first_norm_backward",
    )(pair, mine, other, tokens, grad_hidden, rows)


def per_device(tokens, lengths, w_query, w_key, w_value, w_out, w_up, w_down, norm_gain, norm_shift, out_grad):
    count, depth = tokens.shape
    if lengths.shape[0] != 1 or lax.axis_size("tensor") != 4:
        raise ValueError("unsupported mesh")
    width = w_query.shape[1]
    core = lax.axis_index("tensor") & 1
    half = count // 2
    pair = jnp.stack([core.astype(jnp.int32), lengths[0], (lax.axis_index("tensor") >> 1).astype(jnp.int32)])
    block = 256
    sure = 2 * count // 3

    blank = jnp.zeros((w_query.shape[0], -(3 * width + 4) % LANES), LOW)
    early = jnp.concatenate([w_query, w_key, w_value, norm_gain.T, norm_shift.T, blank], axis=1)
    early = gather_batch(early)
    w_out_turned = gather_batch(w_out.T)
    late = gather_batch(jnp.concatenate([w_up, w_down.T], axis=1))
    full_up = late[:, : w_up.shape[1]]
    full_down = late[:, w_up.shape[1] :]
    outs = gather_tensor(w_out_turned)

    normed, queries, keys, values, rows = project(tokens, early, width, block)
    mixed, sums = attend(queries, keys, values, lengths, 0, count, block, sure)
    pieces = gather_tensor(mixed)
    keep, send, hidden, normed_two, active, upper, sums_two = feed(
        pair, tokens, out_grad, pieces, outs, full_up, full_down, rows, block
    )
    mine, other = pair_sum(keep, send)
    is_valid = (jnp.arange(count, dtype=jnp.int32) < lengths[0])[:, None]
    grad_rows = jnp.where(is_valid, out_grad, jnp.zeros_like(out_grad))
    branch = outer_cols(active, full_down).astype(LOW)
    shard_up = scatter_batch(inner_rows(normed_two, upper).astype(LOW))
    shard_down = scatter_batch(inner_rows(grad_rows, active).astype(LOW)).T

    grad_hidden, grad_attn = second_back(pair, mine, other, hidden, out_grad, rows, block)
    beside = swap(grad_attn, "tensor", 1)
    grad_attn = jnp.where(
        core == 0, jnp.concatenate([grad_attn, beside]), jnp.concatenate([beside, grad_attn])
    )
    grad_mixed = multiply(grad_attn, w_out_turned).astype(LOW)
    shard_out = scatter_batch(inner_rows(grad_attn, mixed).astype(LOW)).T
    dq, dk, dv = attend_back(queries, keys, values, grad_mixed, mixed, sums, lengths, block, sure)

    branch_keep = lax.dynamic_slice(branch, (core * half, 0), (half, depth))
    branch_send = lax.dynamic_slice(branch, ((1 - core) * half, 0), (half, depth))
    branch_mine, branch_other = pair_sum(branch_keep, branch_send)
    own_valid = lax.dynamic_slice(is_valid, (core * half, 0), (half, 1))
    own_out = hidden + (branch_mine.astype(WIDE) + branch_other.astype(WIDE))
    own_out = jnp.where(own_valid, own_out, 0.0).astype(LOW)
    other_out = swap(own_out, "tensor", 1)
    layer_out = jnp.where(
        core == 0, jnp.concatenate([own_out, other_out]), jnp.concatenate([other_out, own_out])
    )

    keep, send, sums_one = inward(pair, dq, dk, dv, tokens, early, block)
    mine, other = pair_sum(keep, send)
    own_grad, grad_input = first_back(pair, mine, other, tokens, grad_hidden, rows, block)
    grad_input = lax.dynamic_update_slice(grad_input, swap(own_grad, "tensor", 1), ((1 - core) * half, 0))

    turned = jnp.stack([sums_one[0], sums_two[0], sums_one[1], sums_two[1]]).T
    grads = inner_rows(normed, jnp.concatenate([dq, dk, dv], axis=1))
    blank = jnp.zeros((depth, early.shape[1] - 3 * width - 4), WIDE)
    grads = scatter_batch(jnp.concatenate([grads, turned, blank], axis=1).astype(LOW))
    small = grads[:, 3 * width : 3 * width + 4]
    small = small + swap(small, "tensor", 2)
    small = (small + swap(small, "tensor", 1)).T
    return (
        layer_out,
        grad_input,
        grads[:, :width],
        grads[:, width : 2 * width],
        grads[:, 2 * width : 3 * width],
        shard_out,
        shard_up,
        shard_down,
        small[:2],
        small[2:],
    )


def solution(mesh):
    tall = P("batch", "tensor")
    wide = P("tensor", "batch")
    rows = P("batch", None)
    pair = P(None, "batch")
    return jax.shard_map(
        per_device,
        mesh=mesh,
        in_specs=(rows, P("batch"), tall, tall, tall, wide, tall, wide, pair, pair, rows),
        out_specs=(rows, rows, tall, tall, tall, wide, tall, wide, pair, pair),
        check_vma=False,
    )
```

```python
import functools

import jax
import jax.numpy as jnp
from jax import lax
from jax.experimental import pallas as pl
from jax.experimental.pallas import tpu as pltpu
from jax.sharding import PartitionSpec as P

HD = 64
EPSILON = 1e-05
LOG2E = 1.4426950408889634
HUGE = 3e38
FAR = -1e30
LOW = jnp.bfloat16
WIDE = jnp.float32
LANES = 128
BLOCK = 256


def multiply(left, right):
    return lax.dot_general(left, right, (((1,), (0,)), ((), ())), preferred_element_type=WIDE)


def outer_cols(left, right):
    return lax.dot_general(left, right, (((1,), (1,)), ((), ())), preferred_element_type=WIDE)


def inner_rows(left, right):
    return lax.dot_general(left, right, (((0,), (0,)), ((), ())), preferred_element_type=WIDE)


def whole():
    return pl.BlockSpec(memory_space=pltpu.VMEM)


def scalars():
    return pl.BlockSpec(memory_space=pltpu.SMEM)


def struct(shape, dtype):
    return jax.ShapeDtypeStruct(shape, dtype)


def held(shape, dtype):
    return pltpu.VMEM(shape, dtype)


def stored_far(shape, dtype):
    return pltpu.HBM(shape, dtype)


def params(mebibytes):
    return pltpu.CompilerParams(vmem_limit_bytes=mebibytes << 20)


def cost(microseconds):
    return pl.CostEstimate(flops=int(microseconds * 1.1e9), bytes_accessed=0, transcendentals=0)


def after(value, *others):
    return lax.optimization_barrier((value, *others))[0]


def swap(value, axis, bits):
    size = lax.axis_size(axis)
    return lax.ppermute(value, axis, [(i, i ^ bits) for i in range(size)])


def gather_far(shard):
    return [swap(shard, "batch", bits) for bits in (2, 4, 6)]


def pair_sum(keep, send):
    mine = (keep.astype(WIDE) + swap(send, "tensor", 1).astype(WIDE)).astype(LOW)
    return mine, swap(mine, "tensor", 2)


def standardize(values):
    middle = jnp.mean(values, axis=-1, keepdims=True)
    centred = values - middle
    spread = jnp.mean(centred * centred, axis=-1, keepdims=True)
    inverse = lax.rsqrt(spread + EPSILON)
    return centred * inverse, inverse


def standardize_back(grad, scaled, inverse, gain):
    grad = grad * gain
    mean_grad = jnp.mean(grad, axis=-1, keepdims=True)
    mean_cross = jnp.mean(grad * scaled, axis=-1, keepdims=True)
    return inverse * (grad - mean_grad - scaled * mean_cross)


def collect(index, pieces, scratch):
    count = pieces[0].shape[0]
    for bits, piece in enumerate(pieces):
        at = pl.multiple_of((index ^ bits) * count, 32) if len(pieces) > 1 else 0
        scratch[pl.ds(at, count), :] = piece[...]


def project_kernel(scalar_ref, *refs, parts, width):
    pieces, refs = refs[:parts], refs[parts:]
    tokens_ref, normed_ref, projected_ref, rows_ref, weights_ref, outs_ref = refs

    @pl.when(pl.program_id(0) == 0)
    def _():
        collect(scalar_ref[3], pieces, weights_ref)
        rows_ref[...] = jnp.transpose(weights_ref[:, 4 * width : 4 * width + LANES].astype(WIDE))[:8, :]
        outs_ref[...] = jnp.transpose(weights_ref[:, 3 * width : 4 * width])

    scaled, _ = standardize(tokens_ref[...].astype(WIDE))
    normed = (scaled * rows_ref[0:1, :] + rows_ref[2:3, :]).astype(LOW)
    normed_ref[...] = normed
    projected_ref[...] = multiply(normed, weights_ref[:, : 3 * width]).astype(LOW)


def project(scalar, tokens, pieces, width):
    count, depth = tokens.shape
    total = pieces[0].shape[1]
    return pl.pallas_call(
        functools.partial(project_kernel, parts=len(pieces), width=width),
        grid=(count // BLOCK,),
        in_specs=[scalars()]
        + [whole()] * len(pieces)
        + [pl.BlockSpec((BLOCK, depth), lambda i: (i, 0))],
        out_specs=(
            pl.BlockSpec((BLOCK, depth), lambda i: (i, 0)),
            pl.BlockSpec((BLOCK, 3 * width), lambda i: (i, 0)),
            pl.BlockSpec((8, depth), lambda i: (0, 0)),
            pl.BlockSpec((depth, total), lambda i: (0, 0)),
            pl.BlockSpec((width, depth), lambda i: (0, 0)),
        ),
        out_shape=(
            stored_far((count, depth), LOW),
            struct((count, 3 * width), LOW),
            struct((8, depth), WIDE),
            struct((depth, total), LOW),
            struct((width, depth), LOW),
        ),
        compiler_params=params(14),
        cost_estimate=cost(4),
        name="project",
    )(scalar, *pieces, pltpu.with_memory_space_constraint(tokens, pltpu.HBM))


def assemble_kernel(scalar_ref, *refs, parts, units):
    pieces, (up_ref, down_ref) = refs[:parts], refs[parts:]
    count = pieces[0].shape[0]
    for bits, piece in enumerate(pieces):
        at = pl.multiple_of((scalar_ref[3] ^ bits) * count, 32) if parts > 1 else 0
        up_ref[pl.ds(at, count), :] = piece[:, :units]
        down_ref[pl.ds(at, count), :] = piece[:, units:]


def assemble(scalar, pieces, units):
    depth = sum(piece.shape[0] for piece in pieces)
    return pl.pallas_call(
        functools.partial(assemble_kernel, parts=len(pieces), units=units),
        in_specs=[scalars()] + [whole()] * len(pieces),
        out_specs=(whole(),) * 2,
        out_shape=(struct((depth, units), LOW), struct((depth, units), LOW)),
        compiler_params=params(10),
        cost_estimate=cost(1),
        name="assemble",
    )(scalar, *pieces)


def sign_of(scores):
    scores = scores.astype(LOW) * LOW(HUGE)
    return jnp.minimum(jnp.maximum(scores, LOW(-1)), LOW(1))


def attend_kernel(scalar_ref, projected_ref, mixed_ref, sums_ref, *, places, heads, sure):
    length = scalar_ref[1]
    factor = LOG2E * HD**-0.5
    width = heads * HD
    for i, place in enumerate(places):
        row0 = place * BLOCK
        here = slice(row0, row0 + BLOCK)
        row = lax.broadcasted_iota(jnp.int32, (BLOCK, 1), 0) + row0
        key = lax.broadcasted_iota(jnp.int32, (BLOCK, BLOCK), 1) + row0
        allowed = key <= jnp.minimum(row, length - 1)
        def each(function):
            return jnp.concatenate([function(h) for h in range(heads)], axis=0)

        def column(kind, h):
            return slice(kind * width + h * HD, kind * width + (h + 1) * HD)

        def split(value, h):
            return value[h * BLOCK : (h + 1) * BLOCK]

        near = each(lambda h: outer_cols(projected_ref[here, column(0, h)], projected_ref[here, column(1, h)]))
        near_size = jnp.where(jnp.concatenate([allowed] * heads, axis=0), jnp.abs(near) * factor, FAR)
        top = jnp.max(near_size, axis=1, keepdims=True)
        if row0 > 0:
            past = each(lambda h: outer_cols(projected_ref[here, column(0, h)], projected_ref[:row0, column(1, h)]))
            past_size = jnp.abs(past) * factor
            if row0 > sure:
                past_key = lax.broadcasted_iota(jnp.int32, (1, row0), 1)
                past_size = jnp.where(past_key < length, past_size, FAR)
            top = jnp.maximum(top, jnp.max(past_size, axis=1, keepdims=True))
            past_prob = jnp.exp2(past_size - top)
            past_signed = past_prob.astype(LOW) * sign_of(past)
        near_prob = jnp.exp2(near_size - top)
        near_signed = near_prob.astype(LOW) * sign_of(near)
        total = jnp.sum(near_prob, axis=1, keepdims=True)
        mixed = each(lambda h: multiply(split(near_signed, h), projected_ref[here, column(2, h)]))
        if row0 > 0:
            total = total + jnp.sum(past_prob, axis=1, keepdims=True)
            mixed = mixed + each(lambda h: multiply(split(past_signed, h), projected_ref[:row0, column(2, h)]))
        mixed = (mixed / total).astype(LOW)
        logs = top + jnp.log2(total)
        outs = [split(mixed, h) for h in range(heads)]
        sums = [split(logs, h) for h in range(heads)]
        part = slice(i * BLOCK, (i + 1) * BLOCK)
        mixed_ref[:, part] = jnp.transpose(jnp.concatenate(outs, axis=1))
        blank = jnp.zeros((BLOCK, LANES - heads), WIDE)
        sums_ref[i] = jnp.transpose(jnp.concatenate(sums + [blank], axis=1))[:8, :]


def attend(scalar, projected, places, sure):
    width = projected.shape[1] // 3
    heads = width // HD
    return pl.pallas_call(
        functools.partial(attend_kernel, places=places, heads=heads, sure=sure),
        in_specs=[scalars(), whole()],
        out_specs=(whole(), whole()),
        out_shape=(struct((width, len(places) * BLOCK), LOW), struct((len(places), 8, BLOCK), WIDE)),
        compiler_params=params(16),
        cost_estimate=cost(sum(places) / 2 + 1),
        name="attend_forward",
    )(scalar, projected)


def attend_back_kernel(scalar_ref, *refs, chunks, rows, heads, sure):
    length = scalar_ref[1]
    core = scalar_ref[0]
    projected_ref, outs_ref, refs = refs[0], refs[1], refs[2:]
    mixed_refs, refs = refs[: len(chunks)], refs[len(chunks) :]
    sums_refs, refs = refs[: len(chunks)], refs[len(chunks) :]
    grad_refs, refs = refs[: 2 * len(chunks)], refs[2 * len(chunks) :]
    grads_ref, outs_grad_ref, whole_ref, grad_mixed, delta, logs, dq_turned = refs
    scaling = HD**-0.5
    factor = LOG2E * scaling
    width = heads * HD
    blocks = rows // BLOCK
    outs_grad = jnp.zeros(outs_ref.shape, WIDE)
    half = blocks // 2
    for number, (begin, size) in enumerate(chunks):
        for side in range(2):
            for k in range(size // BLOCK):
                local = side * size + k * BLOCK
                inside = slice(local, local + BLOCK)
                i = side * half + begin // BLOCK + k
                rows_i = slice(i * BLOCK, (i + 1) * BLOCK)
                mine = grad_refs[2 * number][k * BLOCK : (k + 1) * BLOCK, :]
                other = grad_refs[2 * number + 1][k * BLOCK : (k + 1) * BLOCK, :]

                @pl.when(core == side)
                def _():
                    whole_ref[rows_i, :] = mine

                @pl.when(core != side)
                def _():
                    whole_ref[rows_i, :] = other

                grad = whole_ref[rows_i, :]
                mixed = mixed_refs[number][:, inside]
                outs_grad = outs_grad + multiply(mixed, grad)
                turned = outer_cols(outs_ref[...], grad)
                grad_mixed[rows_i, :] = jnp.transpose(turned).astype(LOW)
                logs[:, rows_i] = sums_refs[number][local // BLOCK]
                both = turned.astype(LOW).astype(WIDE) * mixed.astype(WIDE)
                for h in range(heads):
                    delta[h : h + 1, rows_i] = jnp.sum(both[h * HD : (h + 1) * HD, :], axis=0, keepdims=True)
    outs_grad_ref[...] = jnp.transpose(outs_grad).astype(LOW)
    for j in range(blocks):
        here = slice(j * BLOCK, (j + 1) * BLOCK)
        later = slice((j + 1) * BLOCK, rows)
        dks, dvs = [], []
        for h in range(heads):
            cols = slice(h * HD, (h + 1) * HD)
            k = projected_ref[here, width + h * HD : width + (h + 1) * HD]
            v = projected_ref[here, 2 * width + h * HD : 2 * width + (h + 1) * HD]
            dk = jnp.zeros((BLOCK, HD), WIDE)
            dv = jnp.zeros((BLOCK, HD), WIDE)
            for part in (here, later):
                span = part.stop - part.start
                if span == 0:
                    continue
                q = projected_ref[part, cols]
                g = grad_mixed[part, cols]
                scores = outer_cols(k, q)
                grad_weights = outer_cols(v, g)
                reach = jnp.abs(scores) * factor - logs[h : h + 1, part]
                if part is here:
                    key = lax.broadcasted_iota(jnp.int32, (BLOCK, span), 0) + j * BLOCK
                    row = lax.broadcasted_iota(jnp.int32, (1, span), 1) + j * BLOCK
                    reach = jnp.where(key <= jnp.minimum(row, length - 1), reach, FAR)
                elif (j + 1) * BLOCK > sure:
                    key = lax.broadcasted_iota(jnp.int32, (BLOCK, 1), 0) + j * BLOCK
                    reach = jnp.where(key < length, reach, FAR)
                sign = sign_of(scores)
                weights = jnp.exp2(reach)
                signed = sign.astype(WIDE)
                raw = (weights * (grad_weights - signed * delta[h : h + 1, part])).astype(LOW) * (sign * sign)
                dv = dv + multiply(weights.astype(LOW) * sign, g)
                dk = dk + multiply(raw, q)
                more = inner_rows(k, raw)
                if j == 0:
                    dq_turned[cols, part] = more
                else:
                    dq_turned[cols, part] += more
            dks.append(dk * scaling)
            dvs.append(dv)
        grads_ref[:width, here] = (dq_turned[:, here] * scaling).astype(LOW)
        grads_ref[width : 2 * width, here] = jnp.transpose(jnp.concatenate(dks, axis=1)).astype(LOW)
        grads_ref[2 * width :, here] = jnp.transpose(jnp.concatenate(dvs, axis=1)).astype(LOW)


def attend_back(scalar, projected, outs, mixed, sums, grads, chunks, sure):
    rows = projected.shape[0]
    width = projected.shape[1] // 3
    depth = outs.shape[1]
    heads = width // HD
    return pl.pallas_call(
        functools.partial(attend_back_kernel, chunks=chunks, rows=rows, heads=heads, sure=sure),
        in_specs=[scalars()] + [whole()] * (2 + 4 * len(chunks)),
        out_specs=(whole(),) * 3,
        out_shape=(struct((3 * width, rows), LOW), struct((depth, width), LOW), struct((rows, depth), LOW)),
        scratch_shapes=[
            pltpu.VMEM((rows, width), LOW),
            pltpu.VMEM((8, rows), WIDE),
            pltpu.VMEM((8, rows), WIDE),
            pltpu.VMEM((width, rows), WIDE),
        ],
        compiler_params=params(24),
        cost_estimate=cost(8),
        name="attend_backward",
    )(scalar, projected, outs, *mixed, *sums, *grads)


def gelu_pair(up):
    root = 0.7978845608028654
    square = up * up
    bent = jnp.tanh(up * (root + (root * 0.044715) * square))
    half = 0.5 * bent + 0.5
    slope = half + (0.5 * up) * (1.0 - bent * bent) * (root + (3 * root * 0.044715) * square)
    return up * half, slope


def feed_kernel(scalar_ref, *refs, begin, half, keep, given):
    tokens_ref, grad_ref, m0, m1, m2, m3, o0, o1, o2, o3, up_ref, down_ref, rows_ref = refs[:13]
    results = refs[13 + given : -1]
    back_ref, sums_ref, normed_ref, active_ref, upper_ref = results[:5]
    mixed_ref = refs[-1]
    i = pl.program_id(0)
    place = scalar_ref[0] if keep else 1 - scalar_ref[0]
    row0 = begin + place * half + i * BLOCK
    row = lax.broadcasted_iota(jnp.int32, (BLOCK, 1), 0) + row0

    @pl.when(scalar_ref[2] == 0)
    def _():
        across = inner_rows(m0[...], o0[...]) + inner_rows(m1[...], o1[...])
        mixed_ref[...] = across + inner_rows(m2[...], o2[...]) + inner_rows(m3[...], o3[...])

    @pl.when(scalar_ref[2] != 0)
    def _():
        across = inner_rows(m1[...], o1[...]) + inner_rows(m0[...], o0[...])
        mixed_ref[...] = across + inner_rows(m3[...], o3[...]) + inner_rows(m2[...], o2[...])

    hidden = tokens_ref[...].astype(WIDE) + mixed_ref[...]
    if keep:
        results[5][...] = hidden
    scaled, _ = standardize(hidden)
    normed = (scaled * rows_ref[1:2, :] + rows_ref[3:4, :]).astype(LOW)
    normed_ref[...] = normed
    grad = jnp.where(row < scalar_ref[1], grad_ref[...].astype(WIDE), 0.0).astype(LOW)
    back = jnp.zeros(hidden.shape, WIDE)
    units = up_ref.shape[1]
    for first in range(0, units, BLOCK):
        part = slice(first, first + BLOCK)
        active, slope = gelu_pair(multiply(normed, up_ref[:, part]))
        active_ref[:, part] = active.astype(LOW)
        upper = (multiply(grad, down_ref[:, part]) * slope).astype(LOW)
        upper_ref[:, part] = upper
        back = back + outer_cols(upper, up_ref[:, part])
    back_ref[...] = back.astype(LOW)

    @pl.when(i == 0)
    def _():
        sums_ref[...] = jnp.zeros_like(sums_ref)

    sums_ref[0:1, :] += jnp.sum(back * scaled, axis=0, keepdims=True)
    sums_ref[1:2, :] += jnp.sum(back, axis=0, keepdims=True)


def feed(scalar, tokens, out_grad, mixed, outs, up, down, rows, stored, begin, size, keep):
    count, depth = tokens.shape
    units = up.shape[1]
    width = outs[0].shape[0]
    half = count // 2
    base = begin // BLOCK
    blocks = size // BLOCK

    def side(scalar_ref):
        return scalar_ref[0] if keep else 1 - scalar_ref[0]

    def placed(i, scalar_ref):
        return (base + side(scalar_ref) * (half // BLOCK) + i, 0)

    def inside(i, scalar_ref):
        return (0, side(scalar_ref) * blocks + i)

    def own(i, scalar_ref):
        return (i, 0)

    def kept(i, scalar_ref):
        return (base + i, 0)

    def fixed(i, scalar_ref):
        return (0, 0)

    out_specs = (
        pl.BlockSpec((BLOCK, depth), own),
        pl.BlockSpec((8, depth), fixed),
        pl.BlockSpec((BLOCK, depth), placed),
        pl.BlockSpec((BLOCK, units), placed),
        pl.BlockSpec((BLOCK, units), placed),
        pl.BlockSpec((BLOCK, depth), kept),
    )
    out_shape = (
        struct((size, depth), LOW),
        struct((8, depth), WIDE),
        struct((count, depth), LOW),
        struct((count, units), LOW),
        struct((count, units), LOW),
        struct((half, depth), WIDE),
    )[: 6 if keep else 5]
    stored = stored[: len(out_shape) - 2]
    return pl.pallas_call(
        functools.partial(feed_kernel, begin=begin, half=half, keep=keep, given=len(stored)),
        grid_spec=pltpu.PrefetchScalarGridSpec(
            num_scalar_prefetch=1,
            grid=(blocks,),
            in_specs=[pl.BlockSpec((BLOCK, depth), placed)] * 2
            + [pl.BlockSpec((width, BLOCK), inside)] * 4
            + [whole()] * 7
            + [pl.BlockSpec(memory_space=pl.ANY)] * len(stored),
            out_specs=out_specs[: len(out_shape)],
            scratch_shapes=[pltpu.VMEM((BLOCK, depth), WIDE)],
        ),
        out_shape=out_shape,
        input_output_aliases={14 + k: 2 + k for k in range(len(stored))},
        compiler_params=params(20),
        cost_estimate=cost(size / 100),
        name="feed_forward",
    )(scalar, tokens, out_grad, *mixed, *outs, up, down, rows, *stored)


def weigh_kernel(scalar_ref, normed_ref, upper_ref, active_ref, grad_ref, down_ref, keep_ref, send_ref, grads_ref, up_sum, down_sum, *, blocks):
    i = pl.program_id(0)
    half = blocks // 2
    units = down_ref.shape[1]
    row0 = lax.rem(i + (1 - scalar_ref[0]) * half, blocks) * BLOCK
    row = lax.broadcasted_iota(jnp.int32, (BLOCK, 1), 0) + row0
    branch = outer_cols(active_ref[...], down_ref[...]).astype(LOW)

    @pl.when(i < half)
    def _():
        send_ref[...] = branch

    @pl.when(i >= half)
    def _():
        keep_ref[...] = branch

    grad = jnp.where(row < scalar_ref[1], grad_ref[...].astype(WIDE), 0.0).astype(LOW)

    @pl.when(i == 0)
    def _():
        up_sum[...] = jnp.zeros_like(up_sum)
        down_sum[...] = jnp.zeros_like(down_sum)

    up_sum[...] += inner_rows(normed_ref[...], upper_ref[...])
    down_sum[...] += inner_rows(grad, active_ref[...])

    @pl.when(i == blocks - 1)
    def _():
        grads_ref[:, :units] = up_sum[...].astype(LOW)
        grads_ref[:, units:] = down_sum[...].astype(LOW)


def weigh(scalar, normed, upper, active, out_grad, down):
    count, depth = normed.shape
    units = down.shape[1]
    blocks = count // BLOCK
    half = blocks // 2

    def turned(i, scalar_ref):
        return (lax.rem(i + (1 - scalar_ref[0]) * half, blocks), 0)

    return pl.pallas_call(
        functools.partial(weigh_kernel, blocks=blocks),
        grid_spec=pltpu.PrefetchScalarGridSpec(
            num_scalar_prefetch=1,
            grid=(blocks,),
            in_specs=[pl.BlockSpec((BLOCK, depth), turned)] * 4 + [whole()],
            out_specs=(
                pl.BlockSpec((BLOCK, depth), lambda i, s: (jnp.maximum(i - half, 0), 0)),
                pl.BlockSpec((BLOCK, depth), lambda i, s: (jnp.minimum(i, half - 1), 0)),
                pl.BlockSpec((depth, 2 * units), lambda i, s: (0, 0)),
            ),
            scratch_shapes=[pltpu.VMEM((depth, units), WIDE)] * 2,
        ),
        out_shape=(
            struct((count // 2, depth), LOW),
            struct((count // 2, depth), LOW),
            struct((depth, 2 * units), LOW),
        ),
        compiler_params=params(24),
        cost_estimate=cost(1),
        name="feed_forward_weights",
    )(scalar, normed, upper, active, out_grad, down)


def second_back_kernel(scalar_ref, mine_ref, other_ref, hidden_ref, grad_ref, rows_ref, low_ref, *, begin, half):
    row0 = begin + scalar_ref[0] * half + pl.program_id(0) * BLOCK
    row = lax.broadcasted_iota(jnp.int32, (BLOCK, 1), 0) + row0
    grad_normed = mine_ref[...].astype(WIDE) + other_ref[...].astype(WIDE)
    scaled, inverse = standardize(hidden_ref[...])
    grad = jnp.where(row < scalar_ref[1], grad_ref[...].astype(WIDE), 0.0)
    grad = grad + standardize_back(grad_normed, scaled, inverse, rows_ref[1:2, :])
    low_ref[...] = grad.astype(LOW)


def second_back(scalar, mine, other, hidden, out_grad, rows, begin, size):
    half, depth = hidden.shape
    base = begin // BLOCK

    def own(i, scalar_ref):
        return (i, 0)

    def kept(i, scalar_ref):
        return (base + i, 0)

    def placed(i, scalar_ref):
        return (base + i + scalar_ref[0] * (half // BLOCK), 0)

    return pl.pallas_call(
        functools.partial(second_back_kernel, begin=begin, half=half),
        grid_spec=pltpu.PrefetchScalarGridSpec(
            num_scalar_prefetch=1,
            grid=(size // BLOCK,),
            in_specs=[pl.BlockSpec((BLOCK, depth), own)] * 2
            + [pl.BlockSpec((BLOCK, depth), kept), pl.BlockSpec((BLOCK, depth), placed), whole()],
            out_specs=pl.BlockSpec((BLOCK, depth), own),
        ),
        out_shape=struct((size, depth), LOW),
        compiler_params=params(12),
        cost_estimate=cost(size / 1000),
        name="second_norm_backward",
    )(scalar, mine, other, hidden, out_grad, rows)


def inward_kernel(scalar_ref, grads_ref, tokens_ref, weights_ref, back_ref, sums_ref):
    i = pl.program_id(0)
    width = grads_ref.shape[0]
    back = lax.dot_general(
        grads_ref[...], weights_ref[:, :width], (((0,), (1,)), ((), ())), preferred_element_type=WIDE
    )
    scaled, _ = standardize(tokens_ref[...].astype(WIDE))
    back_ref[...] = back.astype(LOW)

    @pl.when(i == 0)
    def _():
        sums_ref[...] = jnp.zeros_like(sums_ref)

    sums_ref[0:1, :] += jnp.sum(back * scaled, axis=0, keepdims=True)
    sums_ref[1:2, :] += jnp.sum(back, axis=0, keepdims=True)


def inward(scalar, grads, tokens, weights, begin, half, keep):
    depth = tokens.shape[1]
    width = grads.shape[0]
    blocks = half // BLOCK

    def placed(i, scalar_ref):
        place = scalar_ref[0] if keep else 1 - scalar_ref[0]
        return (begin // BLOCK + place * blocks + i, 0)

    def lanes(i, scalar_ref):
        return placed(i, scalar_ref)[::-1]

    return pl.pallas_call(
        inward_kernel,
        grid_spec=pltpu.PrefetchScalarGridSpec(
            num_scalar_prefetch=1,
            grid=(blocks,),
            in_specs=[pl.BlockSpec((width, BLOCK), lanes), pl.BlockSpec((BLOCK, depth), placed), whole()],
            out_specs=(
                pl.BlockSpec((BLOCK, depth), lambda i, s: (i, 0)),
                pl.BlockSpec((8, depth), lambda i, s: (0, 0)),
            ),
        ),
        out_shape=(struct((half, depth), LOW), struct((8, depth), WIDE)),
        compiler_params=params(12),
        cost_estimate=cost(3),
        name="grad_normed",
    )(scalar, grads, tokens, weights)


def project_back_kernel(grads_ref, normed_ref, outs_ref, *refs, width, split):
    sums, out_ref = refs[:-1], refs[-1]
    last = out_ref.shape[1] - outs_ref.shape[1]
    out_ref[:, last:] = outs_ref[...]
    out_ref[:, :width] = jnp.transpose(multiply(grads_ref[...], normed_ref[...])).astype(LOW)
    ones, twos = sums[:split], sums[split:]
    one = sum(ref[...] for ref in ones[1:]) + ones[0][...]
    two = sum(ref[...] for ref in twos[1:]) + twos[0][...]
    rows = jnp.concatenate([one, two, jnp.zeros((LANES - 16, one.shape[1]), WIDE)], axis=0)
    out_ref[:, width:last] = jnp.transpose(rows)[:, : last - width].astype(LOW)


def project_back(grads, normed, outs_grad, ones, twos):
    width = grads.shape[0]
    depth = normed.shape[1]
    sums = list(ones) + list(twos)
    return pl.pallas_call(
        functools.partial(project_back_kernel, width=width, split=len(ones)),
        in_specs=[whole()] * (3 + len(sums)),
        out_specs=whole(),
        out_shape=struct((depth, width + -width % LANES + outs_grad.shape[1]), LOW),
        compiler_params=params(16),
        cost_estimate=cost(3),
        name="projection_weights",
    )(grads, normed, outs_grad, *sums)


def finish_kernel(scalar_ref, mine_ref, other_ref, hidden_ref, own_ref, full_ref, *, begin, half):
    row0 = begin + scalar_ref[0] * half + pl.program_id(0) * BLOCK
    row = lax.broadcasted_iota(jnp.int32, (BLOCK, 1), 0) + row0
    total = hidden_ref[...] + (mine_ref[...].astype(WIDE) + other_ref[...].astype(WIDE))
    low = jnp.where(row < scalar_ref[1], total, 0.0).astype(LOW)
    own_ref[...] = low
    full_ref[...] = low


def first_back_kernel(scalar_ref, mine_ref, other_ref, tokens_ref, grad_ref, rows_ref, own_ref, full_ref):
    grad_normed = mine_ref[...].astype(WIDE) + other_ref[...].astype(WIDE)
    scaled, inverse = standardize(tokens_ref[...].astype(WIDE))
    grad = grad_ref[...].astype(WIDE) + standardize_back(grad_normed, scaled, inverse, rows_ref[0:1, :])
    low = grad.astype(LOW)
    own_ref[...] = low
    full_ref[...] = low


def place_rows(kernel, scalar, owned, spread, fixed, count, begin, half, name):
    depth = owned[0].shape[1]
    blocks = half // BLOCK

    def own(i, scalar_ref):
        return (i, 0)

    def placed(i, scalar_ref):
        return (begin // BLOCK + i + scalar_ref[0] * blocks, 0)

    return pl.pallas_call(
        kernel,
        grid_spec=pltpu.PrefetchScalarGridSpec(
            num_scalar_prefetch=1,
            grid=(blocks,),
            in_specs=[pl.BlockSpec((BLOCK, depth), own)] * 2
            + [pl.BlockSpec((BLOCK, depth), placed)] * len(spread)
            + [pl.BlockSpec((BLOCK, depth), own)] * (len(owned) - 2)
            + [whole()] * len(fixed),
            out_specs=(pl.BlockSpec((BLOCK, depth), own), pl.BlockSpec((BLOCK, depth), placed)),
        ),
        out_shape=(struct((half, depth), LOW), struct((count, depth), LOW)),
        compiler_params=params(12),
        cost_estimate=cost(3),
        name=name,
    )(scalar, *owned[:2], *spread, *owned[2:], *fixed)


def total_kernel(parts_ref, *outs, bounds, flips):
    total = parts_ref[0].astype(WIDE)
    for k in range(1, parts_ref.shape[0]):
        total = total + parts_ref[k].astype(WIDE)
    for out, (first, last), flip in zip(outs, bounds, flips):
        piece = total[:, first:last]
        out[...] = jnp.transpose(piece) if flip else piece


def total_parts(parts, bounds, flips):
    rows = parts.shape[1]
    shapes = []
    for (first, last), flip in zip(bounds, flips):
        shape = (last - first, rows) if flip else (rows, last - first)
        shapes.append(struct(shape, WIDE))
    return pl.pallas_call(
        functools.partial(total_kernel, bounds=bounds, flips=flips),
        in_specs=[whole()],
        out_specs=(whole(),) * len(shapes),
        out_shape=tuple(shapes),
        compiler_params=params(8),
        cost_estimate=cost(1),
        name="total",
    )(parts)


def exchange_batch(value):
    size = lax.axis_size("batch")
    parts = value.reshape(size, value.shape[0] // size, value.shape[1])
    return lax.all_to_all(parts, "batch", 0, 0, tiled=True)


def per_device(tokens, lengths, w_query, w_key, w_value, w_out, w_up, w_down, norm_gain, norm_shift, out_grad):
    count, depth = tokens.shape
    batch = lax.axis_size("batch")
    if lengths.shape[0] != 1 or lax.axis_size("tensor") != 4:
        raise ValueError("unsupported mesh")
    width = w_query.shape[1]
    units = w_up.shape[1]
    tensor = lax.axis_index("tensor").astype(jnp.int32)
    core = tensor & 1
    scalar = jnp.stack([core, lengths[0], tensor >> 1, lax.axis_index("batch").astype(jnp.int32)])
    sure = 2 * count // 3
    half = count // 2
    first = half // 3 * 2
    chunks = ((0, first), (first, half - first))

    blank = jnp.zeros((w_query.shape[0], -(4 * width + 4) % LANES), LOW)
    early = jnp.concatenate([w_query, w_key, w_value, w_out.T, norm_gain.T, norm_shift.T, blank], axis=1)
    late = jnp.concatenate([w_up, w_down.T], axis=1)
    if batch == 8:
        far = gather_far(early)
        early = [early, swap(early, "batch", 1)]
        for piece in far:
            early += [piece, swap(piece, "batch", 1)]
        late = after(late, *far)
        near = swap(late, "batch", 2)
        middle = swap(late, "batch", 4)
        far = swap(middle, "batch", 2)
        late = [late, swap(late, "batch", 1)]
        for piece in (near, middle, far):
            late += [piece, swap(piece, "batch", 1)]
    else:
        early = [lax.all_gather(early, "batch", axis=0, tiled=True)]
        late = [lax.all_gather(late, "batch", axis=0, tiled=True)]

    normed, projected, rows, weights, own_outs = project(scalar, tokens, early, width)
    across = swap(own_outs, "tensor", 2)
    outs = (own_outs, across, swap(own_outs, "tensor", 1), swap(across, "tensor", 1))
    mixed, sums, pieces = [], [], []
    for begin, size in chunks:
        local = tuple(range(begin // BLOCK, (begin + size) // BLOCK))
        part, logs = attend(scalar, projected, local + tuple(k + half // BLOCK for k in local), sure)
        projected = after(projected, part)
        mixed.append(part)
        sums.append(logs)
        across = swap(part, "tensor", 2)
        pieces.append((part, across, swap(part, "tensor", 1), swap(across, "tensor", 1)))
    late = lax.optimization_barrier((*late, *pieces[-1]))[: len(late)]
    full_up, full_down = assemble(scalar, late, units)

    stored = []
    twos, halves = [], []
    for (begin, size), piece in zip(chunks, pieces):
        ends = []
        rows = after(rows, *(mine for mine, _ in halves))
        for keep in (False, True):
            back, two, *fresh = feed(
                scalar, tokens, out_grad, piece, outs, full_up, full_down, rows, stored, begin, size, keep
            )
            stored = fresh + stored[len(fresh) :]
            twos.append(two)
            ends.append(back)
        mine = (ends[1].astype(WIDE) + swap(ends[0], "tensor", 1).astype(WIDE)).astype(LOW)
        halves.append((mine, swap(mine, "tensor", 2)))
    normed_two, active, upper, hidden = stored
    normed_two = after(normed_two, *(mine for mine, _ in halves))
    branch_keep, branch_send, feed_grads = weigh(scalar, normed_two, upper, active, out_grad, full_down)
    feed_parts = exchange_batch(feed_grads)

    beside = swap(branch_send, "tensor", 1)
    grads = []
    for (begin, size), (mine, other) in zip(chunks, halves):
        mine = after(mine, feed_grads)
        low = second_back(scalar, mine, other, hidden, out_grad, rows, begin, size)
        grads += [low, swap(low, "tensor", 1)]
    branch_mine = (branch_keep.astype(WIDE) + beside.astype(WIDE)).astype(LOW)
    branch_mine = after(branch_mine, *grads)
    branch_other = swap(branch_mine, "tensor", 2)
    projected = after(projected, branch_mine)
    attend_grads, outs_grad, grad_attn = attend_back(
        scalar, projected, own_outs, mixed, sums, grads, chunks, sure
    )

    own_out, layer_out = place_rows(
        functools.partial(finish_kernel, begin=0, half=half),
        scalar,
        (branch_mine, branch_other, hidden),
        (),
        (),
        count,
        0,
        half,
        "layer_out",
    )
    there = (1 - core) * half
    layer_out = lax.dynamic_update_slice(layer_out, swap(own_out, "tensor", 1), (there, 0))

    ends, ones = [], []
    attend_grads = after(attend_grads, branch_other)
    for keep in (False, True):
        back, one = inward(scalar, attend_grads, tokens, weights, 0, half, keep)
        ends.append(back)
        ones.append(one)
    back = pair_sum(ends[1], ends[0])
    project_parts = exchange_batch(after(project_back(attend_grads, normed, outs_grad, ones, twos), feed_parts))
    own_grad, grad_input = place_rows(
        first_back_kernel, scalar, back, (tokens, grad_attn), (rows,), count, 0, half, "first_norm_backward"
    )
    grad_input = lax.dynamic_update_slice(grad_input, swap(own_grad, "tensor", 1), (there, 0))

    shard_up, shard_down = total_parts(feed_parts, ((0, units), (units, 2 * units)), (False, True))
    last = 3 * width
    final = project_parts.shape[2]
    shard_query, shard_key, shard_value, small, shard_out = total_parts(
        project_parts,
        ((0, width), (width, 2 * width), (2 * width, last), (last, final - width), (final - width, final)),
        (False, False, False, True, True),
    )
    small = small[:16]
    small = small + swap(small, "tensor", 2)
    small = small + swap(small, "tensor", 1)
    shard_gain = jnp.stack([small[0], small[8]])
    shard_shift = jnp.stack([small[1], small[9]])
    return (
        layer_out,
        grad_input,
        shard_query,
        shard_key,
        shard_value,
        shard_out,
        shard_up,
        shard_down,
        shard_gain,
        shard_shift,
    )


def solution(mesh):
    tall = P("batch", "tensor")
    wide = P("tensor", "batch")
    rows = P("batch", None)
    pair = P(None, "batch")
    return jax.shard_map(
        per_device,
        mesh=mesh,
        in_specs=(rows, P("batch"), tall, tall, tall, wide, tall, wide, pair, pair, rows),
        out_specs=(rows, rows, tall, tall, tall, wide, tall, wide, pair, pair),
        check_vma=False,
    )
```

```python
import functools

import jax
import jax.numpy as jnp
from jax import lax
from jax.experimental import pallas as pl
from jax.experimental.pallas import tpu as pltpu
from jax.sharding import PartitionSpec as P

HD = 64
EPSILON = 1e-05
LOG2E = 1.4426950408889634
HUGE = 3e38
FAR = -1e30
LOW = jnp.bfloat16
WIDE = jnp.float32
LANES = 128
BLOCK = 256
STEP = 384


def multiply(left, right):
    return lax.dot_general(left, right, (((1,), (0,)), ((), ())), preferred_element_type=WIDE)


def outer_cols(left, right):
    return lax.dot_general(left, right, (((1,), (1,)), ((), ())), preferred_element_type=WIDE)


def inner_rows(left, right):
    return lax.dot_general(left, right, (((0,), (0,)), ((), ())), preferred_element_type=WIDE)


def whole():
    return pl.BlockSpec(memory_space=pltpu.VMEM)


def scalars():
    return pl.BlockSpec(memory_space=pltpu.SMEM)


def struct(shape, dtype):
    return jax.ShapeDtypeStruct(shape, dtype)


def held(shape, dtype):
    return pltpu.VMEM(shape, dtype)


def stored_far(shape, dtype):
    return pltpu.HBM(shape, dtype)


def far(value):
    return pltpu.with_memory_space_constraint(value, pltpu.HBM)


def params(mebibytes):
    return pltpu.CompilerParams(vmem_limit_bytes=mebibytes << 20)


def cost(microseconds):
    return pl.CostEstimate(flops=int(microseconds * 1.1e6), bytes_accessed=0, transcendentals=0)


def after(value, *others):
    return lax.optimization_barrier((value, *others))[0]


def swap(value, axis, bits):
    size = lax.axis_size(axis)
    return lax.ppermute(value, axis, [(i, i ^ bits) for i in range(size)])


def gather_far(shard):
    return [swap(shard, "batch", bits) for bits in (2, 4, 6)]


def pair_sum(keep, send):
    mine = (keep.astype(WIDE) + swap(send, "tensor", 1).astype(WIDE)).astype(LOW)
    return mine, swap(mine, "tensor", 2)


def standardize(values):
    middle = jnp.mean(values, axis=-1, keepdims=True)
    centred = values - middle
    spread = jnp.mean(centred * centred, axis=-1, keepdims=True)
    inverse = lax.rsqrt(spread + EPSILON)
    return centred * inverse, inverse


def standardize_back(grad, scaled, inverse, gain):
    grad = grad * gain
    mean_grad = jnp.mean(grad, axis=-1, keepdims=True)
    mean_cross = jnp.mean(grad * scaled, axis=-1, keepdims=True)
    return inverse * (grad - mean_grad - scaled * mean_cross)


def collect(index, pieces, scratch):
    count = pieces[0].shape[0]
    for bits, piece in enumerate(pieces):
        at = pl.multiple_of((index ^ bits) * count, 32) if len(pieces) > 1 else 0
        scratch[pl.ds(at, count), :] = piece[...]


def project_kernel(scalar_ref, *refs, parts, width, block):
    pieces, refs = refs[:parts], refs[parts:]
    tokens_ref, normed_ref, projected_ref, rows_ref, weights_ref, outs_ref = refs

    @pl.when(pl.program_id(0) == 0)
    def _():
        collect(scalar_ref[3], pieces, weights_ref)
        rows_ref[...] = jnp.transpose(weights_ref[:, 4 * width : 4 * width + LANES].astype(WIDE))[:8, :]
        outs_ref[...] = jnp.transpose(weights_ref[:, 3 * width : 4 * width])

    for k in range(tokens_ref.shape[0] // block):
        part = slice(k * block, (k + 1) * block)
        scaled, _ = standardize(tokens_ref[part, :].astype(WIDE))
        normed = (scaled * rows_ref[0:1, :] + rows_ref[2:3, :]).astype(LOW)
        normed_ref[part, :] = normed
        projected_ref[part, :] = multiply(normed, weights_ref[:, : 3 * width]).astype(LOW)


def project(scalar, tokens, pieces, width):
    count, depth = tokens.shape
    total = pieces[0].shape[1]
    step = 768
    return pl.pallas_call(
        functools.partial(project_kernel, parts=len(pieces), width=width, block=256),
        grid=(count // step,),
        in_specs=[scalars()]
        + [whole()] * len(pieces)
        + [pl.BlockSpec((step, depth), lambda i: (i, 0))],
        out_specs=(
            pl.BlockSpec((step, depth), lambda i: (i, 0)),
            pl.BlockSpec((step, 3 * width), lambda i: (i, 0)),
            pl.BlockSpec((8, depth), lambda i: (0, 0)),
            pl.BlockSpec((depth, total), lambda i: (0, 0)),
            pl.BlockSpec((width, depth), lambda i: (0, 0)),
        ),
        out_shape=(
            stored_far((count, depth), LOW),
            struct((count, 3 * width), LOW),
            struct((8, depth), WIDE),
            struct((depth, total), LOW),
            struct((width, depth), LOW),
        ),
        compiler_params=params(20),
        cost_estimate=cost(4),
        name="project",
    )(scalar, *pieces, pltpu.with_memory_space_constraint(tokens, pltpu.HBM))


def assemble_kernel(scalar_ref, *refs, parts, units):
    pieces, (up_ref, down_ref) = refs[:parts], refs[parts:]
    count = pieces[0].shape[0]
    for bits, piece in enumerate(pieces):
        at = pl.multiple_of((scalar_ref[3] ^ bits) * count, 32) if parts > 1 else 0
        up_ref[pl.ds(at, count), :] = piece[:, :units]
        down_ref[pl.ds(at, count), :] = piece[:, units:]


def assemble(scalar, pieces, units):
    depth = sum(piece.shape[0] for piece in pieces)
    return pl.pallas_call(
        functools.partial(assemble_kernel, parts=len(pieces), units=units),
        in_specs=[scalars()] + [whole()] * len(pieces),
        out_specs=(whole(),) * 2,
        out_shape=(struct((depth, units), LOW), struct((depth, units), LOW)),
        compiler_params=params(10),
        cost_estimate=cost(1),
        name="assemble",
    )(scalar, *pieces)


def sign_of(scores):
    scores = scores.astype(LOW) * LOW(HUGE)
    return jnp.minimum(jnp.maximum(scores, LOW(-1)), LOW(1))


def attend_kernel(scalar_ref, projected_ref, mixed_ref, sums_ref, *, places, heads, sure):
    length = scalar_ref[1]
    factor = LOG2E * HD**-0.5
    width = heads * HD
    for i, place in enumerate(places):
        row0 = place * BLOCK
        here = slice(row0, row0 + BLOCK)
        row = lax.broadcasted_iota(jnp.int32, (BLOCK, 1), 0) + row0
        key = lax.broadcasted_iota(jnp.int32, (BLOCK, BLOCK), 1) + row0
        allowed = key <= jnp.minimum(row, length - 1)
        def each(function):
            return jnp.concatenate([function(h) for h in range(heads)], axis=0)

        def column(kind, h):
            return slice(kind * width + h * HD, kind * width + (h + 1) * HD)

        def split(value, h):
            return value[h * BLOCK : (h + 1) * BLOCK]

        near = each(lambda h: outer_cols(projected_ref[here, column(0, h)], projected_ref[here, column(1, h)]))
        near_size = jnp.where(jnp.concatenate([allowed] * heads, axis=0), jnp.abs(near) * factor, FAR)
        top = jnp.max(near_size, axis=1, keepdims=True)
        if row0 > 0:
            past = each(lambda h: outer_cols(projected_ref[here, column(0, h)], projected_ref[:row0, column(1, h)]))
            past_size = jnp.abs(past) * factor
            if row0 > sure:
                past_key = lax.broadcasted_iota(jnp.int32, (1, row0), 1)
                past_size = jnp.where(past_key < length, past_size, FAR)
            top = jnp.maximum(top, jnp.max(past_size, axis=1, keepdims=True))
            past_prob = jnp.exp2(past_size - top)
            past_signed = past_prob.astype(LOW) * sign_of(past)
        near_prob = jnp.exp2(near_size - top)
        near_signed = near_prob.astype(LOW) * sign_of(near)
        total = jnp.sum(near_prob, axis=1, keepdims=True)
        mixed = each(lambda h: multiply(split(near_signed, h), projected_ref[here, column(2, h)]))
        if row0 > 0:
            total = total + jnp.sum(past_prob, axis=1, keepdims=True)
            mixed = mixed + each(lambda h: multiply(split(past_signed, h), projected_ref[:row0, column(2, h)]))
        mixed = (mixed / total).astype(LOW)
        logs = top + jnp.log2(total)
        outs = [split(mixed, h) for h in range(heads)]
        sums = [split(logs, h) for h in range(heads)]
        part = slice(i * BLOCK, (i + 1) * BLOCK)
        mixed_ref[:, part] = jnp.transpose(jnp.concatenate(outs, axis=1))
        blank = jnp.zeros((BLOCK, LANES - heads), WIDE)
        sums_ref[i] = jnp.transpose(jnp.concatenate(sums + [blank], axis=1))[:8, :]


def attend(scalar, projected, places, sure):
    width = projected.shape[1] // 3
    heads = width // HD
    return pl.pallas_call(
        functools.partial(attend_kernel, places=places, heads=heads, sure=sure),
        in_specs=[scalars(), whole()],
        out_specs=(whole(), whole()),
        out_shape=(struct((width, len(places) * BLOCK), LOW), struct((len(places), 8, BLOCK), WIDE)),
        compiler_params=params(16),
        cost_estimate=cost(1),
        name="attend_forward",
    )(scalar, projected)


def attend_back_kernel(scalar_ref, *refs, chunks, rows, heads, sure):
    length = scalar_ref[1]
    core = scalar_ref[0]
    projected_ref, outs_ref, refs = refs[0], refs[1], refs[2:]
    mixed_refs, refs = refs[: len(chunks)], refs[len(chunks) :]
    sums_refs, refs = refs[: len(chunks)], refs[len(chunks) :]
    grad_refs, refs = refs[: 2 * len(chunks)], refs[2 * len(chunks) :]
    grads_ref, outs_grad_ref, whole_ref, grad_mixed, delta, logs, dq_turned = refs
    scaling = HD**-0.5
    factor = LOG2E * scaling
    width = heads * HD
    blocks = rows // BLOCK
    outs_grad = jnp.zeros(outs_ref.shape, WIDE)
    half = blocks // 2
    for number, (begin, size) in enumerate(chunks):
        for side in range(2):
            for k in range(size // BLOCK):
                local = side * size + k * BLOCK
                inside = slice(local, local + BLOCK)
                i = side * half + begin // BLOCK + k
                rows_i = slice(i * BLOCK, (i + 1) * BLOCK)
                mine = grad_refs[2 * number][k * BLOCK : (k + 1) * BLOCK, :]
                other = grad_refs[2 * number + 1][k * BLOCK : (k + 1) * BLOCK, :]

                @pl.when(core == side)
                def _():
                    whole_ref[rows_i, :] = mine

                @pl.when(core != side)
                def _():
                    whole_ref[rows_i, :] = other

                grad = whole_ref[rows_i, :]
                mixed = mixed_refs[number][:, inside]
                outs_grad = outs_grad + multiply(mixed, grad)
                turned = outer_cols(outs_ref[...], grad)
                grad_mixed[rows_i, :] = jnp.transpose(turned).astype(LOW)
                logs[:, rows_i] = sums_refs[number][local // BLOCK]
                both = turned.astype(LOW).astype(WIDE) * mixed.astype(WIDE)
                for h in range(heads):
                    delta[h : h + 1, rows_i] = jnp.sum(both[h * HD : (h + 1) * HD, :], axis=0, keepdims=True)
    outs_grad_ref[...] = jnp.transpose(outs_grad).astype(LOW)
    for j in range(blocks):
        here = slice(j * BLOCK, (j + 1) * BLOCK)
        later = slice((j + 1) * BLOCK, rows)
        dks, dvs = [], []
        for h in range(heads):
            cols = slice(h * HD, (h + 1) * HD)
            k = projected_ref[here, width + h * HD : width + (h + 1) * HD]
            v = projected_ref[here, 2 * width + h * HD : 2 * width + (h + 1) * HD]
            dk = jnp.zeros((BLOCK, HD), WIDE)
            dv = jnp.zeros((BLOCK, HD), WIDE)
            for part in (here, later):
                span = part.stop - part.start
                if span == 0:
                    continue
                q = projected_ref[part, cols]
                g = grad_mixed[part, cols]
                scores = outer_cols(k, q)
                grad_weights = outer_cols(v, g)
                reach = jnp.abs(scores) * factor - logs[h : h + 1, part]
                if part is here:
                    key = lax.broadcasted_iota(jnp.int32, (BLOCK, span), 0) + j * BLOCK
                    row = lax.broadcasted_iota(jnp.int32, (1, span), 1) + j * BLOCK
                    reach = jnp.where(key <= jnp.minimum(row, length - 1), reach, FAR)
                elif (j + 1) * BLOCK > sure:
                    key = lax.broadcasted_iota(jnp.int32, (BLOCK, 1), 0) + j * BLOCK
                    reach = jnp.where(key < length, reach, FAR)
                sign = sign_of(scores)
                weights = jnp.exp2(reach)
                signed = sign.astype(WIDE)
                raw = (weights * (grad_weights - signed * delta[h : h + 1, part])).astype(LOW) * (sign * sign)
                dv = dv + multiply(weights.astype(LOW) * sign, g)
                dk = dk + multiply(raw, q)
                more = inner_rows(k, raw)
                if j == 0:
                    dq_turned[cols, part] = more
                else:
                    dq_turned[cols, part] += more
            dks.append(dk * scaling)
            dvs.append(dv)
        grads_ref[:width, here] = (dq_turned[:, here] * scaling).astype(LOW)
        grads_ref[width : 2 * width, here] = jnp.transpose(jnp.concatenate(dks, axis=1)).astype(LOW)
        grads_ref[2 * width :, here] = jnp.transpose(jnp.concatenate(dvs, axis=1)).astype(LOW)


def attend_back(scalar, projected, outs, mixed, sums, grads, chunks, sure):
    rows = projected.shape[0]
    width = projected.shape[1] // 3
    depth = outs.shape[1]
    heads = width // HD
    return pl.pallas_call(
        functools.partial(attend_back_kernel, chunks=chunks, rows=rows, heads=heads, sure=sure),
        in_specs=[scalars()] + [whole()] * (2 + 4 * len(chunks)),
        out_specs=(whole(),) * 3,
        out_shape=(struct((3 * width, rows), LOW), struct((depth, width), LOW), struct((rows, depth), LOW)),
        scratch_shapes=[
            pltpu.VMEM((rows, width), LOW),
            pltpu.VMEM((8, rows), WIDE),
            pltpu.VMEM((8, rows), WIDE),
            pltpu.VMEM((width, rows), WIDE),
        ],
        compiler_params=params(24),
        cost_estimate=cost(8),
        name="attend_backward",
    )(scalar, projected, outs, *mixed, *sums, *grads)


def gelu_pair(up):
    root = 0.7978845608028654
    square = up * up
    bent = jnp.tanh(up * (root + (root * 0.044715) * square))
    half = 0.5 * bent + 0.5
    slope = half + (0.5 * up) * (1.0 - bent * bent) * (root + (3 * root * 0.044715) * square)
    return up * half, slope


def add_sums(sums_ref, ahead_ref, back, scaled):
    sums_ref[0:1, :] = ahead_ref[0:1, :] + jnp.sum(back * scaled, axis=0, keepdims=True)
    sums_ref[1:2, :] = ahead_ref[1:2, :] + jnp.sum(back, axis=0, keepdims=True)
    sums_ref[2:8, :] = ahead_ref[2:8, :]


def feed_kernel(scalar_ref, *refs, begin, size, half, keep, given):
    tokens_ref, grad_ref, m0, m1, m2, m3, o0, o1, o2, o3, up_ref, down_ref, rows_ref, ahead_ref = refs[:14]
    results = refs[14 + given : -1]
    back_ref, sums_ref, normed_ref, active_ref, upper_ref = results[:5]
    mixed_ref = refs[-1]
    place = scalar_ref[0] if keep else 1 - scalar_ref[0]
    row0 = pl.multiple_of(begin + place * half, BLOCK)
    here = pl.ds(row0, size)
    row = lax.broadcasted_iota(jnp.int32, (size, 1), 0) + row0

    @pl.when(scalar_ref[2] == 0)
    def _():
        across = inner_rows(m0[...], o0[...]) + inner_rows(m1[...], o1[...])
        mixed_ref[...] = across + inner_rows(m2[...], o2[...]) + inner_rows(m3[...], o3[...])

    @pl.when(scalar_ref[2] != 0)
    def _():
        across = inner_rows(m1[...], o1[...]) + inner_rows(m0[...], o0[...])
        mixed_ref[...] = across + inner_rows(m3[...], o3[...]) + inner_rows(m2[...], o2[...])

    hidden = tokens_ref[...].astype(WIDE) + mixed_ref[...]
    if keep:
        results[5][...] = hidden
    scaled, _ = standardize(hidden)
    normed = (scaled * rows_ref[1:2, :] + rows_ref[3:4, :]).astype(LOW)
    normed_ref[here, :] = normed
    grad = jnp.where(row < scalar_ref[1], grad_ref[...].astype(WIDE), 0.0).astype(LOW)
    back = jnp.zeros(hidden.shape, WIDE)
    units = up_ref.shape[1]
    for first in range(0, units, BLOCK):
        part = slice(first, first + BLOCK)
        active, slope = gelu_pair(multiply(normed, up_ref[:, part]))
        active_ref[here, part] = active.astype(LOW)
        upper = (multiply(grad, down_ref[:, part]) * slope).astype(LOW)
        upper_ref[here, part] = upper
        back = back + outer_cols(upper, up_ref[:, part])
    back_ref[...] = back.astype(LOW)
    add_sums(sums_ref, ahead_ref, back, scaled)


def feed(scalar, tokens, out_grad, mixed, outs, up, down, rows, ahead, stored, begin, size, keep):
    count, depth = tokens.shape
    units = up.shape[1]
    width = outs[0].shape[0]
    half = count // 2

    def side(scalar_ref):
        return scalar_ref[0] if keep else 1 - scalar_ref[0]

    def placed(i, scalar_ref):
        return ((begin + side(scalar_ref) * half) // BLOCK * BLOCK, 0)

    def inside(i, scalar_ref):
        return (0, side(scalar_ref))

    rows_spec = pl.BlockSpec((pl.Element(size), pl.Element(depth)), placed)
    out_shape = (
        struct((size, depth), LOW),
        struct((8, depth), WIDE),
        struct((count, depth), LOW),
        struct((count, units), LOW),
        struct((count, units), LOW),
        stored_far((size, depth), WIDE),
    )[: 6 if keep else 5]
    return pl.pallas_call(
        functools.partial(feed_kernel, begin=begin, size=size, half=half, keep=keep, given=len(stored)),
        grid_spec=pltpu.PrefetchScalarGridSpec(
            num_scalar_prefetch=1,
            grid=(1,),
            in_specs=[rows_spec] * 2
            + [pl.BlockSpec((width, size), inside)] * 4
            + [whole()] * 8
            + [pl.BlockSpec(memory_space=pl.ANY)] * len(stored),
            out_specs=(whole(),) * len(out_shape),
            scratch_shapes=[pltpu.VMEM((size, depth), WIDE)],
        ),
        out_shape=out_shape,
        input_output_aliases={15 + k: 2 + k for k in range(len(stored))},
        compiler_params=params(20),
        cost_estimate=cost(size / 1000),
        name="feed_forward",
    )(scalar, tokens, out_grad, *mixed, *outs, up, down, rows, ahead, *stored)


def put_shards(index, outs, value, cols):
    if len(outs) == 1:
        outs[0][:, cols] = value
        return
    mine, other = outs
    rows = value.shape[0] // 8
    for place in range(8):
        piece = value[place * rows : (place + 1) * rows, :]

        @pl.when((index & 1) == place % 2)
        def _():
            mine[place // 2, :, cols] = piece

        @pl.when((index & 1) != place % 2)
        def _():
            other[place // 2, :, cols] = piece


def shard_shapes(batch, depth, cols):
    if batch != 8:
        return (stored_far((depth, cols), LOW),)
    return (struct((4, depth // 8, cols), LOW),) * 2


def weigh_kernel(scalar_ref, normed_ref, upper_ref, active_ref, grad_ref, down_ref, keep_ref, send_ref, *refs):
    outs, (up_sum, down_sum) = refs[:-2], refs[-2:]
    i = pl.program_id(0)
    units = down_ref.shape[1]
    half = grad_ref.shape[0]
    row0 = pl.multiple_of((scalar_ref[0] ^ 1 ^ i) * half, BLOCK)
    here = pl.ds(row0, half)
    row = lax.broadcasted_iota(jnp.int32, (half, 1), 0) + row0
    active = active_ref[here, :]
    branch = outer_cols(active, down_ref[...]).astype(LOW)
    grad = jnp.where(row < scalar_ref[1], grad_ref[...].astype(WIDE), 0.0).astype(LOW)
    up = inner_rows(normed_ref[here, :], upper_ref[here, :])
    down = inner_rows(grad, active)

    @pl.when(i == 0)
    def _():
        send_ref[...] = branch
        up_sum[...] = up
        down_sum[...] = down

    @pl.when(i == 1)
    def _():
        keep_ref[...] = branch
        put_shards(scalar_ref[3], outs, (up_sum[...] + up).astype(LOW), slice(0, units))
        put_shards(scalar_ref[3], outs, (down_sum[...] + down).astype(LOW), slice(units, 2 * units))


def weigh(scalar, normed, upper, active, out_grad, down, batch):
    count, depth = normed.shape
    units = down.shape[1]
    half = count // 2
    return pl.pallas_call(
        weigh_kernel,
        grid_spec=pltpu.PrefetchScalarGridSpec(
            num_scalar_prefetch=1,
            grid=(2,),
            in_specs=[whole()] * 3
            + [pl.BlockSpec((half, depth), lambda i, scalar_ref: (scalar_ref[0] ^ 1 ^ i, 0)), whole()],
            out_specs=(whole(),) * (2 + len(shard_shapes(batch, depth, 2 * units))),
            scratch_shapes=[pltpu.VMEM((depth, units), WIDE)] * 2,
        ),
        out_shape=(
            struct((half, depth), LOW),
            struct((half, depth), LOW),
            *shard_shapes(batch, depth, 2 * units),
        ),
        compiler_params=params(24),
        cost_estimate=cost(1),
        name="feed_forward_weights",
    )(scalar, normed, upper, active, out_grad, down)


def fold_kernel(scalar_ref, mine_ref, other_ref, *outs):
    place = scalar_ref[3] >> 1
    for k, out in enumerate(outs):
        out[...] = (mine_ref[place ^ k].astype(WIDE) + other_ref[place ^ k].astype(WIDE)).astype(LOW)


def fold(scalar, mine, other):
    count, rows, cols = mine.shape
    return pl.pallas_call(
        fold_kernel,
        in_specs=[scalars(), whole(), whole()],
        out_specs=(whole(),) * count,
        out_shape=(struct((rows, cols), LOW),) * count,
        compiler_params=params(10),
        cost_estimate=cost(1),
        name="fold",
    )(scalar, mine, other)


def second_back_kernel(scalar_ref, mine_ref, other_ref, hidden_ref, grad_ref, rows_ref, low_ref, *, begin, half):
    size = low_ref.shape[0]
    row = lax.broadcasted_iota(jnp.int32, (size, 1), 0) + (begin + scalar_ref[0] * half)
    grad_normed = mine_ref[...].astype(WIDE) + other_ref[...].astype(WIDE)
    scaled, inverse = standardize(hidden_ref[...])
    grad = jnp.where(row < scalar_ref[1], grad_ref[...].astype(WIDE), 0.0)
    grad = grad + standardize_back(grad_normed, scaled, inverse, rows_ref[1:2, :])
    low_ref[...] = grad.astype(LOW)


def second_back(scalar, mine, other, hidden, out_grad, rows, begin):
    size, depth = hidden.shape
    half = out_grad.shape[0] // 2
    placed = pl.BlockSpec(
        (pl.Element(size), pl.Element(depth)), lambda i, scalar_ref: ((begin + scalar_ref[0] * half) // BLOCK * BLOCK, 0)
    )
    return pl.pallas_call(
        functools.partial(second_back_kernel, begin=begin, half=half),
        grid_spec=pltpu.PrefetchScalarGridSpec(
            num_scalar_prefetch=1,
            grid=(1,),
            in_specs=[whole()] * 2 + [pl.BlockSpec((size, depth), lambda i, scalar_ref: (0, 0)), placed, whole()],
            out_specs=whole(),
        ),
        out_shape=struct((size, depth), LOW),
        compiler_params=params(14),
        cost_estimate=cost(size / 1000),
        name="second_norm_backward",
    )(scalar, mine, other, far(hidden), far(out_grad), rows)


def inward_kernel(scalar_ref, grads_ref, tokens_ref, weights_ref, ahead_ref, back_ref, sums_ref):
    width = grads_ref.shape[0]
    back = lax.dot_general(
        grads_ref[...], weights_ref[:, :width], (((0,), (1,)), ((), ())), preferred_element_type=WIDE
    )
    scaled, _ = standardize(tokens_ref[...].astype(WIDE))
    back_ref[...] = back.astype(LOW)
    add_sums(sums_ref, ahead_ref, back, scaled)


def inward(scalar, grads, tokens, weights, ahead, keep):
    count, depth = tokens.shape
    width = grads.shape[0]
    half = count // 2

    def side(scalar_ref):
        return scalar_ref[0] if keep else 1 - scalar_ref[0]

    return pl.pallas_call(
        inward_kernel,
        grid_spec=pltpu.PrefetchScalarGridSpec(
            num_scalar_prefetch=1,
            grid=(1,),
            in_specs=[
                pl.BlockSpec((width, half), lambda i, scalar_ref: (0, side(scalar_ref))),
                pl.BlockSpec((half, depth), lambda i, scalar_ref: (side(scalar_ref), 0)),
                whole(),
                whole(),
            ],
            out_specs=(whole(), whole()),
        ),
        out_shape=(struct((half, depth), LOW), struct((8, depth), WIDE)),
        compiler_params=params(16),
        cost_estimate=cost(1),
        name="grad_normed",
    )(scalar, grads, tokens, weights, ahead)


def project_back_kernel(scalar_ref, grads_ref, normed_ref, outs_ref, one_ref, two_ref, *outs, width):
    blank = jnp.zeros((LANES - 16, one_ref.shape[1]), WIDE)
    rows = jnp.concatenate([one_ref[...], two_ref[...], blank], axis=0)
    rows = jnp.transpose(rows)[:, : -width % LANES].astype(LOW)
    grads = jnp.transpose(multiply(grads_ref[...], normed_ref[...])).astype(LOW)
    value = jnp.concatenate([grads, rows, outs_ref[...]], axis=1)
    put_shards(scalar_ref[3], outs, value, slice(0, value.shape[1]))


def project_back(scalar, grads, normed, outs_grad, one, two, batch):
    width = grads.shape[0]
    depth = normed.shape[1]
    shapes = shard_shapes(batch, depth, width + -width % LANES + outs_grad.shape[1])
    return pl.pallas_call(
        functools.partial(project_back_kernel, width=width),
        in_specs=[scalars()] + [whole()] * 5,
        out_specs=(whole(),) * len(shapes),
        out_shape=shapes,
        compiler_params=params(16),
        cost_estimate=cost(1),
        name="projection_weights",
    )(scalar, grads, normed, outs_grad, one, two)


def finish_kernel(scalar_ref, mine_ref, other_ref, *refs, sizes, half):
    hidden_refs, (own_ref, full_ref) = refs[: len(sizes)], refs[len(sizes) :]
    i = pl.program_id(0)
    row = lax.broadcasted_iota(jnp.int32, (BLOCK, 1), 0) + (scalar_ref[0] * half + i * BLOCK)
    branch = mine_ref[...].astype(WIDE) + other_ref[...].astype(WIDE)
    first = 0
    for size, hidden_ref in zip(sizes, hidden_refs):
        last = first + size // BLOCK

        @pl.when((i >= first) & (i < last))
        def _():
            low = jnp.where(row < scalar_ref[1], hidden_ref[...] + branch, 0.0).astype(LOW)
            own_ref[...] = low
            full_ref[...] = low

        first = last


def finish(scalar, mine, other, hiddens, count):
    half, depth = mine.shape
    blocks = half // BLOCK
    sizes = tuple(hidden.shape[0] for hidden in hiddens)
    specs = []
    first = 0
    for size in sizes:
        last = size // BLOCK - 1

        def chunk(i, scalar_ref, first=first, last=last):
            return (jnp.clip(i - first, 0, last), 0)

        specs.append(pl.BlockSpec((BLOCK, depth), chunk))
        first += last + 1

    def own(i, scalar_ref):
        return (i, 0)

    return pl.pallas_call(
        functools.partial(finish_kernel, sizes=sizes, half=half),
        grid_spec=pltpu.PrefetchScalarGridSpec(
            num_scalar_prefetch=1,
            grid=(blocks,),
            in_specs=[pl.BlockSpec((BLOCK, depth), own)] * 2 + specs,
            out_specs=(
                pl.BlockSpec((BLOCK, depth), own),
                pl.BlockSpec((BLOCK, depth), lambda i, scalar_ref: (i + scalar_ref[0] * blocks, 0)),
            ),
        ),
        out_shape=(struct((half, depth), LOW), stored_far((count, depth), LOW)),
        compiler_params=params(12),
        cost_estimate=cost(1),
        name="layer_out",
    )(scalar, mine, other, *(far(hidden) for hidden in hiddens))


def first_back_kernel(scalar_ref, mine_ref, other_ref, tokens_ref, grad_ref, rows_ref, own_ref, full_ref):
    grad_normed = mine_ref[...].astype(WIDE) + other_ref[...].astype(WIDE)
    scaled, inverse = standardize(tokens_ref[...].astype(WIDE))
    grad = grad_ref[...].astype(WIDE) + standardize_back(grad_normed, scaled, inverse, rows_ref[0:1, :])
    low = grad.astype(LOW)
    own_ref[...] = low
    full_ref[...] = low


def place_rows(kernel, scalar, owned, spread, fixed, count, begin, half, name):
    depth = owned[0].shape[1]
    blocks = half // STEP

    def own(i, scalar_ref):
        return (i, 0)

    def placed(i, scalar_ref):
        return (begin // STEP + i + scalar_ref[0] * blocks, 0)

    return pl.pallas_call(
        kernel,
        grid_spec=pltpu.PrefetchScalarGridSpec(
            num_scalar_prefetch=1,
            grid=(blocks,),
            in_specs=[pl.BlockSpec((STEP, depth), own)] * 2
            + [pl.BlockSpec((STEP, depth), placed)] * len(spread)
            + [pl.BlockSpec((STEP, depth), own)] * (len(owned) - 2)
            + [whole()] * len(fixed),
            out_specs=(pl.BlockSpec((STEP, depth), own), pl.BlockSpec((STEP, depth), placed)),
        ),
        out_shape=(struct((half, depth), LOW), stored_far((count, depth), LOW)),
        compiler_params=params(12),
        cost_estimate=cost(3),
        name=name,
    )(scalar, *owned[:2], *spread, *owned[2:], *fixed)


def place_kernel(scalar_ref, *refs, parts):
    for source, target in zip(refs[:parts], refs[2 * parts :]):
        target[...] = source[...]


def place(scalar, sources, targets):
    parts = len(sources)
    rows, depth = sources[0].shape
    blocks = rows // STEP
    return pl.pallas_call(
        functools.partial(place_kernel, parts=parts),
        grid_spec=pltpu.PrefetchScalarGridSpec(
            num_scalar_prefetch=1,
            grid=(blocks,),
            in_specs=[pl.BlockSpec((STEP, depth), lambda i, scalar_ref: (i, 0))] * parts
            + [pl.BlockSpec(memory_space=pl.ANY)] * parts,
            out_specs=(pl.BlockSpec((STEP, depth), lambda i, scalar_ref: (i + (1 - scalar_ref[0]) * blocks, 0)),) * parts,
        ),
        out_shape=tuple(stored_far(value.shape, value.dtype) for value in targets),
        input_output_aliases={1 + parts + k: k for k in range(parts)},
        compiler_params=params(12),
        cost_estimate=cost(1),
        name="place",
    )(scalar, *sources, *targets)


def total_kernel(*refs, parts, bounds, flips):
    parts_refs, outs = refs[:parts], refs[parts:]
    if parts == 1:
        pieces = [parts_refs[0][k] for k in range(parts_refs[0].shape[0])]
    else:
        pieces = [ref[...] for ref in parts_refs]
    total = pieces[0].astype(WIDE)
    for piece in pieces[1:]:
        total = total + piece.astype(WIDE)
    for out, (first, last), flip in zip(outs, bounds, flips):
        piece = total[:, first:last]
        out[...] = jnp.transpose(piece) if flip else piece


def total_parts(parts, bounds, flips):
    rows = parts[0].shape[-2]
    shapes = []
    for (first, last), flip in zip(bounds, flips):
        shape = (last - first, rows) if flip else (rows, last - first)
        shapes.append(struct(shape, WIDE))
    return pl.pallas_call(
        functools.partial(total_kernel, parts=len(parts), bounds=bounds, flips=flips),
        in_specs=[whole()] * len(parts),
        out_specs=(whole(),) * len(shapes),
        out_shape=tuple(shapes),
        compiler_params=params(8),
        cost_estimate=cost(1),
        name="total",
    )(*parts)


def exchange_far(scalar, shards, ahead=()):
    if len(shards) == 1:
        size = lax.axis_size("batch")
        parts = shards[0].reshape(size, shards[0].shape[0] // size, shards[0].shape[1])
        return [lax.all_to_all(parts, "batch", 0, 0, tiled=True)]
    sums = fold(scalar, after(shards[0], *ahead), shards[1])
    return [sums[0]] + [swap(piece, "batch", 2 * k) for k, piece in enumerate(sums) if k > 0]


def exchange_near(shards):
    return shards if len(shards) == 1 else (shards[0], swap(shards[1], "batch", 1))


def per_device(tokens, lengths, w_query, w_key, w_value, w_out, w_up, w_down, norm_gain, norm_shift, out_grad):
    count, depth = tokens.shape
    batch = lax.axis_size("batch")
    if lengths.shape[0] != 1 or lax.axis_size("tensor") != 4:
        raise ValueError("unsupported mesh")
    width = w_query.shape[1]
    units = w_up.shape[1]
    tensor = lax.axis_index("tensor").astype(jnp.int32)
    core = tensor & 1
    scalar = jnp.stack([core, lengths[0], tensor >> 1, lax.axis_index("batch").astype(jnp.int32)])
    sure = 2 * count // 3
    half = count // 2
    first = half // 3 * 2
    chunks = ((0, first), (first, half - first))

    blank = jnp.zeros((w_query.shape[0], -(4 * width + 4) % LANES), LOW)
    early = jnp.concatenate([w_query, w_key, w_value, w_out.T, norm_gain.T, norm_shift.T, blank], axis=1)
    late = jnp.concatenate([w_up, w_down.T], axis=1)
    if batch == 8:
        others = gather_far(early)
        early = [early, swap(early, "batch", 1)]
        early += [others[0], swap(others[0], "batch", 1)]
        early += [others[1], swap(after(others[1], early[1], early[3]), "batch", 1)]
        early += [others[2], swap(others[2], "batch", 1)]
        late = after(late, *others, early[1], early[3], early[5])
        near = swap(late, "batch", 2)
        middle = swap(late, "batch", 4)
        beside = swap(late, "batch", 1)
    else:
        early = [lax.all_gather(early, "batch", axis=0, tiled=True)]
        late = [lax.all_gather(late, "batch", axis=0, tiled=True)]

    normed, projected, rows, weights, own_outs = project(scalar, tokens, early, width)
    across = swap(own_outs, "tensor", 2)
    outs = (own_outs, across, swap(own_outs, "tensor", 1), swap(across, "tensor", 1))
    mixed, sums, pieces = [], [], []
    if batch == 8:
        late = [late, beside, near, swap(after(near, own_outs), "batch", 1)]
    for number, (begin, size) in enumerate(chunks):
        local = tuple(range(begin // BLOCK, (begin + size) // BLOCK))
        if number == 1:
            projected = after(projected, *late[3:4])
        part, logs = attend(scalar, projected, local + tuple(k + half // BLOCK for k in local), sure)
        projected = after(projected, part)
        mixed.append(part)
        sums.append(logs)
        across = swap(part, "tensor", 2)
        pieces.append((part, across, swap(part, "tensor", 1), swap(across, "tensor", 1)))
        if number == 0 and batch == 8:
            middle = after(middle, part)
            late += [middle, swap(middle, "batch", 1)]
            last = swap(middle, "batch", 2)
    if batch == 8:
        last = after(last, part)
        late += [last, swap(last, "batch", 1)]
    late = lax.optimization_barrier((*late, *mixed))[: len(late)]
    full_up, full_down = assemble(scalar, late, units)
    rows = after(rows, pieces[-1][1])

    stored = []
    twos, halves, hiddens = jnp.zeros((8, depth), WIDE), [], []
    for (begin, size), piece in zip(chunks, pieces):
        ends = []
        rows = after(rows, *(mine for mine, _ in halves))
        for keep in (False, True):
            back, twos, *stored = feed(
                scalar, tokens, out_grad, piece, outs, full_up, full_down, rows, twos, stored, begin, size, keep
            )
            ends.append(back)
        hiddens.append(stored.pop())
        mine = (ends[1].astype(WIDE) + swap(ends[0], "tensor", 1).astype(WIDE)).astype(LOW)
        halves.append((mine, swap(mine, "tensor", 2)))
    normed_two, active, upper = stored
    normed_two = after(normed_two, *(mine for mine, _ in halves))
    branch_keep, branch_send, *feed_grads = weigh(scalar, normed_two, upper, active, out_grad, full_down, 0)
    feed_parts = exchange_far(scalar, feed_grads)

    beside = swap(branch_send, "tensor", 1)
    grads = []
    for (begin, size), (mine, other), hidden in zip(chunks, halves, hiddens):
        mine = after(mine, *feed_grads)
        low = second_back(scalar, mine, other, hidden, out_grad, rows, begin)
        grads += [low, swap(low, "tensor", 1)]
    branch_mine = (branch_keep.astype(WIDE) + beside.astype(WIDE)).astype(LOW)
    branch_mine = after(branch_mine, *grads)
    branch_other = swap(branch_mine, "tensor", 2)
    projected = after(projected, branch_mine)
    attend_grads, outs_grad, grad_attn = attend_back(
        scalar, projected, own_outs, mixed, sums, grads, chunks, sure
    )

    there = (1 - core) * half
    ends, ones = [], jnp.zeros((8, depth), WIDE)
    for keep in (False, True):
        if keep:
            attend_grads = after(attend_grads, branch_other)
        back, ones = inward(scalar, attend_grads, tokens, weights, ones, keep)
        ends.append(back)
    mine = (ends[1].astype(WIDE) + swap(ends[0], "tensor", 1).astype(WIDE)).astype(LOW)
    other = swap(mine, "tensor", 2)
    project_grads = project_back(scalar, after(attend_grads, mine), normed, outs_grad, ones, twos, batch)
    project_parts = exchange_far(scalar, exchange_near(project_grads))
    own_out, layer_out = finish(scalar, branch_mine, after(branch_other, project_parts[0]), hiddens, count)
    other_out = swap(own_out, "tensor", 1)
    shard_up, shard_down = total_parts(feed_parts, ((0, units), (units, 2 * units)), (False, False))
    last = 3 * width
    final = project_parts[0].shape[-1]
    shard_query, shard_key, shard_value, small, shard_out = total_parts(
        project_parts,
        ((0, width), (width, 2 * width), (2 * width, last), (last, final - width), (final - width, final)),
        (False, False, False, True, True),
    )
    mine = after(mine, own_out, shard_up, small)
    own_grad, grad_input = place_rows(
        first_back_kernel, scalar, (mine, other), (tokens, grad_attn), (rows,), count, 0, half, "first_norm_backward"
    )
    layer_out, grad_input = place(scalar, (other_out, swap(own_grad, "tensor", 1)), (layer_out, grad_input))
    small = small[:16]
    small = small + swap(small, "tensor", 2)
    small = small + swap(small, "tensor", 1)
    shard_gain = jnp.stack([small[0], small[8]])
    shard_shift = jnp.stack([small[1], small[9]])
    return (
        layer_out,
        grad_input,
        shard_query,
        shard_key,
        shard_value,
        shard_out,
        shard_up,
        shard_down.T,
        shard_gain,
        shard_shift,
    )


def solution(mesh):
    tall = P("batch", "tensor")
    wide = P("tensor", "batch")
    rows = P("batch", None)
    pair = P(None, "batch")
    return jax.shard_map(
        per_device,
        mesh=mesh,
        in_specs=(rows, P("batch"), tall, tall, tall, wide, tall, wide, pair, pair, rows),
        out_specs=(rows, rows, tall, tall, tall, wide, tall, wide, pair, pair),
        check_vma=False,
    )
```

```python
import functools

import jax
import jax.numpy as jnp
from jax import lax
from jax.experimental import pallas as pl
from jax.experimental.pallas import tpu as pltpu
from jax.sharding import PartitionSpec as P

HD = 64
EPSILON = 1e-05
LOG2E = 1.4426950408889634
HUGE = 3e38
FAR = -1e30
LOW = jnp.bfloat16
WIDE = jnp.float32
LANES = 128
BLOCK = 256
STEP = 384


def multiply(left, right):
    return lax.dot_general(left, right, (((1,), (0,)), ((), ())), preferred_element_type=WIDE)


def outer_cols(left, right):
    return lax.dot_general(left, right, (((1,), (1,)), ((), ())), preferred_element_type=WIDE)


def inner_rows(left, right):
    return lax.dot_general(left, right, (((0,), (0,)), ((), ())), preferred_element_type=WIDE)


def whole():
    return pl.BlockSpec(memory_space=pltpu.VMEM)


def scalars():
    return pl.BlockSpec(memory_space=pltpu.SMEM)


def struct(shape, dtype):
    return jax.ShapeDtypeStruct(shape, dtype)


def held(shape, dtype):
    return pltpu.VMEM(shape, dtype)


def stored_far(shape, dtype):
    return pltpu.HBM(shape, dtype)


def far(value):
    return pltpu.with_memory_space_constraint(value, pltpu.HBM)


def params(mebibytes):
    return pltpu.CompilerParams(vmem_limit_bytes=mebibytes << 20)


def cost(microseconds):
    return pl.CostEstimate(flops=int(microseconds * 1.1e6), bytes_accessed=0, transcendentals=0)


def after(value, *others):
    return lax.optimization_barrier((value, *others))[0]


def swap(value, axis, bits):
    size = lax.axis_size(axis)
    return lax.ppermute(value, axis, [(i, i ^ bits) for i in range(size)])


def gather_far(shard):
    return [swap(shard, "batch", bits) for bits in (2, 4, 6)]


def pair_sum(keep, send):
    mine = (keep.astype(WIDE) + swap(send, "tensor", 1).astype(WIDE)).astype(LOW)
    return mine, swap(mine, "tensor", 2)


def standardize(values):
    middle = jnp.mean(values, axis=-1, keepdims=True)
    centred = values - middle
    spread = jnp.mean(centred * centred, axis=-1, keepdims=True)
    inverse = lax.rsqrt(spread + EPSILON)
    return centred * inverse, inverse


def standardize_back(grad, scaled, inverse, gain):
    grad = grad * gain
    mean_grad = jnp.mean(grad, axis=-1, keepdims=True)
    mean_cross = jnp.mean(grad * scaled, axis=-1, keepdims=True)
    return inverse * (grad - mean_grad - scaled * mean_cross)


def collect(index, pieces, scratch):
    count = pieces[0].shape[0]
    for bits, piece in enumerate(pieces):
        at = pl.multiple_of((index ^ bits) * count, 32) if len(pieces) > 1 else 0
        scratch[pl.ds(at, count), :] = piece[...]


def project_kernel(scalar_ref, *refs, parts, width, block):
    pieces, refs = refs[:parts], refs[parts:]
    tokens_ref, normed_ref, projected_ref, rows_ref, weights_ref, outs_ref = refs

    @pl.when(pl.program_id(0) == 0)
    def _():
        collect(scalar_ref[3], pieces, weights_ref)
        rows_ref[...] = jnp.transpose(weights_ref[:, 4 * width : 4 * width + LANES].astype(WIDE))[:8, :]
        outs_ref[...] = jnp.transpose(weights_ref[:, 3 * width : 4 * width])

    for k in range(tokens_ref.shape[0] // block):
        part = slice(k * block, (k + 1) * block)
        scaled, _ = standardize(tokens_ref[part, :].astype(WIDE))
        normed = (scaled * rows_ref[0:1, :] + rows_ref[2:3, :]).astype(LOW)
        normed_ref[part, :] = normed
        projected_ref[part, :] = multiply(normed, weights_ref[:, : 3 * width]).astype(LOW)


def project(scalar, tokens, pieces, width):
    count, depth = tokens.shape
    total = pieces[0].shape[1]
    step = 768
    return pl.pallas_call(
        functools.partial(project_kernel, parts=len(pieces), width=width, block=256),
        grid=(count // step,),
        in_specs=[scalars()]
        + [whole()] * len(pieces)
        + [pl.BlockSpec((step, depth), lambda i: (i, 0))],
        out_specs=(
            pl.BlockSpec((step, depth), lambda i: (i, 0)),
            pl.BlockSpec((step, 3 * width), lambda i: (i, 0)),
            pl.BlockSpec((8, depth), lambda i: (0, 0)),
            pl.BlockSpec((depth, total), lambda i: (0, 0)),
            pl.BlockSpec((width, depth), lambda i: (0, 0)),
        ),
        out_shape=(
            stored_far((count, depth), LOW),
            struct((count, 3 * width), LOW),
            struct((8, depth), WIDE),
            struct((depth, total), LOW),
            struct((width, depth), LOW),
        ),
        compiler_params=params(20),
        cost_estimate=cost(4),
        name="project",
    )(scalar, *pieces, pltpu.with_memory_space_constraint(tokens, pltpu.HBM))


def assemble_kernel(scalar_ref, *refs, parts, units):
    pieces, (up_ref, down_ref) = refs[:parts], refs[parts:]
    count = pieces[0].shape[0]
    for bits, piece in enumerate(pieces):
        at = pl.multiple_of((scalar_ref[3] ^ bits) * count, 32) if parts > 1 else 0
        up_ref[pl.ds(at, count), :] = piece[:, :units]
        down_ref[pl.ds(at, count), :] = piece[:, units:]


def assemble(scalar, pieces, units):
    depth = sum(piece.shape[0] for piece in pieces)
    return pl.pallas_call(
        functools.partial(assemble_kernel, parts=len(pieces), units=units),
        in_specs=[scalars()] + [whole()] * len(pieces),
        out_specs=(whole(),) * 2,
        out_shape=(struct((depth, units), LOW), struct((depth, units), LOW)),
        compiler_params=params(10),
        cost_estimate=cost(1),
        name="assemble",
    )(scalar, *pieces)


def sign_of(scores):
    scores = scores.astype(LOW) * LOW(HUGE)
    return jnp.minimum(jnp.maximum(scores, LOW(-1)), LOW(1))


def attend_kernel(scalar_ref, projected_ref, mixed_ref, sums_ref, *, places, heads, sure):
    length = scalar_ref[1]
    factor = LOG2E * HD**-0.5
    width = heads * HD
    for i, place in enumerate(places):
        row0 = place * BLOCK
        here = slice(row0, row0 + BLOCK)
        row = lax.broadcasted_iota(jnp.int32, (BLOCK, 1), 0) + row0
        key = lax.broadcasted_iota(jnp.int32, (BLOCK, BLOCK), 1) + row0
        allowed = key <= jnp.minimum(row, length - 1)
        def each(function):
            return jnp.concatenate([function(h) for h in range(heads)], axis=0)

        def column(kind, h):
            return slice(kind * width + h * HD, kind * width + (h + 1) * HD)

        def split(value, h):
            return value[h * BLOCK : (h + 1) * BLOCK]

        near = each(lambda h: outer_cols(projected_ref[here, column(0, h)], projected_ref[here, column(1, h)]))
        near_size = jnp.where(jnp.concatenate([allowed] * heads, axis=0), jnp.abs(near) * factor, FAR)
        top = jnp.max(near_size, axis=1, keepdims=True)
        if row0 > 0:
            past = each(lambda h: outer_cols(projected_ref[here, column(0, h)], projected_ref[:row0, column(1, h)]))
            past_size = jnp.abs(past) * factor
            if row0 > sure:
                past_key = lax.broadcasted_iota(jnp.int32, (1, row0), 1)
                past_size = jnp.where(past_key < length, past_size, FAR)
            top = jnp.maximum(top, jnp.max(past_size, axis=1, keepdims=True))
            past_prob = jnp.exp2(past_size - top)
            past_signed = past_prob.astype(LOW) * sign_of(past)
        near_prob = jnp.exp2(near_size - top)
        near_signed = near_prob.astype(LOW) * sign_of(near)
        total = jnp.sum(near_prob, axis=1, keepdims=True)
        mixed = each(lambda h: multiply(split(near_signed, h), projected_ref[here, column(2, h)]))
        if row0 > 0:
            total = total + jnp.sum(past_prob, axis=1, keepdims=True)
            mixed = mixed + each(lambda h: multiply(split(past_signed, h), projected_ref[:row0, column(2, h)]))
        mixed = (mixed / total).astype(LOW)
        logs = top + jnp.log2(total)
        outs = [split(mixed, h) for h in range(heads)]
        sums = [split(logs, h) for h in range(heads)]
        part = slice(i * BLOCK, (i + 1) * BLOCK)
        mixed_ref[:, part] = jnp.transpose(jnp.concatenate(outs, axis=1))
        blank = jnp.zeros((BLOCK, LANES - heads), WIDE)
        sums_ref[i] = jnp.transpose(jnp.concatenate(sums + [blank], axis=1))[:8, :]


def attend(scalar, projected, places, sure):
    width = projected.shape[1] // 3
    heads = width // HD
    return pl.pallas_call(
        functools.partial(attend_kernel, places=places, heads=heads, sure=sure),
        in_specs=[scalars(), whole()],
        out_specs=(whole(), whole()),
        out_shape=(struct((width, len(places) * BLOCK), LOW), struct((len(places), 8, BLOCK), WIDE)),
        compiler_params=params(16),
        cost_estimate=cost(1),
        name="attend_forward",
    )(scalar, projected)


def attend_back_kernel(scalar_ref, *refs, chunks, rows, heads, sure):
    length = scalar_ref[1]
    core = scalar_ref[0]
    projected_ref, outs_ref, refs = refs[0], refs[1], refs[2:]
    mixed_refs, refs = refs[: len(chunks)], refs[len(chunks) :]
    sums_refs, refs = refs[: len(chunks)], refs[len(chunks) :]
    grad_refs, refs = refs[: 2 * len(chunks)], refs[2 * len(chunks) :]
    grads_ref, outs_grad_ref, whole_ref, grad_mixed, delta, logs, dq_turned = refs
    scaling = HD**-0.5
    factor = LOG2E * scaling
    width = heads * HD
    blocks = rows // BLOCK
    outs_grad = jnp.zeros(outs_ref.shape, WIDE)
    half = blocks // 2
    for number, (begin, size) in enumerate(chunks):
        for side in range(2):
            for k in range(size // BLOCK):
                local = side * size + k * BLOCK
                inside = slice(local, local + BLOCK)
                i = side * half + begin // BLOCK + k
                rows_i = slice(i * BLOCK, (i + 1) * BLOCK)
                mine = grad_refs[2 * number][k * BLOCK : (k + 1) * BLOCK, :]
                other = grad_refs[2 * number + 1][k * BLOCK : (k + 1) * BLOCK, :]

                @pl.when(core == side)
                def _():
                    whole_ref[rows_i, :] = mine

                @pl.when(core != side)
                def _():
                    whole_ref[rows_i, :] = other

                grad = whole_ref[rows_i, :]
                mixed = mixed_refs[number][:, inside]
                outs_grad = outs_grad + multiply(mixed, grad)
                turned = outer_cols(outs_ref[...], grad)
                grad_mixed[rows_i, :] = jnp.transpose(turned).astype(LOW)
                logs[:, rows_i] = sums_refs[number][local // BLOCK]
                both = turned.astype(LOW).astype(WIDE) * mixed.astype(WIDE)
                for h in range(heads):
                    delta[h : h + 1, rows_i] = jnp.sum(both[h * HD : (h + 1) * HD, :], axis=0, keepdims=True)
    outs_grad_ref[...] = jnp.transpose(outs_grad).astype(LOW)
    for j in range(blocks):
        here = slice(j * BLOCK, (j + 1) * BLOCK)
        later = slice((j + 1) * BLOCK, rows)
        dks, dvs = [], []
        for h in range(heads):
            cols = slice(h * HD, (h + 1) * HD)
            k = projected_ref[here, width + h * HD : width + (h + 1) * HD]
            v = projected_ref[here, 2 * width + h * HD : 2 * width + (h + 1) * HD]
            dk = jnp.zeros((BLOCK, HD), WIDE)
            dv = jnp.zeros((BLOCK, HD), WIDE)
            for part in (here, later):
                span = part.stop - part.start
                if span == 0:
                    continue
                q = projected_ref[part, cols]
                g = grad_mixed[part, cols]
                scores = outer_cols(k, q)
                grad_weights = outer_cols(v, g)
                reach = jnp.abs(scores) * factor - logs[h : h + 1, part]
                if part is here:
                    key = lax.broadcasted_iota(jnp.int32, (BLOCK, span), 0) + j * BLOCK
                    row = lax.broadcasted_iota(jnp.int32, (1, span), 1) + j * BLOCK
                    reach = jnp.where(key <= jnp.minimum(row, length - 1), reach, FAR)
                elif (j + 1) * BLOCK > sure:
                    key = lax.broadcasted_iota(jnp.int32, (BLOCK, 1), 0) + j * BLOCK
                    reach = jnp.where(key < length, reach, FAR)
                sign = sign_of(scores)
                weights = jnp.exp2(reach)
                signed = sign.astype(WIDE)
                raw = (weights * (grad_weights - signed * delta[h : h + 1, part])).astype(LOW) * (sign * sign)
                dv = dv + multiply(weights.astype(LOW) * sign, g)
                dk = dk + multiply(raw, q)
                more = inner_rows(k, raw)
                if j == 0:
                    dq_turned[cols, part] = more
                else:
                    dq_turned[cols, part] += more
            dks.append(dk * scaling)
            dvs.append(dv)
        grads_ref[:width, here] = (dq_turned[:, here] * scaling).astype(LOW)
        grads_ref[width : 2 * width, here] = jnp.transpose(jnp.concatenate(dks, axis=1)).astype(LOW)
        grads_ref[2 * width :, here] = jnp.transpose(jnp.concatenate(dvs, axis=1)).astype(LOW)


def attend_back(scalar, projected, outs, mixed, sums, grads, chunks, sure):
    rows = projected.shape[0]
    width = projected.shape[1] // 3
    depth = outs.shape[1]
    heads = width // HD
    return pl.pallas_call(
        functools.partial(attend_back_kernel, chunks=chunks, rows=rows, heads=heads, sure=sure),
        in_specs=[scalars()] + [whole()] * (2 + 4 * len(chunks)),
        out_specs=(whole(),) * 3,
        out_shape=(struct((3 * width, rows), LOW), struct((depth, width), LOW), struct((rows, depth), LOW)),
        scratch_shapes=[
            pltpu.VMEM((rows, width), LOW),
            pltpu.VMEM((8, rows), WIDE),
            pltpu.VMEM((8, rows), WIDE),
            pltpu.VMEM((width, rows), WIDE),
        ],
        compiler_params=params(24),
        cost_estimate=cost(8),
        name="attend_backward",
    )(scalar, projected, outs, *mixed, *sums, *grads)


def gelu_pair(up):
    root = 0.7978845608028654
    square = up * up
    bent = jnp.tanh(up * (root + (root * 0.044715) * square))
    half = 0.5 * bent + 0.5
    slope = half + (0.5 * up) * (1.0 - bent * bent) * (root + (3 * root * 0.044715) * square)
    return up * half, slope


def add_sums(sums_ref, ahead_ref, back, scaled):
    sums_ref[0:1, :] = ahead_ref[0:1, :] + jnp.sum(back * scaled, axis=0, keepdims=True)
    sums_ref[1:2, :] = ahead_ref[1:2, :] + jnp.sum(back, axis=0, keepdims=True)
    sums_ref[2:8, :] = ahead_ref[2:8, :]


def feed_kernel(scalar_ref, *refs, begin, size, half, keep, given):
    tokens_ref, grad_ref, m0, m1, m2, m3, o0, o1, o2, o3, up_ref, down_ref, rows_ref, ahead_ref = refs[:14]
    results = refs[14 + given : -1]
    back_ref, sums_ref, normed_ref, active_ref, upper_ref = results[:5]
    mixed_ref = refs[-1]
    place = scalar_ref[0] if keep else 1 - scalar_ref[0]
    row0 = pl.multiple_of(begin + place * half, BLOCK)
    here = pl.ds(row0, size)
    row = lax.broadcasted_iota(jnp.int32, (size, 1), 0) + row0

    @pl.when(scalar_ref[2] == 0)
    def _():
        across = inner_rows(m0[...], o0[...]) + inner_rows(m1[...], o1[...])
        mixed_ref[...] = across + inner_rows(m2[...], o2[...]) + inner_rows(m3[...], o3[...])

    @pl.when(scalar_ref[2] != 0)
    def _():
        across = inner_rows(m1[...], o1[...]) + inner_rows(m0[...], o0[...])
        mixed_ref[...] = across + inner_rows(m3[...], o3[...]) + inner_rows(m2[...], o2[...])

    hidden = tokens_ref[...].astype(WIDE) + mixed_ref[...]
    if keep:
        results[5][...] = hidden
    scaled, _ = standardize(hidden)
    normed = (scaled * rows_ref[1:2, :] + rows_ref[3:4, :]).astype(LOW)
    normed_ref[here, :] = normed
    grad = jnp.where(row < scalar_ref[1], grad_ref[...].astype(WIDE), 0.0).astype(LOW)
    back = jnp.zeros(hidden.shape, WIDE)
    units = up_ref.shape[1]
    for first in range(0, units, BLOCK):
        part = slice(first, first + BLOCK)
        active, slope = gelu_pair(multiply(normed, up_ref[:, part]))
        active_ref[here, part] = active.astype(LOW)
        upper = (multiply(grad, down_ref[:, part]) * slope).astype(LOW)
        upper_ref[here, part] = upper
        back = back + outer_cols(upper, up_ref[:, part])
    back_ref[...] = back.astype(LOW)
    add_sums(sums_ref, ahead_ref, back, scaled)


def feed(scalar, tokens, out_grad, mixed, outs, up, down, rows, ahead, stored, begin, size, keep):
    count, depth = tokens.shape
    units = up.shape[1]
    width = outs[0].shape[0]
    half = count // 2

    def side(scalar_ref):
        return scalar_ref[0] if keep else 1 - scalar_ref[0]

    def placed(i, scalar_ref):
        return ((begin + side(scalar_ref) * half) // BLOCK * BLOCK, 0)

    def inside(i, scalar_ref):
        return (0, side(scalar_ref))

    rows_spec = pl.BlockSpec((pl.Element(size), pl.Element(depth)), placed)
    out_shape = (
        struct((size, depth), LOW),
        struct((8, depth), WIDE),
        struct((count, depth), LOW),
        struct((count, units), LOW),
        struct((count, units), LOW),
        stored_far((size, depth), WIDE),
    )[: 6 if keep else 5]
    return pl.pallas_call(
        functools.partial(feed_kernel, begin=begin, size=size, half=half, keep=keep, given=len(stored)),
        grid_spec=pltpu.PrefetchScalarGridSpec(
            num_scalar_prefetch=1,
            grid=(1,),
            in_specs=[rows_spec] * 2
            + [pl.BlockSpec((width, size), inside)] * 4
            + [whole()] * 8
            + [pl.BlockSpec(memory_space=pl.ANY)] * len(stored),
            out_specs=(whole(),) * len(out_shape),
            scratch_shapes=[pltpu.VMEM((size, depth), WIDE)],
        ),
        out_shape=out_shape,
        input_output_aliases={15 + k: 2 + k for k in range(len(stored))},
        compiler_params=params(20),
        cost_estimate=cost(size / 1000),
        name="feed_forward",
    )(scalar, tokens, out_grad, *mixed, *outs, up, down, rows, ahead, *stored)


def put_shards(index, outs, value, cols):
    if len(outs) == 1:
        outs[0][:, cols] = value
        return
    mine, other = outs
    rows = value.shape[0] // 8
    for place in range(8):
        piece = value[place * rows : (place + 1) * rows, :]

        @pl.when((index & 1) == place % 2)
        def _():
            mine[place // 2, :, cols] = piece

        @pl.when((index & 1) != place % 2)
        def _():
            other[place // 2, :, cols] = piece


def shard_shapes(batch, depth, cols):
    if batch != 8:
        return (stored_far((depth, cols), LOW),)
    return (struct((4, depth // 8, cols), LOW),) * 2


def weigh_kernel(scalar_ref, normed_ref, upper_ref, active_ref, grad_ref, down_ref, keep_ref, send_ref, *refs):
    outs, (up_sum, down_sum) = refs[:-2], refs[-2:]
    i = pl.program_id(0)
    units = down_ref.shape[1]
    half = grad_ref.shape[0]
    row0 = pl.multiple_of((scalar_ref[0] ^ 1 ^ i) * half, BLOCK)
    here = pl.ds(row0, half)
    row = lax.broadcasted_iota(jnp.int32, (half, 1), 0) + row0
    active = active_ref[here, :]
    branch = outer_cols(active, down_ref[...]).astype(LOW)
    grad = jnp.where(row < scalar_ref[1], grad_ref[...].astype(WIDE), 0.0).astype(LOW)
    up = inner_rows(normed_ref[here, :], upper_ref[here, :])
    down = inner_rows(grad, active)

    @pl.when(i == 0)
    def _():
        send_ref[...] = branch
        up_sum[...] = up
        down_sum[...] = down

    @pl.when(i == 1)
    def _():
        keep_ref[...] = branch
        put_shards(scalar_ref[3], outs, (up_sum[...] + up).astype(LOW), slice(0, units))
        put_shards(scalar_ref[3], outs, (down_sum[...] + down).astype(LOW), slice(units, 2 * units))


def weigh(scalar, normed, upper, active, out_grad, down, batch):
    count, depth = normed.shape
    units = down.shape[1]
    half = count // 2
    return pl.pallas_call(
        weigh_kernel,
        grid_spec=pltpu.PrefetchScalarGridSpec(
            num_scalar_prefetch=1,
            grid=(2,),
            in_specs=[whole()] * 3
            + [pl.BlockSpec((half, depth), lambda i, scalar_ref: (scalar_ref[0] ^ 1 ^ i, 0)), whole()],
            out_specs=(whole(),) * (2 + len(shard_shapes(batch, depth, 2 * units))),
            scratch_shapes=[pltpu.VMEM((depth, units), WIDE)] * 2,
        ),
        out_shape=(
            stored_far((half, depth), LOW),
            stored_far((half, depth), LOW),
            *shard_shapes(batch, depth, 2 * units),
        ),
        compiler_params=params(24),
        cost_estimate=cost(1),
        name="feed_forward_weights",
    )(scalar, normed, upper, active, out_grad, down)


def fold_kernel(scalar_ref, mine_ref, other_ref, *outs):
    place = scalar_ref[3] >> 1
    for k, out in enumerate(outs):
        out[...] = (mine_ref[place ^ k].astype(WIDE) + other_ref[place ^ k].astype(WIDE)).astype(LOW)


def fold(scalar, mine, other):
    count, rows, cols = mine.shape
    return pl.pallas_call(
        fold_kernel,
        in_specs=[scalars(), whole(), whole()],
        out_specs=(whole(),) * count,
        out_shape=(struct((rows, cols), LOW),) * count,
        compiler_params=params(10),
        cost_estimate=cost(1),
        name="fold",
    )(scalar, mine, other)


def second_back_kernel(scalar_ref, mine_ref, other_ref, hidden_ref, grad_ref, rows_ref, low_ref, *, begin, half):
    size = low_ref.shape[0]
    row = lax.broadcasted_iota(jnp.int32, (size, 1), 0) + (begin + scalar_ref[0] * half)
    grad_normed = mine_ref[...].astype(WIDE) + other_ref[...].astype(WIDE)
    scaled, inverse = standardize(hidden_ref[...])
    grad = jnp.where(row < scalar_ref[1], grad_ref[...].astype(WIDE), 0.0)
    grad = grad + standardize_back(grad_normed, scaled, inverse, rows_ref[1:2, :])
    low_ref[...] = grad.astype(LOW)


def second_back(scalar, mine, other, hidden, out_grad, rows, begin, guess):
    size, depth = hidden.shape
    half = out_grad.shape[0] // 2
    placed = pl.BlockSpec(
        (pl.Element(size), pl.Element(depth)), lambda i, scalar_ref: ((begin + scalar_ref[0] * half) // BLOCK * BLOCK, 0)
    )
    return pl.pallas_call(
        functools.partial(second_back_kernel, begin=begin, half=half),
        grid_spec=pltpu.PrefetchScalarGridSpec(
            num_scalar_prefetch=1,
            grid=(1,),
            in_specs=[whole()] * 2 + [pl.BlockSpec((size, depth), lambda i, scalar_ref: (0, 0)), placed, whole()],
            out_specs=whole(),
        ),
        out_shape=struct((size, depth), LOW),
        compiler_params=params(14),
        cost_estimate=cost(guess),
        name="second_norm_backward",
    )(scalar, mine, other, far(hidden), far(out_grad), rows)


def inward_kernel(scalar_ref, grads_ref, tokens_ref, weights_ref, ahead_ref, back_ref, sums_ref):
    width = grads_ref.shape[0]
    back = lax.dot_general(
        grads_ref[...], weights_ref[:, :width], (((0,), (1,)), ((), ())), preferred_element_type=WIDE
    )
    scaled, _ = standardize(tokens_ref[...].astype(WIDE))
    back_ref[...] = back.astype(LOW)
    add_sums(sums_ref, ahead_ref, back, scaled)


def inward(scalar, grads, tokens, weights, ahead, keep):
    count, depth = tokens.shape
    width = grads.shape[0]
    half = count // 2

    def side(scalar_ref):
        return scalar_ref[0] if keep else 1 - scalar_ref[0]

    return pl.pallas_call(
        inward_kernel,
        grid_spec=pltpu.PrefetchScalarGridSpec(
            num_scalar_prefetch=1,
            grid=(1,),
            in_specs=[
                pl.BlockSpec((width, half), lambda i, scalar_ref: (0, side(scalar_ref))),
                pl.BlockSpec((half, depth), lambda i, scalar_ref: (side(scalar_ref), 0)),
                whole(),
                whole(),
            ],
            out_specs=(whole(), whole()),
        ),
        out_shape=(struct((half, depth), LOW), struct((8, depth), WIDE)),
        compiler_params=params(16),
        cost_estimate=cost(1),
        name="grad_normed",
    )(scalar, grads, tokens, weights, ahead)


def project_back_kernel(scalar_ref, grads_ref, normed_ref, outs_ref, one_ref, two_ref, *outs, width):
    blank = jnp.zeros((LANES - 16, one_ref.shape[1]), WIDE)
    rows = jnp.concatenate([one_ref[...], two_ref[...], blank], axis=0)
    rows = jnp.transpose(rows)[:, : -width % LANES].astype(LOW)
    grads = jnp.transpose(multiply(grads_ref[...], normed_ref[...])).astype(LOW)
    value = jnp.concatenate([grads, rows, outs_ref[...]], axis=1)
    put_shards(scalar_ref[3], outs, value, slice(0, value.shape[1]))


def project_back(scalar, grads, normed, outs_grad, one, two, batch):
    width = grads.shape[0]
    depth = normed.shape[1]
    shapes = shard_shapes(batch, depth, width + -width % LANES + outs_grad.shape[1])
    return pl.pallas_call(
        functools.partial(project_back_kernel, width=width),
        in_specs=[scalars()] + [whole()] * 5,
        out_specs=(whole(),) * len(shapes),
        out_shape=shapes,
        compiler_params=params(16),
        cost_estimate=cost(1),
        name="projection_weights",
    )(scalar, grads, normed, outs_grad, one, two)


def finish_kernel(scalar_ref, mine_ref, other_ref, *refs, sizes, half):
    hidden_refs, owns, full_ref = refs[: len(sizes)], refs[len(sizes) : -1], refs[-1]
    hidden = jnp.concatenate([ref[...] for ref in hidden_refs], axis=0)
    row = lax.broadcasted_iota(jnp.int32, (half, 1), 0) + scalar_ref[0] * half
    branch = mine_ref[...].astype(WIDE) + other_ref[...].astype(WIDE)
    low = jnp.where(row < scalar_ref[1], hidden + branch, 0.0).astype(LOW)
    full_ref[...] = low
    for k, own_ref in enumerate(owns):
        own_ref[...] = low[k * STEP : (k + 1) * STEP, :]


def finish(scalar, mine, other, hiddens, count):
    half, depth = mine.shape
    sizes = tuple(hidden.shape[0] for hidden in hiddens)
    parts = half // STEP
    return pl.pallas_call(
        functools.partial(finish_kernel, sizes=sizes, half=half),
        grid_spec=pltpu.PrefetchScalarGridSpec(
            num_scalar_prefetch=1,
            grid=(1,),
            in_specs=[whole()] * (2 + len(sizes)),
            out_specs=(whole(),) * parts
            + (pl.BlockSpec((half, depth), lambda i, scalar_ref: (scalar_ref[0], 0)),),
        ),
        out_shape=(stored_far((STEP, depth), LOW),) * parts + (stored_far((count, depth), LOW),),
        compiler_params=params(16),
        cost_estimate=cost(1),
        name="layer_out",
    )(scalar, mine, other, *(far(hidden) for hidden in hiddens))


def first_back_kernel(scalar_ref, mine_ref, other_ref, tokens_ref, grad_ref, rows_ref, *refs):
    own_ref, full_ref = refs[-2:]
    grad_normed = mine_ref[...].astype(WIDE) + other_ref[...].astype(WIDE)
    scaled, inverse = standardize(tokens_ref[...].astype(WIDE))
    grad = grad_ref[...].astype(WIDE) + standardize_back(grad_normed, scaled, inverse, rows_ref[0:1, :])
    low = grad.astype(LOW)
    own_ref[...] = low
    full_ref[...] = low


def first_back(scalar, mine, other, tokens, grad, rows, number, stored):
    size, depth = mine.shape
    count = tokens.shape[0]
    blocks = count // 2 // size

    def placed(i, scalar_ref):
        return (number + scalar_ref[0] * blocks, 0)

    return pl.pallas_call(
        first_back_kernel,
        grid_spec=pltpu.PrefetchScalarGridSpec(
            num_scalar_prefetch=1,
            grid=(1,),
            in_specs=[whole(), whole()]
            + [pl.BlockSpec((size, depth), placed)] * 2
            + [whole()]
            + [pl.BlockSpec(memory_space=pl.ANY)] * len(stored),
            out_specs=(whole(), pl.BlockSpec((size, depth), placed)),
        ),
        out_shape=(stored_far((size, depth), LOW), stored_far((count, depth), LOW)),
        input_output_aliases={6: 1} if stored else {},
        compiler_params=params(12),
        cost_estimate=cost(1),
        name="first_norm_backward",
    )(scalar, mine, other, tokens, grad, rows, *stored)


def place_kernel(scalar_ref, *refs, parts):
    first_refs, second_refs = refs[:parts], refs[parts : 2 * parts]
    for k in range(parts):

        @pl.when(pl.program_id(0) == k)
        def _():
            refs[-2][...] = first_refs[k][...]
            refs[-1][...] = second_refs[k][...]


def place(scalar, first, second, targets):
    parts = len(first)
    rows, depth = first[0].shape
    placed = pl.BlockSpec((rows, depth), lambda i, scalar_ref: (i + (1 - scalar_ref[0]) * parts, 0))
    return pl.pallas_call(
        functools.partial(place_kernel, parts=parts),
        grid_spec=pltpu.PrefetchScalarGridSpec(
            num_scalar_prefetch=1,
            grid=(parts,),
            in_specs=[whole()] * (2 * parts) + [pl.BlockSpec(memory_space=pl.ANY)] * 2,
            out_specs=(placed, placed),
        ),
        out_shape=tuple(stored_far(value.shape, value.dtype) for value in targets),
        input_output_aliases={1 + 2 * parts: 0, 2 + 2 * parts: 1},
        compiler_params=params(12),
        cost_estimate=cost(1),
        name="place",
    )(scalar, *first, *second, *targets)


def total_kernel(*refs, parts, bounds, flips):
    parts_refs, outs = refs[:parts], refs[parts:]
    if parts == 1:
        pieces = [parts_refs[0][k] for k in range(parts_refs[0].shape[0])]
    else:
        pieces = [ref[...] for ref in parts_refs]
    total = pieces[0].astype(WIDE)
    for piece in pieces[1:]:
        total = total + piece.astype(WIDE)
    for out, (first, last), flip in zip(outs, bounds, flips):
        piece = total[:, first:last]
        out[...] = jnp.transpose(piece) if flip else piece


def total_parts(parts, bounds, flips, guess):
    rows = parts[0].shape[-2]
    shapes = []
    for (first, last), flip in zip(bounds, flips):
        shape = (last - first, rows) if flip else (rows, last - first)
        shapes.append(struct(shape, WIDE))
    return pl.pallas_call(
        functools.partial(total_kernel, parts=len(parts), bounds=bounds, flips=flips),
        in_specs=[whole()] * len(parts),
        out_specs=(whole(),) * len(shapes),
        out_shape=tuple(shapes),
        compiler_params=params(8),
        cost_estimate=cost(guess),
        name="total",
    )(*parts)


def exchange_far(scalar, shards, ahead=()):
    if len(shards) == 1:
        size = lax.axis_size("batch")
        parts = shards[0].reshape(size, shards[0].shape[0] // size, shards[0].shape[1])
        return [lax.all_to_all(parts, "batch", 0, 0, tiled=True)]
    sums = fold(scalar, after(shards[0], *ahead), shards[1])
    return [sums[0]] + [swap(piece, "batch", 2 * k) for k, piece in enumerate(sums) if k > 0]


def exchange_near(shards):
    return shards if len(shards) == 1 else (shards[0], swap(shards[1], "batch", 1))


def per_device(tokens, lengths, w_query, w_key, w_value, w_out, w_up, w_down, norm_gain, norm_shift, out_grad):
    count, depth = tokens.shape
    batch = lax.axis_size("batch")
    if lengths.shape[0] != 1 or lax.axis_size("tensor") != 4:
        raise ValueError("unsupported mesh")
    width = w_query.shape[1]
    units = w_up.shape[1]
    tensor = lax.axis_index("tensor").astype(jnp.int32)
    core = tensor & 1
    scalar = jnp.stack([core, lengths[0], tensor >> 1, lax.axis_index("batch").astype(jnp.int32)])
    sure = 2 * count // 3
    half = count // 2
    first = half // 3 * 2
    chunks = ((0, first), (first, half - first))

    blank = jnp.zeros((w_query.shape[0], -(4 * width + 4) % LANES), LOW)
    early = jnp.concatenate([w_query, w_key, w_value, w_out.T, norm_gain.T, norm_shift.T, blank], axis=1)
    late = jnp.concatenate([w_up, w_down.T], axis=1)
    if batch == 8:
        others = gather_far(early)
        early = [early, swap(early, "batch", 1)]
        early += [others[0], swap(others[0], "batch", 1)]
        early += [others[1], swap(after(others[1], early[1], early[3]), "batch", 1)]
        early += [others[2], swap(others[2], "batch", 1)]
        late = after(late, *others, early[1], early[3], early[5])
        near = swap(late, "batch", 2)
        middle = swap(late, "batch", 4)
        beside = swap(late, "batch", 1)
    else:
        early = [lax.all_gather(early, "batch", axis=0, tiled=True)]
        late = [lax.all_gather(late, "batch", axis=0, tiled=True)]

    normed, projected, rows, weights, own_outs = project(scalar, tokens, early, width)
    across = swap(own_outs, "tensor", 2)
    outs = (own_outs, across, swap(own_outs, "tensor", 1), swap(across, "tensor", 1))
    mixed, sums, pieces = [], [], []
    if batch == 8:
        late = [late, beside, near, swap(after(near, own_outs), "batch", 1)]
    for number, (begin, size) in enumerate(chunks):
        local = tuple(range(begin // BLOCK, (begin + size) // BLOCK))
        if number == 1:
            projected = after(projected, *late[3:4])
        part, logs = attend(scalar, projected, local + tuple(k + half // BLOCK for k in local), sure)
        projected = after(projected, part)
        mixed.append(part)
        sums.append(logs)
        across = swap(part, "tensor", 2)
        pieces.append((part, across, swap(part, "tensor", 1), swap(across, "tensor", 1)))
        if number == 0 and batch == 8:
            middle = after(middle, part)
            late += [middle, swap(middle, "batch", 1)]
            last = swap(middle, "batch", 2)
    if batch == 8:
        last = after(last, part)
        late += [last, swap(last, "batch", 1)]
    late = lax.optimization_barrier((*late, *mixed))[: len(late)]
    full_up, full_down = assemble(scalar, late, units)
    rows = after(rows, *pieces[-1][1:])

    stored, sends = [], []
    twos, halves, hiddens = jnp.zeros((8, depth), WIDE), [], []
    for (begin, size), piece in zip(chunks, pieces):
        back, twos, *stored = feed(
            scalar, tokens, out_grad, piece, outs, full_up, full_down, rows, twos, stored, begin, size, False
        )
        sends.append(back)
    for (begin, size), piece, send in zip(chunks, pieces, sends):
        rows = after(rows, *(mine for mine, _ in halves))
        back, twos, *stored = feed(
            scalar, tokens, out_grad, piece, outs, full_up, full_down, rows, twos, stored, begin, size, True
        )
        hiddens.append(stored.pop())
        mine = (back.astype(WIDE) + swap(send, "tensor", 1).astype(WIDE)).astype(LOW)
        halves.append((mine, swap(mine, "tensor", 2)))
    normed_two, active, upper = stored
    normed_two = after(normed_two, *(mine for mine, _ in halves))
    branch_keep, branch_send, *feed_grads = weigh(scalar, normed_two, upper, active, out_grad, full_down, 0)
    feed_parts = exchange_far(scalar, feed_grads)

    beside = swap(branch_send, "tensor", 1)
    grads = []
    for (begin, size), (mine, other), hidden in zip(chunks, halves, hiddens):
        mine = after(mine, *feed_grads)
        low = second_back(scalar, mine, other, hidden, out_grad, rows, begin, 40000 if grads else 1)
        grads += [low, swap(low, "tensor", 1)]
    branch_mine = (branch_keep.astype(WIDE) + beside.astype(WIDE)).astype(LOW)
    branch_mine = after(branch_mine, halves[-1][1])
    branch_other = swap(branch_mine, "tensor", 2)
    projected = after(projected, branch_mine)
    attend_grads, outs_grad, grad_attn = attend_back(
        scalar, projected, own_outs, mixed, sums, grads, chunks, sure
    )

    there = (1 - core) * half
    ends, ones = [], jnp.zeros((8, depth), WIDE)
    for keep in (False, True):
        back, ones = inward(scalar, attend_grads, tokens, weights, ones, keep)
        ends.append(back)
    project_grads = project_back(scalar, attend_grads, normed, outs_grad, ones, twos, batch)
    keep = after(ends[1], branch_other, *project_grads)
    beside = swap(ends[0], "tensor", 1)
    tails = []
    for begin in range(0, half, STEP):
        part = slice(begin, begin + STEP)
        mine = (keep[part].astype(WIDE) + beside[part].astype(WIDE)).astype(LOW)
        tails.append((mine, swap(mine, "tensor", 2)))
    *own_out, layer_out = finish(scalar, branch_mine, after(branch_other, tails[-1][0]), hiddens, count)
    project_parts = exchange_far(scalar, exchange_near(project_grads), own_out)
    other_out = [swap(own, "tensor", 1) for own in own_out]
    stored, other_grads = [], []
    for number, (mine, other) in enumerate(tails):
        mine = after(mine, *own_out)
        own_grad, *stored = first_back(scalar, mine, other, tokens, grad_attn, rows, number, stored)
        other_grads.append(swap(own_grad, "tensor", 1))
    feed_parts[0] = after(feed_parts[0], own_grad)
    shard_up, shard_down = total_parts(feed_parts, ((0, units), (units, 2 * units)), (False, False), 1)
    last = 3 * width
    final = project_parts[0].shape[-1]
    project_parts[0] = after(project_parts[0], shard_up)
    (small,) = total_parts(project_parts, ((last, final - width),), (True,), 40000)
    small = small[:16]
    across = swap(small, "tensor", 2)
    project_parts[0] = after(project_parts[0], small)
    shard_query, shard_key, shard_value, shard_out = total_parts(
        project_parts,
        ((0, width), (width, 2 * width), (2 * width, last), (final - width, final)),
        (False, False, False, True),
        1,
    )
    small = small + after(across, shard_query)
    across = swap(small, "tensor", 1)
    other_out[0] = after(other_out[0], small)
    layer_out, grad_input = place(scalar, other_out, other_grads, (layer_out, stored[0]))
    small = small + after(across, layer_out)
    shard_gain = jnp.stack([small[0], small[8]])
    shard_shift = jnp.stack([small[1], small[9]])
    return (
        layer_out,
        grad_input,
        shard_query,
        shard_key,
        shard_value,
        shard_out,
        shard_up,
        shard_down.T,
        shard_gain,
        shard_shift,
    )


def solution(mesh):
    tall = P("batch", "tensor")
    wide = P("tensor", "batch")
    rows = P("batch", None)
    pair = P(None, "batch")
    return jax.shard_map(
        per_device,
        mesh=mesh,
        in_specs=(rows, P("batch"), tall, tall, tall, wide, tall, wide, pair, pair, rows),
        out_specs=(rows, rows, tall, tall, tall, wide, tall, wide, pair, pair),
        check_vma=False,
    )
```

```python
import functools

import jax
import jax.numpy as jnp
from jax import lax
from jax.experimental import pallas as pl
from jax.experimental.pallas import tpu as pltpu
from jax.sharding import PartitionSpec as P

HD = 64
EPSILON = 1e-05
LOG2E = 1.4426950408889634
HUGE = 3e38
FAR = -1e30
LOW = jnp.bfloat16
WIDE = jnp.float32
LANES = 128
BLOCK = 256
STEP = 384


def multiply(left, right):
    return lax.dot_general(left, right, (((1,), (0,)), ((), ())), preferred_element_type=WIDE)


def outer_cols(left, right):
    return lax.dot_general(left, right, (((1,), (1,)), ((), ())), preferred_element_type=WIDE)


def inner_rows(left, right):
    return lax.dot_general(left, right, (((0,), (0,)), ((), ())), preferred_element_type=WIDE)


def whole():
    return pl.BlockSpec(memory_space=pltpu.VMEM)


def scalars():
    return pl.BlockSpec(memory_space=pltpu.SMEM)


def struct(shape, dtype):
    return jax.ShapeDtypeStruct(shape, dtype)


def held(shape, dtype):
    return pltpu.VMEM(shape, dtype)


def stored_far(shape, dtype):
    return pltpu.HBM(shape, dtype)


def far(value):
    return pltpu.with_memory_space_constraint(value, pltpu.HBM)


def params(mebibytes):
    return pltpu.CompilerParams(vmem_limit_bytes=mebibytes << 20)


def cost(microseconds):
    return pl.CostEstimate(flops=int(microseconds * 1.1e6), bytes_accessed=0, transcendentals=0)


def after(value, *others):
    return lax.optimization_barrier((value, *others))[0]


def swap(value, axis, bits):
    size = lax.axis_size(axis)
    return lax.ppermute(value, axis, [(i, i ^ bits) for i in range(size)])


def gather_far(shard):
    return [swap(shard, "batch", bits) for bits in (2, 4, 6)]


def pair_sum(keep, send):
    mine = (keep.astype(WIDE) + swap(send, "tensor", 1).astype(WIDE)).astype(LOW)
    return mine, swap(mine, "tensor", 2)


def standardize(values):
    middle = jnp.mean(values, axis=-1, keepdims=True)
    centred = values - middle
    spread = jnp.mean(centred * centred, axis=-1, keepdims=True)
    inverse = lax.rsqrt(spread + EPSILON)
    return centred * inverse, inverse


def standardize_back(grad, scaled, inverse, gain):
    grad = grad * gain
    mean_grad = jnp.mean(grad, axis=-1, keepdims=True)
    mean_cross = jnp.mean(grad * scaled, axis=-1, keepdims=True)
    return inverse * (grad - mean_grad - scaled * mean_cross)


def collect(index, pieces, scratch):
    count = pieces[0].shape[0]
    for bits, piece in enumerate(pieces):
        at = pl.multiple_of((index ^ bits) * count, 32) if len(pieces) > 1 else 0
        scratch[pl.ds(at, count), :] = piece[...]


def pack_kernel(query_ref, key_ref, value_ref, outs_ref, gain_ref, shift_ref, out_ref):
    width = query_ref.shape[1]
    out_ref[:, :width] = query_ref[...]
    out_ref[:, width : 2 * width] = key_ref[...]
    out_ref[:, 2 * width : 3 * width] = value_ref[...]
    out_ref[:, 3 * width : 4 * width] = jnp.transpose(outs_ref[...].astype(WIDE)).astype(LOW)
    rows = [gain_ref[...].astype(WIDE), shift_ref[...].astype(WIDE)]
    rows.append(jnp.zeros((LANES - 4, gain_ref.shape[1]), WIDE))
    out_ref[:, 4 * width :] = jnp.transpose(jnp.concatenate(rows, axis=0)).astype(LOW)


def pack(*shards):
    rows, width = shards[0].shape
    return pl.pallas_call(
        pack_kernel,
        grid=(1,),
        in_specs=[pl.BlockSpec(shard.shape, lambda i: (0, 0)) for shard in shards],
        out_specs=whole(),
        out_shape=struct((rows, 4 * width + LANES), LOW),
        compiler_params=params(4),
        cost_estimate=cost(1),
        name="pack",
    )(*(far(shard) for shard in shards))


def project_kernel(scalar_ref, *refs, parts, width, block):
    pieces, refs = refs[:parts], refs[parts:]
    tokens_ref, normed_ref, projected_ref, rows_ref, weights_ref, outs_ref = refs

    @pl.when(pl.program_id(0) == 0)
    def _():
        collect(scalar_ref[3], pieces, weights_ref)
        rows_ref[...] = jnp.transpose(weights_ref[:, 4 * width : 4 * width + LANES].astype(WIDE))[:8, :]
        outs_ref[...] = jnp.transpose(weights_ref[:, 3 * width : 4 * width])

    for k in range(tokens_ref.shape[0] // block):
        part = slice(k * block, (k + 1) * block)
        scaled, _ = standardize(tokens_ref[part, :].astype(WIDE))
        normed = (scaled * rows_ref[0:1, :] + rows_ref[2:3, :]).astype(LOW)
        normed_ref[part, :] = normed
        projected_ref[part, :] = multiply(normed, weights_ref[:, : 3 * width]).astype(LOW)


def project(scalar, tokens, pieces, width):
    count, depth = tokens.shape
    total = pieces[0].shape[1]
    step = 768
    return pl.pallas_call(
        functools.partial(project_kernel, parts=len(pieces), width=width, block=256),
        grid=(count // step,),
        in_specs=[scalars()]
        + [whole()] * len(pieces)
        + [pl.BlockSpec((step, depth), lambda i: (i, 0))],
        out_specs=(
            pl.BlockSpec((step, depth), lambda i: (i, 0)),
            pl.BlockSpec((step, 3 * width), lambda i: (i, 0)),
            pl.BlockSpec((8, depth), lambda i: (0, 0)),
            pl.BlockSpec((depth, total), lambda i: (0, 0)),
            pl.BlockSpec((width, depth), lambda i: (0, 0)),
        ),
        out_shape=(
            stored_far((count, depth), LOW),
            struct((count, 3 * width), LOW),
            struct((8, depth), WIDE),
            struct((depth, total), LOW),
            struct((width, depth), LOW),
        ),
        compiler_params=params(20),
        cost_estimate=cost(4),
        name="project",
    )(scalar, *pieces, pltpu.with_memory_space_constraint(tokens, pltpu.HBM))


def assemble_kernel(scalar_ref, *refs, parts, units):
    pieces, (up_ref, down_ref) = refs[:parts], refs[parts:]
    count = pieces[0].shape[0]
    for bits, piece in enumerate(pieces):
        at = pl.multiple_of((scalar_ref[3] ^ bits) * count, 32) if parts > 1 else 0
        up_ref[pl.ds(at, count), :] = piece[:, :units]
        down_ref[pl.ds(at, count), :] = piece[:, units:]


def assemble(scalar, pieces, units):
    depth = sum(piece.shape[0] for piece in pieces)
    return pl.pallas_call(
        functools.partial(assemble_kernel, parts=len(pieces), units=units),
        in_specs=[scalars()] + [whole()] * len(pieces),
        out_specs=(whole(),) * 2,
        out_shape=(struct((depth, units), LOW), struct((depth, units), LOW)),
        compiler_params=params(10),
        cost_estimate=cost(1),
        name="assemble",
    )(scalar, *pieces)


def sign_of(scores):
    scores = scores.astype(LOW) * LOW(HUGE)
    return jnp.minimum(jnp.maximum(scores, LOW(-1)), LOW(1))


def attend_kernel(scalar_ref, projected_ref, mixed_ref, sums_ref, *, places, heads, sure):
    length = scalar_ref[1]
    factor = LOG2E * HD**-0.5
    width = heads * HD
    for i, place in enumerate(places):
        row0 = place * BLOCK
        here = slice(row0, row0 + BLOCK)
        row = lax.broadcasted_iota(jnp.int32, (BLOCK, 1), 0) + row0
        key = lax.broadcasted_iota(jnp.int32, (BLOCK, BLOCK), 1) + row0
        allowed = key <= jnp.minimum(row, length - 1)
        def each(function):
            return jnp.concatenate([function(h) for h in range(heads)], axis=0)

        def column(kind, h):
            return slice(kind * width + h * HD, kind * width + (h + 1) * HD)

        def split(value, h):
            return value[h * BLOCK : (h + 1) * BLOCK]

        near = each(lambda h: outer_cols(projected_ref[here, column(0, h)], projected_ref[here, column(1, h)]))
        near_size = jnp.where(jnp.concatenate([allowed] * heads, axis=0), jnp.abs(near) * factor, FAR)
        top = jnp.max(near_size, axis=1, keepdims=True)
        if row0 > 0:
            past = each(lambda h: outer_cols(projected_ref[here, column(0, h)], projected_ref[:row0, column(1, h)]))
            past_size = jnp.abs(past) * factor
            if row0 > sure:
                past_key = lax.broadcasted_iota(jnp.int32, (1, row0), 1)
                past_size = jnp.where(past_key < length, past_size, FAR)
            top = jnp.maximum(top, jnp.max(past_size, axis=1, keepdims=True))
            past_prob = jnp.exp2(past_size - top)
            past_signed = past_prob.astype(LOW) * sign_of(past)
        near_prob = jnp.exp2(near_size - top)
        near_signed = near_prob.astype(LOW) * sign_of(near)
        total = jnp.sum(near_prob, axis=1, keepdims=True)
        mixed = each(lambda h: multiply(split(near_signed, h), projected_ref[here, column(2, h)]))
        if row0 > 0:
            total = total + jnp.sum(past_prob, axis=1, keepdims=True)
            mixed = mixed + each(lambda h: multiply(split(past_signed, h), projected_ref[:row0, column(2, h)]))
        mixed = (mixed / total).astype(LOW)
        logs = top + jnp.log2(total)
        outs = [split(mixed, h) for h in range(heads)]
        sums = [split(logs, h) for h in range(heads)]
        part = slice(i * BLOCK, (i + 1) * BLOCK)
        mixed_ref[:, part] = jnp.transpose(jnp.concatenate(outs, axis=1))
        blank = jnp.zeros((BLOCK, LANES - heads), WIDE)
        sums_ref[i] = jnp.transpose(jnp.concatenate(sums + [blank], axis=1))[:8, :]


def attend(scalar, projected, places, sure):
    width = projected.shape[1] // 3
    heads = width // HD
    return pl.pallas_call(
        functools.partial(attend_kernel, places=places, heads=heads, sure=sure),
        in_specs=[scalars(), whole()],
        out_specs=(whole(), whole()),
        out_shape=(struct((width, len(places) * BLOCK), LOW), struct((len(places), 8, BLOCK), WIDE)),
        compiler_params=params(16),
        cost_estimate=cost(1),
        name="attend_forward",
    )(scalar, projected)


def attend_back_kernel(scalar_ref, *refs, chunks, rows, heads, sure):
    length = scalar_ref[1]
    core = scalar_ref[0]
    projected_ref, outs_ref, refs = refs[0], refs[1], refs[2:]
    mixed_refs, refs = refs[: len(chunks)], refs[len(chunks) :]
    sums_refs, refs = refs[: len(chunks)], refs[len(chunks) :]
    grad_refs, refs = refs[: 2 * len(chunks)], refs[2 * len(chunks) :]
    grads_ref, outs_grad_ref, whole_ref, grad_mixed, delta, logs, dq_turned = refs
    scaling = HD**-0.5
    factor = LOG2E * scaling
    width = heads * HD
    blocks = rows // BLOCK
    outs_grad = jnp.zeros(outs_ref.shape, WIDE)
    half = blocks // 2
    for number, (begin, size) in enumerate(chunks):
        for side in range(2):
            for k in range(size // BLOCK):
                local = side * size + k * BLOCK
                inside = slice(local, local + BLOCK)
                i = side * half + begin // BLOCK + k
                rows_i = slice(i * BLOCK, (i + 1) * BLOCK)
                mine = grad_refs[2 * number][k * BLOCK : (k + 1) * BLOCK, :]
                other = grad_refs[2 * number + 1][k * BLOCK : (k + 1) * BLOCK, :]

                @pl.when(core == side)
                def _():
                    whole_ref[rows_i, :] = mine

                @pl.when(core != side)
                def _():
                    whole_ref[rows_i, :] = other

                grad = whole_ref[rows_i, :]
                mixed = mixed_refs[number][:, inside]
                outs_grad = outs_grad + multiply(mixed, grad)
                turned = outer_cols(outs_ref[...], grad)
                grad_mixed[rows_i, :] = jnp.transpose(turned).astype(LOW)
                logs[:, rows_i] = sums_refs[number][local // BLOCK]
                both = turned.astype(LOW).astype(WIDE) * mixed.astype(WIDE)
                for h in range(heads):
                    delta[h : h + 1, rows_i] = jnp.sum(both[h * HD : (h + 1) * HD, :], axis=0, keepdims=True)
    outs_grad_ref[...] = jnp.transpose(outs_grad).astype(LOW)
    for j in range(blocks):
        here = slice(j * BLOCK, (j + 1) * BLOCK)
        later = slice((j + 1) * BLOCK, rows)
        dks, dvs = [], []
        for h in range(heads):
            cols = slice(h * HD, (h + 1) * HD)
            k = projected_ref[here, width + h * HD : width + (h + 1) * HD]
            v = projected_ref[here, 2 * width + h * HD : 2 * width + (h + 1) * HD]
            dk = jnp.zeros((BLOCK, HD), WIDE)
            dv = jnp.zeros((BLOCK, HD), WIDE)
            for part in (here, later):
                span = part.stop - part.start
                if span == 0:
                    continue
                q = projected_ref[part, cols]
                g = grad_mixed[part, cols]
                scores = outer_cols(k, q)
                grad_weights = outer_cols(v, g)
                reach = jnp.abs(scores) * factor - logs[h : h + 1, part]
                if part is here:
                    key = lax.broadcasted_iota(jnp.int32, (BLOCK, span), 0) + j * BLOCK
                    row = lax.broadcasted_iota(jnp.int32, (1, span), 1) + j * BLOCK
                    reach = jnp.where(key <= jnp.minimum(row, length - 1), reach, FAR)
                elif (j + 1) * BLOCK > sure:
                    key = lax.broadcasted_iota(jnp.int32, (BLOCK, 1), 0) + j * BLOCK
                    reach = jnp.where(key < length, reach, FAR)
                sign = sign_of(scores)
                weights = jnp.exp2(reach)
                signed = sign.astype(WIDE)
                raw = (weights * (grad_weights - signed * delta[h : h + 1, part])).astype(LOW) * (sign * sign)
                dv = dv + multiply(weights.astype(LOW) * sign, g)
                dk = dk + multiply(raw, q)
                more = inner_rows(k, raw)
                if j == 0:
                    dq_turned[cols, part] = more
                else:
                    dq_turned[cols, part] += more
            dks.append(dk * scaling)
            dvs.append(dv)
        grads_ref[:width, here] = (dq_turned[:, here] * scaling).astype(LOW)
        grads_ref[width : 2 * width, here] = jnp.transpose(jnp.concatenate(dks, axis=1)).astype(LOW)
        grads_ref[2 * width :, here] = jnp.transpose(jnp.concatenate(dvs, axis=1)).astype(LOW)


def attend_back(scalar, projected, outs, mixed, sums, grads, chunks, sure):
    rows = projected.shape[0]
    width = projected.shape[1] // 3
    depth = outs.shape[1]
    heads = width // HD
    return pl.pallas_call(
        functools.partial(attend_back_kernel, chunks=chunks, rows=rows, heads=heads, sure=sure),
        in_specs=[scalars()] + [whole()] * (2 + 4 * len(chunks)),
        out_specs=(whole(),) * 3,
        out_shape=(struct((3 * width, rows), LOW), struct((depth, width), LOW), struct((rows, depth), LOW)),
        scratch_shapes=[
            pltpu.VMEM((rows, width), LOW),
            pltpu.VMEM((8, rows), WIDE),
            pltpu.VMEM((8, rows), WIDE),
            pltpu.VMEM((width, rows), WIDE),
        ],
        compiler_params=params(24),
        cost_estimate=cost(8),
        name="attend_backward",
    )(scalar, projected, outs, *mixed, *sums, *grads)


def gelu_pair(up):
    root = 0.7978845608028654
    square = up * up
    bent = jnp.tanh(up * (root + (root * 0.044715) * square))
    half = 0.5 * bent + 0.5
    slope = half + (0.5 * up) * (1.0 - bent * bent) * (root + (3 * root * 0.044715) * square)
    return up * half, slope


def add_sums(sums_ref, ahead_ref, back, scaled, at):
    sums_ref[...] = ahead_ref[...]
    sums_ref[at : at + 1, :] += jnp.sum(back * scaled, axis=0, keepdims=True)
    sums_ref[at + 1 : at + 2, :] += jnp.sum(back, axis=0, keepdims=True)


def feed_kernel(scalar_ref, *refs, begin, size, half, keep, given):
    tokens_ref, grad_ref, m0, m1, m2, m3, o0, o1, o2, o3, up_ref, down_ref, rows_ref, ahead_ref = refs[:14]
    results = refs[14 + given : -1]
    back_ref, sums_ref, normed_ref, active_ref, upper_ref = results[:5]
    mixed_ref = refs[-1]
    place = scalar_ref[0] if keep else 1 - scalar_ref[0]
    row0 = pl.multiple_of(begin + place * half, BLOCK)
    here = pl.ds(row0, size)
    row = lax.broadcasted_iota(jnp.int32, (size, 1), 0) + row0

    @pl.when(scalar_ref[2] == 0)
    def _():
        across = inner_rows(m0[...], o0[...]) + inner_rows(m1[...], o1[...])
        mixed_ref[...] = across + inner_rows(m2[...], o2[...]) + inner_rows(m3[...], o3[...])

    @pl.when(scalar_ref[2] != 0)
    def _():
        across = inner_rows(m1[...], o1[...]) + inner_rows(m0[...], o0[...])
        mixed_ref[...] = across + inner_rows(m3[...], o3[...]) + inner_rows(m2[...], o2[...])

    hidden = tokens_ref[...].astype(WIDE) + mixed_ref[...]
    if keep:
        results[5][...] = hidden
    scaled, _ = standardize(hidden)
    normed = (scaled * rows_ref[1:2, :] + rows_ref[3:4, :]).astype(LOW)
    normed_ref[here, :] = normed
    grad = jnp.where(row < scalar_ref[1], grad_ref[...].astype(WIDE), 0.0).astype(LOW)
    back = jnp.zeros(hidden.shape, WIDE)
    units = up_ref.shape[1]
    for first in range(0, units, BLOCK):
        part = slice(first, first + BLOCK)
        active, slope = gelu_pair(multiply(normed, up_ref[:, part]))
        active_ref[here, part] = active.astype(LOW)
        upper = (multiply(grad, down_ref[:, part]) * slope).astype(LOW)
        upper_ref[here, part] = upper
        back = back + outer_cols(upper, up_ref[:, part])
    back_ref[...] = back.astype(LOW)
    add_sums(sums_ref, ahead_ref, back, scaled, 2)


def feed(scalar, tokens, out_grad, mixed, outs, up, down, rows, ahead, stored, begin, size, keep):
    count, depth = tokens.shape
    units = up.shape[1]
    width = outs[0].shape[0]
    half = count // 2

    def side(scalar_ref):
        return scalar_ref[0] if keep else 1 - scalar_ref[0]

    def placed(i, scalar_ref):
        return ((begin + side(scalar_ref) * half) // BLOCK * BLOCK, 0)

    def inside(i, scalar_ref):
        return (0, side(scalar_ref))

    rows_spec = pl.BlockSpec((pl.Element(size), pl.Element(depth)), placed)
    out_shape = (
        struct((size, depth), LOW),
        struct((8, depth), WIDE),
        struct((count, depth), LOW),
        struct((count, units), LOW),
        struct((count, units), LOW),
        stored_far((size, depth), WIDE),
    )[: 6 if keep else 5]
    return pl.pallas_call(
        functools.partial(feed_kernel, begin=begin, size=size, half=half, keep=keep, given=len(stored)),
        grid_spec=pltpu.PrefetchScalarGridSpec(
            num_scalar_prefetch=1,
            grid=(1,),
            in_specs=[rows_spec] * 2
            + [pl.BlockSpec((width, size), inside)] * 4
            + [whole()] * 8
            + [pl.BlockSpec(memory_space=pl.ANY)] * len(stored),
            out_specs=(whole(),) * len(out_shape),
            scratch_shapes=[pltpu.VMEM((size, depth), WIDE)],
        ),
        out_shape=out_shape,
        input_output_aliases={15 + k: 2 + k for k in range(len(stored))},
        compiler_params=params(20),
        cost_estimate=cost(size / 1000),
        name="feed_forward",
    )(scalar, tokens, out_grad, *mixed, *outs, up, down, rows, ahead, *stored)


def put_shards(index, outs, value, cols):
    if len(outs) == 1:
        outs[0][:, cols] = value
        return
    mine, other = outs
    rows = value.shape[0] // 8
    for place in range(8):
        piece = value[place * rows : (place + 1) * rows, :]

        @pl.when((index & 1) == place % 2)
        def _():
            mine[place // 2, :, cols] = piece

        @pl.when((index & 1) != place % 2)
        def _():
            other[place // 2, :, cols] = piece


def shard_shapes(batch, depth, cols):
    if batch != 8:
        return (stored_far((depth, cols), LOW),)
    return (struct((4, depth // 8, cols), LOW),) * 2


def weigh_kernel(scalar_ref, normed_ref, upper_ref, active_ref, grad_ref, down_ref, keep_ref, send_ref, *refs):
    outs, (up_sum, down_sum) = refs[:-2], refs[-2:]
    i = pl.program_id(0)
    units = down_ref.shape[1]
    half = grad_ref.shape[0]
    row0 = pl.multiple_of((scalar_ref[0] ^ 1 ^ i) * half, BLOCK)
    here = pl.ds(row0, half)
    row = lax.broadcasted_iota(jnp.int32, (half, 1), 0) + row0
    active = active_ref[here, :]
    branch = outer_cols(active, down_ref[...]).astype(LOW)
    grad = jnp.where(row < scalar_ref[1], grad_ref[...].astype(WIDE), 0.0).astype(LOW)
    up = inner_rows(normed_ref[here, :], upper_ref[here, :])
    down = inner_rows(grad, active)

    @pl.when(i == 0)
    def _():
        send_ref[...] = branch
        up_sum[...] = up
        down_sum[...] = down

    @pl.when(i == 1)
    def _():
        keep_ref[...] = branch
        put_shards(scalar_ref[3], outs, (up_sum[...] + up).astype(LOW), slice(0, units))
        put_shards(scalar_ref[3], outs, (down_sum[...] + down).astype(LOW), slice(units, 2 * units))


def weigh(scalar, normed, upper, active, out_grad, down, batch):
    count, depth = normed.shape
    units = down.shape[1]
    half = count // 2
    return pl.pallas_call(
        weigh_kernel,
        grid_spec=pltpu.PrefetchScalarGridSpec(
            num_scalar_prefetch=1,
            grid=(2,),
            in_specs=[whole()] * 3
            + [pl.BlockSpec((half, depth), lambda i, scalar_ref: (scalar_ref[0] ^ 1 ^ i, 0)), whole()],
            out_specs=(whole(),) * (2 + len(shard_shapes(batch, depth, 2 * units))),
            scratch_shapes=[pltpu.VMEM((depth, units), WIDE)] * 2,
        ),
        out_shape=(
            stored_far((half, depth), LOW),
            stored_far((half, depth), LOW),
            *shard_shapes(batch, depth, 2 * units),
        ),
        compiler_params=params(24),
        cost_estimate=cost(1),
        name="feed_forward_weights",
    )(scalar, normed, upper, active, out_grad, down)


def fold_kernel(scalar_ref, mine_ref, other_ref, *refs, given):
    place = scalar_ref[3] >> 1
    outs = refs[given:-1] if given else refs
    rows, cols = mine_ref.shape[1:]
    if given:
        refs[-1][...] = turned_sums(refs[0][...] + refs[1][...])
    for k, out in enumerate(outs):
        shard = place ^ k
        out[:, :cols] = (mine_ref[shard].astype(WIDE) + other_ref[shard].astype(WIDE)).astype(LOW)
        if given:
            at = pl.multiple_of((shard * 2 + (scalar_ref[3] & 1)) * rows, 32)
            out[:, cols:] = refs[-1][pl.ds(at, rows), :].astype(LOW)


def fold(scalar, mine, other, sums):
    count, rows, cols = mine.shape
    given = len(sums)
    cols += LANES if given else 0
    return pl.pallas_call(
        functools.partial(fold_kernel, given=given),
        in_specs=[scalars()] + [whole()] * (2 + given),
        out_specs=(whole(),) * count,
        out_shape=(struct((rows, cols), LOW),) * count,
        scratch_shapes=[pltpu.VMEM((sums[0].shape[1], LANES), WIDE)] if given else [],
        compiler_params=params(10),
        cost_estimate=cost(1),
        name="fold",
    )(scalar, mine, other, *sums)


def second_back_kernel(scalar_ref, mine_ref, other_ref, hidden_ref, grad_ref, rows_ref, low_ref, *, begin, half):
    size = low_ref.shape[0]
    row = lax.broadcasted_iota(jnp.int32, (size, 1), 0) + (begin + scalar_ref[0] * half)
    grad_normed = mine_ref[...].astype(WIDE) + other_ref[...].astype(WIDE)
    scaled, inverse = standardize(hidden_ref[...])
    grad = jnp.where(row < scalar_ref[1], grad_ref[...].astype(WIDE), 0.0)
    grad = grad + standardize_back(grad_normed, scaled, inverse, rows_ref[1:2, :])
    low_ref[...] = grad.astype(LOW)


def second_back(scalar, mine, other, hidden, out_grad, rows, begin, guess):
    size, depth = hidden.shape
    half = out_grad.shape[0] // 2
    placed = pl.BlockSpec(
        (pl.Element(size), pl.Element(depth)), lambda i, scalar_ref: ((begin + scalar_ref[0] * half) // BLOCK * BLOCK, 0)
    )
    return pl.pallas_call(
        functools.partial(second_back_kernel, begin=begin, half=half),
        grid_spec=pltpu.PrefetchScalarGridSpec(
            num_scalar_prefetch=1,
            grid=(1,),
            in_specs=[whole()] * 2 + [pl.BlockSpec((size, depth), lambda i, scalar_ref: (0, 0)), placed, whole()],
            out_specs=whole(),
        ),
        out_shape=struct((size, depth), LOW),
        compiler_params=params(14),
        cost_estimate=cost(guess),
        name="second_norm_backward",
    )(scalar, mine, other, far(hidden), far(out_grad), rows)


def inward_kernel(scalar_ref, grads_ref, tokens_ref, weights_ref, ahead_ref, back_ref, sums_ref):
    width = grads_ref.shape[0]
    back = lax.dot_general(
        grads_ref[...], weights_ref[:, :width], (((0,), (1,)), ((), ())), preferred_element_type=WIDE
    )
    scaled, _ = standardize(tokens_ref[...].astype(WIDE))
    back_ref[...] = back.astype(LOW)
    add_sums(sums_ref, ahead_ref, back, scaled, 0)


def inward(scalar, grads, tokens, weights, ahead, keep):
    count, depth = tokens.shape
    width = grads.shape[0]
    half = count // 2

    def side(scalar_ref):
        return scalar_ref[0] if keep else 1 - scalar_ref[0]

    return pl.pallas_call(
        inward_kernel,
        grid_spec=pltpu.PrefetchScalarGridSpec(
            num_scalar_prefetch=1,
            grid=(1,),
            in_specs=[
                pl.BlockSpec((width, half), lambda i, scalar_ref: (0, side(scalar_ref))),
                pl.BlockSpec((half, depth), lambda i, scalar_ref: (side(scalar_ref), 0)),
                whole(),
                whole(),
            ],
            out_specs=(whole(), whole()),
        ),
        out_shape=(struct((half, depth), LOW), struct((8, depth), WIDE)),
        compiler_params=params(16),
        cost_estimate=cost(1),
        name="grad_normed",
    )(scalar, grads, tokens, weights, ahead)


def turned_sums(sums):
    blank = jnp.zeros((LANES - sums.shape[0], sums.shape[1]), WIDE)
    return jnp.transpose(jnp.concatenate([sums, blank], axis=0))


def project_back_kernel(scalar_ref, grads_ref, normed_ref, outs_ref, *refs, given):
    outs = refs[given:]
    grads = jnp.transpose(multiply(grads_ref[...], normed_ref[...])).astype(LOW)
    value = [grads, outs_ref[...]] + [turned_sums(ref[...]).astype(LOW) for ref in refs[:given]]
    value = jnp.concatenate(value, axis=1)
    put_shards(scalar_ref[3], outs, value, slice(0, value.shape[1]))


def project_back(scalar, grads, normed, outs_grad, sums, batch):
    width = grads.shape[0]
    depth = normed.shape[1]
    shapes = shard_shapes(batch, depth, width + outs_grad.shape[1] + LANES * len(sums))
    return pl.pallas_call(
        functools.partial(project_back_kernel, given=len(sums)),
        in_specs=[scalars()] + [whole()] * (3 + len(sums)),
        out_specs=(whole(),) * len(shapes),
        out_shape=shapes,
        compiler_params=params(16),
        cost_estimate=cost(1),
        name="projection_weights",
    )(scalar, grads, normed, outs_grad, *sums)


def finish_kernel(scalar_ref, mine_ref, other_ref, *refs, sizes, half):
    hidden_refs, owns, full_ref = refs[: len(sizes)], refs[len(sizes) : -1], refs[-1]
    hidden = jnp.concatenate([ref[...] for ref in hidden_refs], axis=0)
    row = lax.broadcasted_iota(jnp.int32, (half, 1), 0) + scalar_ref[0] * half
    branch = mine_ref[...].astype(WIDE) + other_ref[...].astype(WIDE)
    low = jnp.where(row < scalar_ref[1], hidden + branch, 0.0).astype(LOW)
    full_ref[...] = low
    for k, own_ref in enumerate(owns):
        own_ref[...] = low[k * STEP : (k + 1) * STEP, :]


def finish(scalar, mine, other, hiddens, count):
    half, depth = mine.shape
    sizes = tuple(hidden.shape[0] for hidden in hiddens)
    parts = half // STEP
    return pl.pallas_call(
        functools.partial(finish_kernel, sizes=sizes, half=half),
        grid_spec=pltpu.PrefetchScalarGridSpec(
            num_scalar_prefetch=1,
            grid=(1,),
            in_specs=[whole()] * (2 + len(sizes)),
            out_specs=(whole(),) * parts
            + (pl.BlockSpec((half, depth), lambda i, scalar_ref: (scalar_ref[0], 0)),),
        ),
        out_shape=(stored_far((STEP, depth), LOW),) * parts + (stored_far((count, depth), LOW),),
        compiler_params=params(16),
        cost_estimate=cost(1),
        name="layer_out",
    )(scalar, mine, other, *(far(hidden) for hidden in hiddens))


def first_back_kernel(scalar_ref, mine_ref, other_ref, tokens_ref, grad_ref, rows_ref, *refs):
    own_ref, full_ref = refs[-2:]
    grad_normed = mine_ref[...].astype(WIDE) + other_ref[...].astype(WIDE)
    scaled, inverse = standardize(tokens_ref[...].astype(WIDE))
    grad = grad_ref[...].astype(WIDE) + standardize_back(grad_normed, scaled, inverse, rows_ref[0:1, :])
    low = grad.astype(LOW)
    own_ref[...] = low
    full_ref[...] = low


def first_back(scalar, mine, other, tokens, grad, rows, number, stored):
    size, depth = mine.shape
    count = tokens.shape[0]
    blocks = count // 2 // size

    def placed(i, scalar_ref):
        return (number + scalar_ref[0] * blocks, 0)

    return pl.pallas_call(
        first_back_kernel,
        grid_spec=pltpu.PrefetchScalarGridSpec(
            num_scalar_prefetch=1,
            grid=(1,),
            in_specs=[whole(), whole()]
            + [pl.BlockSpec((size, depth), placed)] * 2
            + [whole()]
            + [pl.BlockSpec(memory_space=pl.ANY)] * len(stored),
            out_specs=(whole(), pl.BlockSpec((size, depth), placed)),
        ),
        out_shape=(stored_far((size, depth), LOW), stored_far((count, depth), LOW)),
        input_output_aliases={6: 1} if stored else {},
        compiler_params=params(12),
        cost_estimate=cost(1),
        name="first_norm_backward",
    )(scalar, mine, other, tokens, grad, rows, *stored)


def place_kernel(scalar_ref, *refs, parts):
    first_refs, second_refs = refs[:parts], refs[parts : 2 * parts]
    for k in range(parts):

        @pl.when(pl.program_id(0) == k)
        def _():
            refs[-2][...] = first_refs[k][...]
            refs[-1][...] = second_refs[k][...]


def place(scalar, first, second, targets):
    parts = len(first)
    rows, depth = first[0].shape
    placed = pl.BlockSpec((rows, depth), lambda i, scalar_ref: (i + (1 - scalar_ref[0]) * parts, 0))
    return pl.pallas_call(
        functools.partial(place_kernel, parts=parts),
        grid_spec=pltpu.PrefetchScalarGridSpec(
            num_scalar_prefetch=1,
            grid=(parts,),
            in_specs=[whole()] * (2 * parts) + [pl.BlockSpec(memory_space=pl.ANY)] * 2,
            out_specs=(placed, placed),
        ),
        out_shape=tuple(stored_far(value.shape, value.dtype) for value in targets),
        input_output_aliases={1 + 2 * parts: 0, 2 + 2 * parts: 1},
        compiler_params=params(12),
        cost_estimate=cost(1),
        name="place",
    )(scalar, *first, *second, *targets)


def total_kernel(*refs, parts, bounds, flips):
    parts_refs, outs = refs[:parts], refs[parts:]
    if parts == 1:
        pieces = [parts_refs[0][k] for k in range(parts_refs[0].shape[0])]
    else:
        pieces = [ref[...] for ref in parts_refs]
    total = pieces[0].astype(WIDE)
    for piece in pieces[1:]:
        total = total + piece.astype(WIDE)
    for out, (first, last), flip in zip(outs, bounds, flips):
        piece = total[:, first:last]
        out[...] = jnp.transpose(piece) if flip else piece


def total_parts(parts, bounds, flips, guess):
    rows = parts[0].shape[-2]
    shapes = []
    for (first, last), flip in zip(bounds, flips):
        shape = (last - first, rows) if flip else (rows, last - first)
        shapes.append(struct(shape, WIDE))
    return pl.pallas_call(
        functools.partial(total_kernel, parts=len(parts), bounds=bounds, flips=flips),
        in_specs=[whole()] * len(parts),
        out_specs=(whole(),) * len(shapes),
        out_shape=tuple(shapes),
        compiler_params=params(8),
        cost_estimate=cost(guess),
        name="total",
    )(*parts)


def exchange_far(scalar, shards, ahead=(), sums=()):
    if len(shards) == 1:
        size = lax.axis_size("batch")
        parts = shards[0].reshape(size, shards[0].shape[0] // size, shards[0].shape[1])
        return [lax.all_to_all(parts, "batch", 0, 0, tiled=True)]
    pieces = fold(scalar, after(shards[0], *ahead), shards[1], sums)
    return [pieces[0]] + [swap(piece, "batch", 2 * k) for k, piece in enumerate(pieces) if k > 0]


def exchange_near(shards):
    return shards if len(shards) == 1 else (shards[0], swap(shards[1], "batch", 1))


def per_device(tokens, lengths, w_query, w_key, w_value, w_out, w_up, w_down, norm_gain, norm_shift, out_grad):
    count, depth = tokens.shape
    batch = lax.axis_size("batch")
    if lengths.shape[0] != 1 or lax.axis_size("tensor") != 4:
        raise ValueError("unsupported mesh")
    width = w_query.shape[1]
    units = w_up.shape[1]
    tensor = lax.axis_index("tensor").astype(jnp.int32)
    core = tensor & 1
    scalar = jnp.stack([core, lengths[0], tensor >> 1, lax.axis_index("batch").astype(jnp.int32)])
    sure = 2 * count // 3
    half = count // 2
    first = half // 3 * 2
    chunks = ((0, first), (first, half - first))

    if batch == 8:
        early = pack(w_query, w_key, w_value, w_out, norm_gain, norm_shift)
    else:
        blank = jnp.zeros((w_query.shape[0], -(4 * width + 4) % LANES), LOW)
        early = jnp.concatenate([w_query, w_key, w_value, w_out.T, norm_gain.T, norm_shift.T, blank], axis=1)
    late = jnp.concatenate([w_up, w_down.T], axis=1)
    if batch == 8:
        others = gather_far(early)
        early = [early, swap(early, "batch", 1)]
        early += [others[0], swap(others[0], "batch", 1)]
        early += [others[1], swap(after(others[1], early[1], early[3]), "batch", 1)]
        early += [others[2], swap(others[2], "batch", 1)]
        late = after(late, *others, early[1], early[3], early[5])
        near = swap(late, "batch", 2)
        middle = swap(late, "batch", 4)
        beside = swap(late, "batch", 1)
    else:
        early = [lax.all_gather(early, "batch", axis=0, tiled=True)]
        late = [lax.all_gather(late, "batch", axis=0, tiled=True)]

    normed, projected, rows, weights, own_outs = project(scalar, tokens, early, width)
    across = swap(own_outs, "tensor", 2)
    outs = (own_outs, across, swap(own_outs, "tensor", 1), swap(across, "tensor", 1))
    mixed, sums, pieces = [], [], []
    if batch == 8:
        late = [late, beside, near, swap(after(near, own_outs), "batch", 1)]
    for number, (begin, size) in enumerate(chunks):
        local = tuple(range(begin // BLOCK, (begin + size) // BLOCK))
        if number == 1:
            projected = after(projected, *late[3:4])
        part, logs = attend(scalar, projected, local + tuple(k + half // BLOCK for k in local), sure)
        projected = after(projected, part)
        mixed.append(part)
        sums.append(logs)
        across = swap(part, "tensor", 2)
        pieces.append((part, across, swap(part, "tensor", 1), swap(across, "tensor", 1)))
        if number == 0 and batch == 8:
            middle = after(middle, part)
            late += [middle, swap(middle, "batch", 1)]
            last = swap(middle, "batch", 2)
    if batch == 8:
        last = after(last, part)
        late += [last, swap(last, "batch", 1)]
    late = lax.optimization_barrier((*late, *mixed))[: len(late)]
    full_up, full_down = assemble(scalar, late, units)
    rows = after(rows, *pieces[-1][1:])

    stored, sends = [], []
    twos, halves, hiddens = jnp.zeros((8, depth), WIDE), [], []
    for (begin, size), piece in zip(chunks, pieces):
        back, twos, *stored = feed(
            scalar, tokens, out_grad, piece, outs, full_up, full_down, rows, twos, stored, begin, size, False
        )
        sends.append(back)
    for (begin, size), piece, send in zip(chunks, pieces, sends):
        rows = after(rows, *(mine for mine, _ in halves))
        back, twos, *stored = feed(
            scalar, tokens, out_grad, piece, outs, full_up, full_down, rows, twos, stored, begin, size, True
        )
        hiddens.append(stored.pop())
        mine = (back.astype(WIDE) + swap(send, "tensor", 1).astype(WIDE)).astype(LOW)
        halves.append((mine, swap(mine, "tensor", 2)))
    normed_two, active, upper = stored
    normed_two = after(normed_two, *(mine for mine, _ in halves))
    branch_keep, branch_send, *feed_grads = weigh(scalar, normed_two, upper, active, out_grad, full_down, 0)
    feed_parts = exchange_far(scalar, feed_grads)

    beside = swap(branch_send, "tensor", 1)
    grads = []
    for (begin, size), (mine, other), hidden in zip(chunks, halves, hiddens):
        mine = after(mine, *feed_grads)
        low = second_back(scalar, mine, other, hidden, out_grad, rows, begin, 40000 if grads else 1)
        grads += [low, swap(low, "tensor", 1)]
    branch_mine = (branch_keep.astype(WIDE) + beside.astype(WIDE)).astype(LOW)
    branch_mine = after(branch_mine, halves[0][1])
    branch_other = swap(branch_mine, "tensor", 2)
    projected = after(projected, branch_mine)
    attend_grads, outs_grad, grad_attn = attend_back(
        scalar, projected, own_outs, mixed, sums, grads, chunks, sure
    )

    there = (1 - core) * half
    ends = []
    if batch == 8:
        project_grads = exchange_near(project_back(scalar, attend_grads, normed, outs_grad, (), batch))
        attend_grads = after(attend_grads, project_grads[0])
    for keep in (False, True):
        back, twos = inward(scalar, attend_grads, tokens, weights, twos, keep)
        ends.append(back)
    if batch == 8:
        sums = (twos, swap(twos, "batch", 1))
    else:
        project_grads = project_back(scalar, attend_grads, normed, outs_grad, (twos,), batch)
        sums = ()
    keep = after(ends[1], branch_other)
    beside = swap(ends[0], "tensor", 1)
    tails = []
    for begin in range(0, half, STEP):
        part = slice(begin, begin + STEP)
        mine = (keep[part].astype(WIDE) + beside[part].astype(WIDE)).astype(LOW)
        tails.append((mine, swap(mine, "tensor", 2)))
    *own_out, layer_out = finish(scalar, branch_mine, after(branch_other, tails[-1][0]), hiddens, count)
    project_parts = exchange_far(scalar, project_grads, own_out, sums)
    other_out = [swap(own, "tensor", 1) for own in own_out]
    stored, other_grads = [], []
    for number, (mine, other) in enumerate(tails):
        mine = after(mine, *own_out)
        own_grad, *stored = first_back(scalar, mine, other, tokens, grad_attn, rows, number, stored)
        other_grads.append(swap(own_grad, "tensor", 1))
    feed_parts[0] = after(feed_parts[0], own_grad)
    shard_up, shard_down = total_parts(feed_parts, ((0, units), (units, 2 * units)), (False, False), 1)
    last = 4 * width
    project_parts[0] = after(project_parts[0], shard_up)
    (small,) = total_parts(project_parts, ((last, last + LANES),), (True,), 40000)
    small = small[:8]
    across = swap(small, "tensor", 2)
    project_parts[0] = after(project_parts[0], small)
    shard_query, shard_key, shard_value, shard_out = total_parts(
        project_parts,
        ((0, width), (width, 2 * width), (2 * width, 3 * width), (3 * width, last)),
        (False, False, False, True),
        1,
    )
    small = small + after(across, shard_query)
    across = swap(small, "tensor", 1)
    other_grads[0] = after(other_grads[0], small)
    layer_out, grad_input = place(scalar, other_out, other_grads, (layer_out, stored[0]))
    small = small + after(across, grad_input)
    shard_gain = jnp.stack([small[0], small[2]])
    shard_shift = jnp.stack([small[1], small[3]])
    return (
        layer_out,
        grad_input,
        shard_query,
        shard_key,
        shard_value,
        shard_out,
        shard_up,
        shard_down.T,
        shard_gain,
        shard_shift,
    )


def solution(mesh):
    tall = P("batch", "tensor")
    wide = P("tensor", "batch")
    rows = P("batch", None)
    pair = P(None, "batch")
    return jax.shard_map(
        per_device,
        mesh=mesh,
        in_specs=(rows, P("batch"), tall, tall, tall, wide, tall, wide, pair, pair, rows),
        out_specs=(rows, rows, tall, tall, tall, wide, tall, wide, pair, pair),
        check_vma=False,
    )
```

```python
import functools

import jax
import jax.numpy as jnp
from jax import lax
from jax.experimental import pallas as pl
from jax.experimental.pallas import tpu as pltpu
from jax.sharding import PartitionSpec as P

HD = 64
EPSILON = 1e-05
LOG2E = 1.4426950408889634
HUGE = 3e38
FAR = -1e30
LOW = jnp.bfloat16
WIDE = jnp.float32
LANES = 128
BLOCK = 256
STEP = 384


def multiply(left, right):
    return lax.dot_general(left, right, (((1,), (0,)), ((), ())), preferred_element_type=WIDE)


def outer_cols(left, right):
    return lax.dot_general(left, right, (((1,), (1,)), ((), ())), preferred_element_type=WIDE)


def inner_rows(left, right):
    return lax.dot_general(left, right, (((0,), (0,)), ((), ())), preferred_element_type=WIDE)


def whole():
    return pl.BlockSpec(memory_space=pltpu.VMEM)


def scalars():
    return pl.BlockSpec(memory_space=pltpu.SMEM)


def struct(shape, dtype):
    return jax.ShapeDtypeStruct(shape, dtype)


def held(shape, dtype):
    return pltpu.VMEM(shape, dtype)


def stored_far(shape, dtype):
    return pltpu.HBM(shape, dtype)


def far(value):
    return pltpu.with_memory_space_constraint(value, pltpu.HBM)


def params(mebibytes):
    return pltpu.CompilerParams(vmem_limit_bytes=mebibytes << 20)


def cost(microseconds):
    return pl.CostEstimate(flops=int(microseconds * 1.1e6), bytes_accessed=0, transcendentals=0)


def after(value, *others):
    return lax.optimization_barrier((value, *others))[0]


def swap(value, axis, bits):
    size = lax.axis_size(axis)
    return lax.ppermute(value, axis, [(i, i ^ bits) for i in range(size)])


def gather_far(shard):
    return [swap(shard, "batch", bits) for bits in (2, 4, 6)]


def pair_sum(keep, send):
    mine = (keep.astype(WIDE) + swap(send, "tensor", 1).astype(WIDE)).astype(LOW)
    return mine, swap(mine, "tensor", 2)


def standardize(values):
    middle = jnp.mean(values, axis=-1, keepdims=True)
    centred = values - middle
    spread = jnp.mean(centred * centred, axis=-1, keepdims=True)
    inverse = lax.rsqrt(spread + EPSILON)
    return centred * inverse, inverse


def standardize_back(grad, scaled, inverse, gain):
    grad = grad * gain
    mean_grad = jnp.mean(grad, axis=-1, keepdims=True)
    mean_cross = jnp.mean(grad * scaled, axis=-1, keepdims=True)
    return inverse * (grad - mean_grad - scaled * mean_cross)


def collect(index, pieces, scratch):
    count = pieces[0].shape[0]
    for bits, piece in enumerate(pieces):
        at = pl.multiple_of((index ^ bits) * count, 32) if len(pieces) > 1 else 0
        scratch[pl.ds(at, count), :] = piece[...]


def pack_kernel(query_ref, key_ref, value_ref, outs_ref, gain_ref, shift_ref, out_ref):
    width = query_ref.shape[1]
    out_ref[:, :width] = query_ref[...]
    out_ref[:, width : 2 * width] = key_ref[...]
    out_ref[:, 2 * width : 3 * width] = value_ref[...]
    out_ref[:, 3 * width : 4 * width] = jnp.transpose(outs_ref[...].astype(WIDE)).astype(LOW)
    rows = [gain_ref[...].astype(WIDE), shift_ref[...].astype(WIDE)]
    rows.append(jnp.zeros((LANES - 4, gain_ref.shape[1]), WIDE))
    out_ref[:, 4 * width :] = jnp.transpose(jnp.concatenate(rows, axis=0)).astype(LOW)


def pack(*shards):
    rows, width = shards[0].shape
    return pl.pallas_call(
        pack_kernel,
        grid=(1,),
        in_specs=[pl.BlockSpec(shard.shape, lambda i: (0, 0)) for shard in shards],
        out_specs=whole(),
        out_shape=struct((rows, 4 * width + LANES), LOW),
        compiler_params=params(4),
        cost_estimate=cost(1),
        name="pack",
    )(*(far(shard) for shard in shards))


def project_kernel(scalar_ref, *refs, parts, width, block):
    pieces, refs = refs[:parts], refs[parts:]
    tokens_ref, normed_ref, projected_ref, rows_ref, weights_ref, outs_ref = refs

    @pl.when(pl.program_id(0) == 0)
    def _():
        collect(scalar_ref[3], pieces, weights_ref)
        rows_ref[...] = jnp.transpose(weights_ref[:, 4 * width : 4 * width + LANES].astype(WIDE))[:8, :]
        outs_ref[...] = jnp.transpose(weights_ref[:, 3 * width : 4 * width])

    for k in range(tokens_ref.shape[0] // block):
        part = slice(k * block, (k + 1) * block)
        scaled, _ = standardize(tokens_ref[part, :].astype(WIDE))
        normed = (scaled * rows_ref[0:1, :] + rows_ref[2:3, :]).astype(LOW)
        normed_ref[part, :] = normed
        projected_ref[part, :] = multiply(normed, weights_ref[:, : 3 * width]).astype(LOW)


def project(scalar, tokens, pieces, width):
    count, depth = tokens.shape
    total = pieces[0].shape[1]
    step = 768
    return pl.pallas_call(
        functools.partial(project_kernel, parts=len(pieces), width=width, block=256),
        grid=(count // step,),
        in_specs=[scalars()]
        + [whole()] * len(pieces)
        + [pl.BlockSpec((step, depth), lambda i: (i, 0))],
        out_specs=(
            pl.BlockSpec((step, depth), lambda i: (i, 0)),
            pl.BlockSpec((step, 3 * width), lambda i: (i, 0)),
            pl.BlockSpec((8, depth), lambda i: (0, 0)),
            pl.BlockSpec((depth, total), lambda i: (0, 0)),
            pl.BlockSpec((width, depth), lambda i: (0, 0)),
        ),
        out_shape=(
            stored_far((count, depth), LOW),
            struct((count, 3 * width), LOW),
            struct((8, depth), WIDE),
            struct((depth, total), LOW),
            struct((width, depth), LOW),
        ),
        compiler_params=params(20),
        cost_estimate=cost(4),
        name="project",
    )(scalar, *pieces, pltpu.with_memory_space_constraint(tokens, pltpu.HBM))


def assemble_kernel(scalar_ref, *refs, parts, units):
    pieces, (up_ref, down_ref) = refs[:parts], refs[parts:]
    count = pieces[0].shape[0]
    for bits, piece in enumerate(pieces):
        at = pl.multiple_of((scalar_ref[3] ^ bits) * count, 32) if parts > 1 else 0
        up_ref[pl.ds(at, count), :] = piece[:, :units]
        down_ref[pl.ds(at, count), :] = piece[:, units:]


def assemble(scalar, pieces, units):
    depth = sum(piece.shape[0] for piece in pieces)
    return pl.pallas_call(
        functools.partial(assemble_kernel, parts=len(pieces), units=units),
        in_specs=[scalars()] + [whole()] * len(pieces),
        out_specs=(whole(),) * 2,
        out_shape=(struct((depth, units), LOW), struct((depth, units), LOW)),
        compiler_params=params(10),
        cost_estimate=cost(1),
        name="assemble",
    )(scalar, *pieces)


def sign_of(scores):
    scores = scores.astype(LOW) * LOW(HUGE)
    return jnp.minimum(jnp.maximum(scores, LOW(-1)), LOW(1))


def attend_kernel(scalar_ref, projected_ref, mixed_ref, sums_ref, *, places, heads, sure):
    length = scalar_ref[1]
    factor = LOG2E * HD**-0.5
    width = heads * HD
    for i, place in enumerate(places):
        row0 = place * BLOCK
        here = slice(row0, row0 + BLOCK)
        row = lax.broadcasted_iota(jnp.int32, (BLOCK, 1), 0) + row0
        key = lax.broadcasted_iota(jnp.int32, (BLOCK, BLOCK), 1) + row0
        allowed = key <= jnp.minimum(row, length - 1)
        def each(function):
            return jnp.concatenate([function(h) for h in range(heads)], axis=0)

        def column(kind, h):
            return slice(kind * width + h * HD, kind * width + (h + 1) * HD)

        def split(value, h):
            return value[h * BLOCK : (h + 1) * BLOCK]

        near = each(lambda h: outer_cols(projected_ref[here, column(0, h)], projected_ref[here, column(1, h)]))
        near_size = jnp.where(jnp.concatenate([allowed] * heads, axis=0), jnp.abs(near) * factor, FAR)
        top = jnp.max(near_size, axis=1, keepdims=True)
        if row0 > 0:
            past = each(lambda h: outer_cols(projected_ref[here, column(0, h)], projected_ref[:row0, column(1, h)]))
            past_size = jnp.abs(past) * factor
            if row0 > sure:
                past_key = lax.broadcasted_iota(jnp.int32, (1, row0), 1)
                past_size = jnp.where(past_key < length, past_size, FAR)
            top = jnp.maximum(top, jnp.max(past_size, axis=1, keepdims=True))
            past_prob = jnp.exp2(past_size - top)
            past_signed = past_prob.astype(LOW) * sign_of(past)
        near_prob = jnp.exp2(near_size - top)
        near_signed = near_prob.astype(LOW) * sign_of(near)
        total = jnp.sum(near_prob, axis=1, keepdims=True)
        mixed = each(lambda h: multiply(split(near_signed, h), projected_ref[here, column(2, h)]))
        if row0 > 0:
            total = total + jnp.sum(past_prob, axis=1, keepdims=True)
            mixed = mixed + each(lambda h: multiply(split(past_signed, h), projected_ref[:row0, column(2, h)]))
        mixed = (mixed / total).astype(LOW)
        logs = top + jnp.log2(total)
        outs = [split(mixed, h) for h in range(heads)]
        sums = [split(logs, h) for h in range(heads)]
        part = slice(i * BLOCK, (i + 1) * BLOCK)
        mixed_ref[:, part] = jnp.transpose(jnp.concatenate(outs, axis=1))
        blank = jnp.zeros((BLOCK, LANES - heads), WIDE)
        sums_ref[i] = jnp.transpose(jnp.concatenate(sums + [blank], axis=1))[:8, :]


def attend(scalar, projected, places, sure):
    width = projected.shape[1] // 3
    heads = width // HD
    return pl.pallas_call(
        functools.partial(attend_kernel, places=places, heads=heads, sure=sure),
        in_specs=[scalars(), whole()],
        out_specs=(whole(), whole()),
        out_shape=(struct((width, len(places) * BLOCK), LOW), struct((len(places), 8, BLOCK), WIDE)),
        compiler_params=params(16),
        cost_estimate=cost(1),
        name="attend_forward",
    )(scalar, projected)


def attend_back_kernel(scalar_ref, *refs, chunks, rows, heads, sure):
    length = scalar_ref[1]
    core = scalar_ref[0]
    projected_ref, outs_ref, refs = refs[0], refs[1], refs[2:]
    mixed_refs, refs = refs[: len(chunks)], refs[len(chunks) :]
    sums_refs, refs = refs[: len(chunks)], refs[len(chunks) :]
    grad_refs, refs = refs[: 2 * len(chunks)], refs[2 * len(chunks) :]
    grads_ref, outs_grad_ref, whole_ref, grad_mixed, delta, logs, dq_turned = refs
    scaling = HD**-0.5
    factor = LOG2E * scaling
    width = heads * HD
    blocks = rows // BLOCK
    outs_grad = jnp.zeros(outs_ref.shape, WIDE)
    half = blocks // 2
    for number, (begin, size) in enumerate(chunks):
        for side in range(2):
            for k in range(size // BLOCK):
                local = side * size + k * BLOCK
                inside = slice(local, local + BLOCK)
                i = side * half + begin // BLOCK + k
                rows_i = slice(i * BLOCK, (i + 1) * BLOCK)
                mine = grad_refs[2 * number][k * BLOCK : (k + 1) * BLOCK, :]
                other = grad_refs[2 * number + 1][k * BLOCK : (k + 1) * BLOCK, :]

                @pl.when(core == side)
                def _():
                    whole_ref[rows_i, :] = mine

                @pl.when(core != side)
                def _():
                    whole_ref[rows_i, :] = other

                grad = whole_ref[rows_i, :]
                mixed = mixed_refs[number][:, inside]
                outs_grad = outs_grad + multiply(mixed, grad)
                turned = outer_cols(outs_ref[...], grad)
                grad_mixed[rows_i, :] = jnp.transpose(turned).astype(LOW)
                logs[:, rows_i] = sums_refs[number][local // BLOCK]
                both = turned.astype(LOW).astype(WIDE) * mixed.astype(WIDE)
                for h in range(heads):
                    delta[h : h + 1, rows_i] = jnp.sum(both[h * HD : (h + 1) * HD, :], axis=0, keepdims=True)
    outs_grad_ref[...] = jnp.transpose(outs_grad).astype(LOW)
    for j in range(blocks):
        here = slice(j * BLOCK, (j + 1) * BLOCK)
        later = slice((j + 1) * BLOCK, rows)
        dks, dvs = [], []
        for h in range(heads):
            cols = slice(h * HD, (h + 1) * HD)
            k = projected_ref[here, width + h * HD : width + (h + 1) * HD]
            v = projected_ref[here, 2 * width + h * HD : 2 * width + (h + 1) * HD]
            part = slice(j * BLOCK, rows)
            q = projected_ref[part, cols]
            g = grad_mixed[part, cols]
            scores = outer_cols(k, q)
            grad_weights = outer_cols(v, g)
            reach = jnp.abs(scores) * factor - logs[h : h + 1, part]
            key = lax.broadcasted_iota(jnp.int32, (BLOCK, 1), 0) + j * BLOCK
            row = lax.broadcasted_iota(jnp.int32, (1, BLOCK), 1) + j * BLOCK
            near = jnp.where(key <= jnp.minimum(row, length - 1), reach[:, :BLOCK], FAR)
            if part.stop > (j + 1) * BLOCK:
                past = reach[:, BLOCK:]
                if (j + 1) * BLOCK > sure:
                    past = jnp.where(key < length, past, FAR)
                near = jnp.concatenate([near, past], axis=1)
            sign = sign_of(scores)
            weights = jnp.exp2(near)
            signed = sign.astype(WIDE)
            raw = (weights * (grad_weights - signed * delta[h : h + 1, part])).astype(LOW) * (sign * sign)
            dv = multiply(weights.astype(LOW) * sign, g)
            dk = multiply(raw, q)
            more = inner_rows(k, raw)
            if j == 0:
                dq_turned[cols, part] = more
            else:
                dq_turned[cols, part] += more
            dks.append(dk * scaling)
            dvs.append(dv)
        grads_ref[:width, here] = (dq_turned[:, here] * scaling).astype(LOW)
        grads_ref[width : 2 * width, here] = jnp.transpose(jnp.concatenate(dks, axis=1)).astype(LOW)
        grads_ref[2 * width :, here] = jnp.transpose(jnp.concatenate(dvs, axis=1)).astype(LOW)


def attend_back(scalar, projected, outs, mixed, sums, grads, chunks, sure):
    rows = projected.shape[0]
    width = projected.shape[1] // 3
    depth = outs.shape[1]
    heads = width // HD
    return pl.pallas_call(
        functools.partial(attend_back_kernel, chunks=chunks, rows=rows, heads=heads, sure=sure),
        in_specs=[scalars()] + [whole()] * (2 + 4 * len(chunks)),
        out_specs=(whole(),) * 3,
        out_shape=(struct((3 * width, rows), LOW), struct((depth, width), LOW), struct((rows, depth), LOW)),
        scratch_shapes=[
            pltpu.VMEM((rows, width), LOW),
            pltpu.VMEM((8, rows), WIDE),
            pltpu.VMEM((8, rows), WIDE),
            pltpu.VMEM((width, rows), WIDE),
        ],
        compiler_params=params(24),
        cost_estimate=cost(8),
        name="attend_backward",
    )(scalar, projected, outs, *mixed, *sums, *grads)


def gelu_pair(up):
    root = 0.7978845608028654
    square = up * up
    bent = jnp.tanh(up * (root + (root * 0.044715) * square))
    half = 0.5 * bent + 0.5
    slope = half + (0.5 * up) * (1.0 - bent * bent) * (root + (3 * root * 0.044715) * square)
    return up * half, slope


def add_sums(sums_ref, ahead_ref, back, scaled, at):
    sums_ref[...] = ahead_ref[...]
    sums_ref[at : at + 1, :] += jnp.sum(back * scaled, axis=0, keepdims=True)
    sums_ref[at + 1 : at + 2, :] += jnp.sum(back, axis=0, keepdims=True)


def feed_kernel(scalar_ref, *refs, begin, size, half, keep, given):
    tokens_ref, grad_ref, m0, m1, m2, m3, o0, o1, o2, o3, up_ref, down_ref, rows_ref, ahead_ref = refs[:14]
    results = refs[14 + given : -1]
    back_ref, sums_ref, normed_ref, active_ref, upper_ref = results[:5]
    mixed_ref = refs[-1]
    place = scalar_ref[0] if keep else 1 - scalar_ref[0]
    row0 = pl.multiple_of(begin + place * half, BLOCK)
    here = pl.ds(row0, size)
    row = lax.broadcasted_iota(jnp.int32, (size, 1), 0) + row0

    @pl.when(scalar_ref[2] == 0)
    def _():
        across = inner_rows(m0[...], o0[...]) + inner_rows(m1[...], o1[...])
        mixed_ref[...] = across + inner_rows(m2[...], o2[...]) + inner_rows(m3[...], o3[...])

    @pl.when(scalar_ref[2] != 0)
    def _():
        across = inner_rows(m1[...], o1[...]) + inner_rows(m0[...], o0[...])
        mixed_ref[...] = across + inner_rows(m3[...], o3[...]) + inner_rows(m2[...], o2[...])

    hidden = tokens_ref[...].astype(WIDE) + mixed_ref[...]
    if keep:
        results[5][...] = hidden
    scaled, _ = standardize(hidden)
    normed = (scaled * rows_ref[1:2, :] + rows_ref[3:4, :]).astype(LOW)
    normed_ref[here, :] = normed
    grad = jnp.where(row < scalar_ref[1], grad_ref[...].astype(WIDE), 0.0).astype(LOW)
    back = jnp.zeros(hidden.shape, WIDE)
    units = up_ref.shape[1]
    for first in range(0, units, BLOCK):
        part = slice(first, first + BLOCK)
        active, slope = gelu_pair(multiply(normed, up_ref[:, part]))
        active_ref[here, part] = active.astype(LOW)
        upper = (multiply(grad, down_ref[:, part]) * slope).astype(LOW)
        upper_ref[here, part] = upper
        back = back + outer_cols(upper, up_ref[:, part])
    back_ref[...] = back.astype(LOW)
    add_sums(sums_ref, ahead_ref, back, scaled, 2)


def feed(scalar, tokens, out_grad, mixed, outs, up, down, rows, ahead, stored, begin, size, keep):
    count, depth = tokens.shape
    units = up.shape[1]
    width = outs[0].shape[0]
    half = count // 2

    def side(scalar_ref):
        return scalar_ref[0] if keep else 1 - scalar_ref[0]

    def placed(i, scalar_ref):
        return ((begin + side(scalar_ref) * half) // BLOCK * BLOCK, 0)

    def inside(i, scalar_ref):
        return (0, side(scalar_ref))

    rows_spec = pl.BlockSpec((pl.Element(size), pl.Element(depth)), placed)
    out_shape = (
        struct((size, depth), LOW),
        struct((8, depth), WIDE),
        struct((count, depth), LOW),
        struct((count, units), LOW),
        struct((count, units), LOW),
        (struct if begin else stored_far)((size, depth), WIDE),
    )[: 6 if keep else 5]
    return pl.pallas_call(
        functools.partial(feed_kernel, begin=begin, size=size, half=half, keep=keep, given=len(stored)),
        grid_spec=pltpu.PrefetchScalarGridSpec(
            num_scalar_prefetch=1,
            grid=(1,),
            in_specs=[rows_spec] * 2
            + [pl.BlockSpec((width, size), inside)] * 4
            + [whole()] * 8
            + [pl.BlockSpec(memory_space=pl.ANY)] * len(stored),
            out_specs=(whole(),) * len(out_shape),
            scratch_shapes=[pltpu.VMEM((size, depth), WIDE)],
        ),
        out_shape=out_shape,
        input_output_aliases={15 + k: 2 + k for k in range(len(stored))},
        compiler_params=params(20),
        cost_estimate=cost(size / 1000),
        name="feed_forward",
    )(scalar, tokens, out_grad, *mixed, *outs, up, down, rows, ahead, *stored)


def put_shards(index, outs, value, cols):
    if len(outs) == 1:
        outs[0][:, cols] = value
        return
    mine, other = outs
    rows = value.shape[0] // 8
    for place in range(8):
        piece = value[place * rows : (place + 1) * rows, :]

        @pl.when((index & 1) == place % 2)
        def _():
            mine[place // 2, :, cols] = piece

        @pl.when((index & 1) != place % 2)
        def _():
            other[place // 2, :, cols] = piece


def shard_shapes(batch, depth, cols):
    if batch != 8:
        return (stored_far((depth, cols), LOW),)
    return (struct((4, depth // 8, cols), LOW),) * 2


def weigh_kernel(scalar_ref, normed_ref, upper_ref, active_ref, grad_ref, down_ref, keep_ref, send_ref, *refs):
    outs, (up_sum, down_sum) = refs[:-2], refs[-2:]
    i = pl.program_id(0)
    units = down_ref.shape[1]
    half = grad_ref.shape[0]
    row0 = pl.multiple_of((scalar_ref[0] ^ 1 ^ i) * half, BLOCK)
    here = pl.ds(row0, half)
    row = lax.broadcasted_iota(jnp.int32, (half, 1), 0) + row0
    active = active_ref[here, :]
    branch = outer_cols(active, down_ref[...]).astype(LOW)
    grad = jnp.where(row < scalar_ref[1], grad_ref[...].astype(WIDE), 0.0).astype(LOW)
    up = inner_rows(normed_ref[here, :], upper_ref[here, :])
    down = inner_rows(grad, active)

    @pl.when(i == 0)
    def _():
        send_ref[...] = branch
        up_sum[...] = up
        down_sum[...] = down

    @pl.when(i == 1)
    def _():
        keep_ref[...] = branch
        put_shards(scalar_ref[3], outs, (up_sum[...] + up).astype(LOW), slice(0, units))
        put_shards(scalar_ref[3], outs, (down_sum[...] + down).astype(LOW), slice(units, 2 * units))


def weigh(scalar, normed, upper, active, out_grad, down, batch):
    count, depth = normed.shape
    units = down.shape[1]
    half = count // 2
    return pl.pallas_call(
        weigh_kernel,
        grid_spec=pltpu.PrefetchScalarGridSpec(
            num_scalar_prefetch=1,
            grid=(2,),
            in_specs=[whole()] * 3
            + [pl.BlockSpec((half, depth), lambda i, scalar_ref: (scalar_ref[0] ^ 1 ^ i, 0)), whole()],
            out_specs=(whole(),) * (2 + len(shard_shapes(batch, depth, 2 * units))),
            scratch_shapes=[pltpu.VMEM((depth, units), WIDE)] * 2,
        ),
        out_shape=(
            stored_far((half, depth), LOW),
            stored_far((half, depth), LOW),
            *shard_shapes(batch, depth, 2 * units),
        ),
        compiler_params=params(24),
        cost_estimate=cost(1),
        name="feed_forward_weights",
    )(scalar, normed, upper, active, out_grad, down)


def fold_kernel(scalar_ref, mine_ref, other_ref, *refs, given):
    place = scalar_ref[3] >> 1
    outs = refs[given:-1] if given else refs
    rows, cols = mine_ref.shape[1:]
    if given:
        refs[-1][...] = turned_sums(refs[0][...] + refs[1][...])
    for k, out in enumerate(outs):
        shard = place ^ k
        out[:, :cols] = (mine_ref[shard].astype(WIDE) + other_ref[shard].astype(WIDE)).astype(LOW)
        if given:
            at = pl.multiple_of((shard * 2 + (scalar_ref[3] & 1)) * rows, 32)
            out[:, cols:] = refs[-1][pl.ds(at, rows), :].astype(LOW)


def fold(scalar, mine, other, sums):
    count, rows, cols = mine.shape
    given = len(sums)
    cols += LANES if given else 0
    return pl.pallas_call(
        functools.partial(fold_kernel, given=given),
        in_specs=[scalars()] + [whole()] * (2 + given),
        out_specs=(whole(),) * count,
        out_shape=(struct((rows, cols), LOW),) * count,
        scratch_shapes=[pltpu.VMEM((sums[0].shape[1], LANES), WIDE)] if given else [],
        compiler_params=params(10),
        cost_estimate=cost(1),
        name="fold",
    )(scalar, mine, other, *sums)


def second_back_kernel(scalar_ref, mine_ref, other_ref, hidden_ref, grad_ref, rows_ref, low_ref, *, begin, half):
    size = low_ref.shape[0]
    row = lax.broadcasted_iota(jnp.int32, (size, 1), 0) + (begin + scalar_ref[0] * half)
    grad_normed = mine_ref[...].astype(WIDE) + other_ref[...].astype(WIDE)
    scaled, inverse = standardize(hidden_ref[...])
    grad = jnp.where(row < scalar_ref[1], grad_ref[...].astype(WIDE), 0.0)
    grad = grad + standardize_back(grad_normed, scaled, inverse, rows_ref[1:2, :])
    low_ref[...] = grad.astype(LOW)


def second_back(scalar, mine, other, hidden, out_grad, rows, begin, guess):
    size, depth = hidden.shape
    half = out_grad.shape[0] // 2
    placed = pl.BlockSpec(
        (pl.Element(size), pl.Element(depth)), lambda i, scalar_ref: ((begin + scalar_ref[0] * half) // BLOCK * BLOCK, 0)
    )
    return pl.pallas_call(
        functools.partial(second_back_kernel, begin=begin, half=half),
        grid_spec=pltpu.PrefetchScalarGridSpec(
            num_scalar_prefetch=1,
            grid=(1,),
            in_specs=[whole()] * 3 + [placed, whole()],
            out_specs=whole(),
        ),
        out_shape=struct((size, depth), LOW),
        compiler_params=params(14),
        cost_estimate=cost(guess),
        name="second_norm_backward",
    )(scalar, mine, other, hidden if begin else far(hidden), far(out_grad), rows)


def inward_kernel(scalar_ref, grads_ref, tokens_ref, weights_ref, ahead_ref, back_ref, sums_ref):
    width = grads_ref.shape[0]
    back = lax.dot_general(
        grads_ref[...], weights_ref[:, :width], (((0,), (1,)), ((), ())), preferred_element_type=WIDE
    )
    scaled, _ = standardize(tokens_ref[...].astype(WIDE))
    back_ref[...] = back.astype(LOW)
    add_sums(sums_ref, ahead_ref, back, scaled, 0)


def inward(scalar, grads, tokens, weights, ahead, keep):
    count, depth = tokens.shape
    width = grads.shape[0]
    half = count // 2

    def side(scalar_ref):
        return scalar_ref[0] if keep else 1 - scalar_ref[0]

    return pl.pallas_call(
        inward_kernel,
        grid_spec=pltpu.PrefetchScalarGridSpec(
            num_scalar_prefetch=1,
            grid=(1,),
            in_specs=[
                pl.BlockSpec((width, half), lambda i, scalar_ref: (0, side(scalar_ref))),
                pl.BlockSpec((half, depth), lambda i, scalar_ref: (side(scalar_ref), 0)),
                whole(),
                whole(),
            ],
            out_specs=(whole(), whole()),
        ),
        out_shape=(struct((half, depth), LOW), struct((8, depth), WIDE)),
        compiler_params=params(16),
        cost_estimate=cost(1),
        name="grad_normed",
    )(scalar, grads, tokens, weights, ahead)


def turned_sums(sums):
    blank = jnp.zeros((LANES - sums.shape[0], sums.shape[1]), WIDE)
    return jnp.transpose(jnp.concatenate([sums, blank], axis=0))


def project_back_kernel(scalar_ref, grads_ref, normed_ref, outs_ref, *refs, given):
    outs = refs[given:]
    grads = jnp.transpose(multiply(grads_ref[...], normed_ref[...])).astype(LOW)
    value = [grads, outs_ref[...]] + [turned_sums(ref[...]).astype(LOW) for ref in refs[:given]]
    value = jnp.concatenate(value, axis=1)
    put_shards(scalar_ref[3], outs, value, slice(0, value.shape[1]))


def project_back(scalar, grads, normed, outs_grad, sums, batch):
    width = grads.shape[0]
    depth = normed.shape[1]
    shapes = shard_shapes(batch, depth, width + outs_grad.shape[1] + LANES * len(sums))
    return pl.pallas_call(
        functools.partial(project_back_kernel, given=len(sums)),
        in_specs=[scalars()] + [whole()] * (3 + len(sums)),
        out_specs=(whole(),) * len(shapes),
        out_shape=shapes,
        compiler_params=params(16),
        cost_estimate=cost(1),
        name="projection_weights",
    )(scalar, grads, normed, outs_grad, *sums)


def finish_kernel(scalar_ref, mine_ref, other_ref, *refs, sizes, half):
    hidden_refs, owns, full_ref = refs[: len(sizes)], refs[len(sizes) : -1], refs[-1]
    hidden = jnp.concatenate([ref[...] for ref in hidden_refs], axis=0)
    row = lax.broadcasted_iota(jnp.int32, (half, 1), 0) + scalar_ref[0] * half
    branch = mine_ref[...].astype(WIDE) + other_ref[...].astype(WIDE)
    low = jnp.where(row < scalar_ref[1], hidden + branch, 0.0).astype(LOW)
    full_ref[...] = low
    for k, own_ref in enumerate(owns):
        own_ref[...] = low[k * STEP : (k + 1) * STEP, :]


def finish(scalar, mine, other, hiddens, count):
    half, depth = mine.shape
    sizes = tuple(hidden.shape[0] for hidden in hiddens)
    parts = half // STEP
    return pl.pallas_call(
        functools.partial(finish_kernel, sizes=sizes, half=half),
        grid_spec=pltpu.PrefetchScalarGridSpec(
            num_scalar_prefetch=1,
            grid=(1,),
            in_specs=[whole()] * (2 + len(sizes)),
            out_specs=(whole(),) * parts
            + (pl.BlockSpec((half, depth), lambda i, scalar_ref: (scalar_ref[0], 0)),),
        ),
        out_shape=(stored_far((STEP, depth), LOW),) * parts + (stored_far((count, depth), LOW),),
        compiler_params=params(16),
        cost_estimate=cost(1),
        name="layer_out",
    )(scalar, mine, other, *(far(hidden) for hidden in hiddens))


def first_back_kernel(scalar_ref, mine_ref, other_ref, tokens_ref, grad_ref, rows_ref, *refs):
    own_ref, full_ref = refs[-2:]
    grad_normed = mine_ref[...].astype(WIDE) + other_ref[...].astype(WIDE)
    scaled, inverse = standardize(tokens_ref[...].astype(WIDE))
    grad = grad_ref[...].astype(WIDE) + standardize_back(grad_normed, scaled, inverse, rows_ref[0:1, :])
    low = grad.astype(LOW)
    own_ref[...] = low
    full_ref[...] = low


def first_back(scalar, mine, other, tokens, grad, rows, number, stored):
    size, depth = mine.shape
    count = tokens.shape[0]
    blocks = count // 2 // size

    def placed(i, scalar_ref):
        return (number + scalar_ref[0] * blocks, 0)

    return pl.pallas_call(
        first_back_kernel,
        grid_spec=pltpu.PrefetchScalarGridSpec(
            num_scalar_prefetch=1,
            grid=(1,),
            in_specs=[whole(), whole()]
            + [pl.BlockSpec((size, depth), placed)] * 2
            + [whole()]
            + [pl.BlockSpec(memory_space=pl.ANY)] * len(stored),
            out_specs=(whole(), pl.BlockSpec((size, depth), placed)),
        ),
        out_shape=(stored_far((size, depth), LOW), stored_far((count, depth), LOW)),
        input_output_aliases={6: 1} if stored else {},
        compiler_params=params(12),
        cost_estimate=cost(1),
        name="first_norm_backward",
    )(scalar, mine, other, tokens, grad, rows, *stored)


def place_kernel(scalar_ref, *refs, parts):
    first_refs, second_refs = refs[:parts], refs[parts : 2 * parts]
    for k in range(parts):

        @pl.when(pl.program_id(0) == k)
        def _():
            refs[-2][...] = first_refs[k][...]
            refs[-1][...] = second_refs[k][...]


def place(scalar, first, second, targets):
    parts = len(first)
    rows, depth = first[0].shape
    placed = pl.BlockSpec((rows, depth), lambda i, scalar_ref: (i + (1 - scalar_ref[0]) * parts, 0))
    return pl.pallas_call(
        functools.partial(place_kernel, parts=parts),
        grid_spec=pltpu.PrefetchScalarGridSpec(
            num_scalar_prefetch=1,
            grid=(parts,),
            in_specs=[whole()] * (2 * parts) + [pl.BlockSpec(memory_space=pl.ANY)] * 2,
            out_specs=(placed, placed),
        ),
        out_shape=tuple(stored_far(value.shape, value.dtype) for value in targets),
        input_output_aliases={1 + 2 * parts: 0, 2 + 2 * parts: 1},
        compiler_params=params(12),
        cost_estimate=cost(1),
        name="place",
    )(scalar, *first, *second, *targets)


def total_kernel(*refs, parts, bounds, flips):
    parts_refs, outs = refs[:parts], refs[parts:]
    if parts == 1:
        pieces = [parts_refs[0][k] for k in range(parts_refs[0].shape[0])]
    else:
        pieces = [ref[...] for ref in parts_refs]
    total = pieces[0].astype(WIDE)
    for piece in pieces[1:]:
        total = total + piece.astype(WIDE)
    for out, (first, last), flip in zip(outs, bounds, flips):
        piece = total[:, first:last]
        out[...] = jnp.transpose(piece) if flip else piece


def total_parts(parts, bounds, flips, guess):
    rows = parts[0].shape[-2]
    shapes = []
    for (first, last), flip in zip(bounds, flips):
        shape = (last - first, rows) if flip else (rows, last - first)
        shapes.append(struct(shape, WIDE))
    return pl.pallas_call(
        functools.partial(total_kernel, parts=len(parts), bounds=bounds, flips=flips),
        in_specs=[whole()] * len(parts),
        out_specs=(whole(),) * len(shapes),
        out_shape=tuple(shapes),
        compiler_params=params(8),
        cost_estimate=cost(guess),
        name="total",
    )(*parts)


def exchange_far(scalar, shards, ahead=(), sums=()):
    if len(shards) == 1:
        size = lax.axis_size("batch")
        parts = shards[0].reshape(size, shards[0].shape[0] // size, shards[0].shape[1])
        return [lax.all_to_all(parts, "batch", 0, 0, tiled=True)]
    pieces = fold(scalar, after(shards[0], *ahead), shards[1], sums)
    return [pieces[0]] + [swap(piece, "batch", 2 * k) for k, piece in enumerate(pieces) if k > 0]


def exchange_near(shards):
    return shards if len(shards) == 1 else (shards[0], swap(shards[1], "batch", 1))


def per_device(tokens, lengths, w_query, w_key, w_value, w_out, w_up, w_down, norm_gain, norm_shift, out_grad):
    count, depth = tokens.shape
    batch = lax.axis_size("batch")
    if lengths.shape[0] != 1 or lax.axis_size("tensor") != 4:
        raise ValueError("unsupported mesh")
    width = w_query.shape[1]
    units = w_up.shape[1]
    tensor = lax.axis_index("tensor").astype(jnp.int32)
    core = tensor & 1
    scalar = jnp.stack([core, lengths[0], tensor >> 1, lax.axis_index("batch").astype(jnp.int32)])
    sure = 2 * count // 3
    half = count // 2
    first = half // 3 * 2
    chunks = ((0, first), (first, half - first))

    if batch == 8:
        early = pack(w_query, w_key, w_value, w_out, norm_gain, norm_shift)
    else:
        blank = jnp.zeros((w_query.shape[0], -(4 * width + 4) % LANES), LOW)
        early = jnp.concatenate([w_query, w_key, w_value, w_out.T, norm_gain.T, norm_shift.T, blank], axis=1)
    late = jnp.concatenate([w_up, w_down.T], axis=1)
    if batch == 8:
        others = gather_far(early)
        early = [early, swap(early, "batch", 1)]
        early += [others[0], swap(others[0], "batch", 1)]
        early += [others[1], swap(after(others[1], early[1], early[3]), "batch", 1)]
        early += [others[2], swap(others[2], "batch", 1)]
        late = after(late, *others, early[1], early[3], early[5])
        near = swap(late, "batch", 2)
        middle = swap(late, "batch", 4)
        beside = swap(late, "batch", 1)
    else:
        early = [lax.all_gather(early, "batch", axis=0, tiled=True)]
        late = [lax.all_gather(late, "batch", axis=0, tiled=True)]

    normed, projected, rows, weights, own_outs = project(scalar, tokens, early, width)
    across = swap(own_outs, "tensor", 2)
    outs = (own_outs, across, swap(own_outs, "tensor", 1), swap(across, "tensor", 1))
    mixed, sums, pieces = [], [], []
    if batch == 8:
        late = [late, beside, near, swap(after(near, own_outs), "batch", 1)]
    for number, (begin, size) in enumerate(chunks):
        local = tuple(range(begin // BLOCK, (begin + size) // BLOCK))
        if number == 1:
            projected = after(projected, *late[3:4])
        part, logs = attend(scalar, projected, local + tuple(k + half // BLOCK for k in local), sure)
        projected = after(projected, part)
        mixed.append(part)
        sums.append(logs)
        across = swap(part, "tensor", 2)
        pieces.append((part, across, swap(part, "tensor", 1), swap(across, "tensor", 1)))
        if number == 0 and batch == 8:
            middle = after(middle, part)
            late += [middle, swap(middle, "batch", 1)]
            last = swap(middle, "batch", 2)
    if batch == 8:
        last = after(last, part)
        late += [last, swap(last, "batch", 1)]
    late = lax.optimization_barrier((*late, *mixed))[: len(late)]
    full_up, full_down = assemble(scalar, late, units)
    rows = after(rows, *pieces[-1][1:])

    stored, sends = [], []
    twos, halves, hiddens = jnp.zeros((8, depth), WIDE), [], []
    for (begin, size), piece in zip(chunks, pieces):
        back, twos, *stored = feed(
            scalar, tokens, out_grad, piece, outs, full_up, full_down, rows, twos, stored, begin, size, False
        )
        sends.append(back)
    for (begin, size), piece, send in zip(chunks, pieces, sends):
        rows = after(rows, *(mine for mine, _ in halves))
        back, twos, *stored = feed(
            scalar, tokens, out_grad, piece, outs, full_up, full_down, rows, twos, stored, begin, size, True
        )
        hiddens.append(stored.pop())
        mine = (back.astype(WIDE) + swap(send, "tensor", 1).astype(WIDE)).astype(LOW)
        halves.append((mine, swap(mine, "tensor", 2)))
    normed_two, active, upper = stored
    normed_two = after(normed_two, *(mine for mine, _ in halves))
    branch_keep, branch_send, *feed_grads = weigh(scalar, normed_two, upper, active, out_grad, full_down, 0)
    feed_parts = exchange_far(scalar, feed_grads)

    beside = swap(branch_send, "tensor", 1)
    grads = []
    for (begin, size), (mine, other), hidden in zip(chunks, halves, hiddens):
        mine = after(mine, *feed_grads)
        low = second_back(scalar, mine, other, hidden, out_grad, rows, begin, 40000 if grads else 1)
        grads += [low, swap(low, "tensor", 1)]
    branch_mine = (branch_keep.astype(WIDE) + beside.astype(WIDE)).astype(LOW)
    branch_mine = after(branch_mine, halves[0][1])
    branch_other = swap(branch_mine, "tensor", 2)
    projected = after(projected, branch_mine)
    attend_grads, outs_grad, grad_attn = attend_back(
        scalar, projected, own_outs, mixed, sums, grads, chunks, sure
    )

    there = (1 - core) * half
    ends = []
    if batch == 8:
        project_grads = exchange_near(project_back(scalar, attend_grads, normed, outs_grad, (), batch))
        attend_grads = after(attend_grads, project_grads[0])
    for keep in (False, True):
        back, twos = inward(scalar, attend_grads, tokens, weights, twos, keep)
        ends.append(back)
    if batch == 8:
        sums = (twos, swap(twos, "batch", 1))
    else:
        project_grads = project_back(scalar, attend_grads, normed, outs_grad, (twos,), batch)
        sums = ()
    keep = after(ends[1], branch_other)
    beside = swap(ends[0], "tensor", 1)
    tails = []
    for begin in range(0, half, STEP):
        part = slice(begin, begin + STEP)
        mine = (keep[part].astype(WIDE) + beside[part].astype(WIDE)).astype(LOW)
        tails.append((mine, swap(mine, "tensor", 2)))
    *own_out, layer_out = finish(scalar, branch_mine, after(branch_other, tails[-1][0]), hiddens, count)
    project_parts = exchange_far(scalar, project_grads, own_out, sums)
    other_out = [swap(own, "tensor", 1) for own in own_out]
    stored, other_grads = [], []
    for number, (mine, other) in enumerate(tails):
        mine = after(mine, *own_out)
        own_grad, *stored = first_back(scalar, mine, other, tokens, grad_attn, rows, number, stored)
        other_grads.append(swap(own_grad, "tensor", 1))
    feed_parts[0] = after(feed_parts[0], own_grad)
    shard_up, shard_down = total_parts(feed_parts, ((0, units), (units, 2 * units)), (False, False), 1)
    last = 4 * width
    project_parts[0] = after(project_parts[0], shard_up)
    (small,) = total_parts(project_parts, ((last, last + LANES),), (True,), 40000)
    small = small[:8]
    across = swap(small, "tensor", 2)
    project_parts[0] = after(project_parts[0], small)
    shard_query, shard_key, shard_value, shard_out = total_parts(
        project_parts,
        ((0, width), (width, 2 * width), (2 * width, 3 * width), (3 * width, last)),
        (False, False, False, True),
        1,
    )
    small = small + after(across, shard_query)
    across = swap(small, "tensor", 1)
    other_grads[0] = after(other_grads[0], small)
    layer_out, grad_input = place(scalar, other_out, other_grads, (layer_out, stored[0]))
    small = small + after(across, grad_input)
    shard_gain = jnp.stack([small[0], small[2]])
    shard_shift = jnp.stack([small[1], small[3]])
    return (
        layer_out,
        grad_input,
        shard_query,
        shard_key,
        shard_value,
        shard_out,
        shard_up,
        shard_down.T,
        shard_gain,
        shard_shift,
    )


def solution(mesh):
    tall = P("batch", "tensor")
    wide = P("tensor", "batch")
    rows = P("batch", None)
    pair = P(None, "batch")
    return jax.shard_map(
        per_device,
        mesh=mesh,
        in_specs=(rows, P("batch"), tall, tall, tall, wide, tall, wide, pair, pair, rows),
        out_specs=(rows, rows, tall, tall, tall, wide, tall, wide, pair, pair),
        check_vma=False,
    )
```

```python
import functools

import jax
import jax.numpy as jnp
from jax import lax
from jax.experimental import pallas as pl
from jax.experimental.pallas import tpu as pltpu
from jax.sharding import PartitionSpec as P

HD = 64
EPSILON = 1e-05
LOG2E = 1.4426950408889634
HUGE = 3e38
FAR = -1e30
LOW = jnp.bfloat16
WIDE = jnp.float32
LANES = 128
BLOCK = 256
STEP = 384


def multiply(left, right):
    return lax.dot_general(left, right, (((1,), (0,)), ((), ())), preferred_element_type=WIDE)


def outer_cols(left, right):
    return lax.dot_general(left, right, (((1,), (1,)), ((), ())), preferred_element_type=WIDE)


def inner_rows(left, right):
    return lax.dot_general(left, right, (((0,), (0,)), ((), ())), preferred_element_type=WIDE)


def whole():
    return pl.BlockSpec(memory_space=pltpu.VMEM)


def scalars():
    return pl.BlockSpec(memory_space=pltpu.SMEM)


def struct(shape, dtype):
    return jax.ShapeDtypeStruct(shape, dtype)


def held(shape, dtype):
    return pltpu.VMEM(shape, dtype)


def stored_far(shape, dtype):
    return pltpu.HBM(shape, dtype)


def far(value):
    return pltpu.with_memory_space_constraint(value, pltpu.HBM)


def params(mebibytes):
    return pltpu.CompilerParams(vmem_limit_bytes=mebibytes << 20)


def cost(microseconds):
    return pl.CostEstimate(flops=int(microseconds * 1.1e6), bytes_accessed=0, transcendentals=0)


def after(value, *others):
    return lax.optimization_barrier((value, *others))[0]


def swap(value, axis, bits):
    size = lax.axis_size(axis)
    return lax.ppermute(value, axis, [(i, i ^ bits) for i in range(size)])


def gather_far(shard):
    return [swap(shard, "batch", bits) for bits in (2, 4, 6)]


def pair_sum(keep, send):
    mine = (keep.astype(WIDE) + swap(send, "tensor", 1).astype(WIDE)).astype(LOW)
    return mine, swap(mine, "tensor", 2)


def standardize(values):
    middle = jnp.mean(values, axis=-1, keepdims=True)
    centred = values - middle
    spread = jnp.mean(centred * centred, axis=-1, keepdims=True)
    inverse = lax.rsqrt(spread + EPSILON)
    return centred * inverse, inverse


def standardize_back(grad, scaled, inverse, gain):
    grad = grad * gain
    mean_grad = jnp.mean(grad, axis=-1, keepdims=True)
    mean_cross = jnp.mean(grad * scaled, axis=-1, keepdims=True)
    return inverse * (grad - mean_grad - scaled * mean_cross)


def collect(index, pieces, scratch):
    count = pieces[0].shape[0]
    for bits, piece in enumerate(pieces):
        at = pl.multiple_of((index ^ bits) * count, 32) if len(pieces) > 1 else 0
        scratch[pl.ds(at, count), :] = piece[...]


def pack_kernel(query_ref, key_ref, value_ref, outs_ref, gain_ref, shift_ref, out_ref):
    width = query_ref.shape[1]
    out_ref[:, :width] = query_ref[...]
    out_ref[:, width : 2 * width] = key_ref[...]
    out_ref[:, 2 * width : 3 * width] = value_ref[...]
    out_ref[:, 3 * width : 4 * width] = jnp.transpose(outs_ref[...].astype(WIDE)).astype(LOW)
    rows = [gain_ref[...].astype(WIDE), shift_ref[...].astype(WIDE)]
    rows.append(jnp.zeros((LANES - 4, gain_ref.shape[1]), WIDE))
    out_ref[:, 4 * width :] = jnp.transpose(jnp.concatenate(rows, axis=0)).astype(LOW)


def pack(*shards):
    rows, width = shards[0].shape
    return pl.pallas_call(
        pack_kernel,
        grid=(1,),
        in_specs=[pl.BlockSpec(shard.shape, lambda i: (0, 0)) for shard in shards],
        out_specs=whole(),
        out_shape=struct((rows, 4 * width + LANES), LOW),
        compiler_params=params(4),
        cost_estimate=cost(1),
        name="pack",
    )(*(far(shard) for shard in shards))


def project_kernel(scalar_ref, *refs, parts, width, block):
    pieces, refs = refs[:parts], refs[parts:]
    tokens_ref, normed_ref, projected_ref, rows_ref, weights_ref, outs_ref = refs

    @pl.when(pl.program_id(0) == 0)
    def _():
        collect(scalar_ref[3], pieces, weights_ref)
        rows_ref[...] = jnp.transpose(weights_ref[:, 4 * width : 4 * width + LANES].astype(WIDE))[:8, :]
        outs_ref[...] = jnp.transpose(weights_ref[:, 3 * width : 4 * width])

    for k in range(tokens_ref.shape[0] // block):
        part = slice(k * block, (k + 1) * block)
        scaled, _ = standardize(tokens_ref[part, :].astype(WIDE))
        normed = (scaled * rows_ref[0:1, :] + rows_ref[2:3, :]).astype(LOW)
        normed_ref[part, :] = normed
        projected_ref[part, :] = multiply(normed, weights_ref[:, : 3 * width]).astype(LOW)


def project(scalar, tokens, pieces, width):
    count, depth = tokens.shape
    total = pieces[0].shape[1]
    step = 768
    return pl.pallas_call(
        functools.partial(project_kernel, parts=len(pieces), width=width, block=256),
        grid=(count // step,),
        in_specs=[scalars()]
        + [whole()] * len(pieces)
        + [pl.BlockSpec((step, depth), lambda i: (i, 0))],
        out_specs=(
            pl.BlockSpec((step, depth), lambda i: (i, 0)),
            pl.BlockSpec((step, 3 * width), lambda i: (i, 0)),
            pl.BlockSpec((8, depth), lambda i: (0, 0)),
            pl.BlockSpec((depth, total), lambda i: (0, 0)),
            pl.BlockSpec((width, depth), lambda i: (0, 0)),
        ),
        out_shape=(
            stored_far((count, depth), LOW),
            struct((count, 3 * width), LOW),
            struct((8, depth), WIDE),
            struct((depth, total), LOW),
            struct((width, depth), LOW),
        ),
        compiler_params=params(20),
        cost_estimate=cost(4),
        name="project",
    )(scalar, *pieces, pltpu.with_memory_space_constraint(tokens, pltpu.HBM))


def assemble_kernel(scalar_ref, *refs, parts, units):
    pieces, (up_ref, down_ref) = refs[:parts], refs[parts:]
    count = pieces[0].shape[0]
    for bits, piece in enumerate(pieces):
        at = pl.multiple_of((scalar_ref[3] ^ bits) * count, 32) if parts > 1 else 0
        up_ref[pl.ds(at, count), :] = piece[:, :units]
        down_ref[pl.ds(at, count), :] = piece[:, units:]


def assemble(scalar, pieces, units):
    depth = sum(piece.shape[0] for piece in pieces)
    return pl.pallas_call(
        functools.partial(assemble_kernel, parts=len(pieces), units=units),
        in_specs=[scalars()] + [whole()] * len(pieces),
        out_specs=(whole(),) * 2,
        out_shape=(struct((depth, units), LOW), struct((depth, units), LOW)),
        compiler_params=params(10),
        cost_estimate=cost(1),
        name="assemble",
    )(scalar, *pieces)


def sign_of(scores):
    scores = scores.astype(LOW) * LOW(HUGE)
    return jnp.minimum(jnp.maximum(scores, LOW(-1)), LOW(1))


def attend_kernel(scalar_ref, projected_ref, mixed_ref, sums_ref, *, places, heads, sure):
    length = scalar_ref[1]
    factor = LOG2E * HD**-0.5
    width = heads * HD
    for i, place in enumerate(places):
        row0 = place * BLOCK
        here = slice(row0, row0 + BLOCK)
        row = lax.broadcasted_iota(jnp.int32, (BLOCK, 1), 0) + row0
        key = lax.broadcasted_iota(jnp.int32, (BLOCK, BLOCK), 1) + row0
        allowed = key <= jnp.minimum(row, length - 1)
        def each(function):
            return jnp.concatenate([function(h) for h in range(heads)], axis=0)

        def column(kind, h):
            return slice(kind * width + h * HD, kind * width + (h + 1) * HD)

        def split(value, h):
            return value[h * BLOCK : (h + 1) * BLOCK]

        until = slice(0, row0 + BLOCK)
        scores = each(lambda h: outer_cols(projected_ref[here, column(0, h)], projected_ref[until, column(1, h)]))
        reach = jnp.abs(scores) * factor
        near = jnp.where(jnp.concatenate([allowed] * heads, axis=0), reach[:, row0:], FAR)
        if row0 > 0:
            past = reach[:, :row0]
            if row0 > sure:
                past_key = lax.broadcasted_iota(jnp.int32, (1, row0), 1)
                past = jnp.where(past_key < length, past, FAR)
            near = jnp.concatenate([past, near], axis=1)
        top = jnp.max(near, axis=1, keepdims=True)
        prob = jnp.exp2(near - top)
        signed = prob.astype(LOW) * sign_of(scores)
        total = jnp.sum(prob, axis=1, keepdims=True)
        mixed = each(lambda h: multiply(split(signed, h), projected_ref[until, column(2, h)]))
        mixed = (mixed / total).astype(LOW)
        logs = top + jnp.log2(total)
        outs = [split(mixed, h) for h in range(heads)]
        sums = [split(logs, h) for h in range(heads)]
        part = slice(i * BLOCK, (i + 1) * BLOCK)
        mixed_ref[:, part] = jnp.transpose(jnp.concatenate(outs, axis=1))
        blank = jnp.zeros((BLOCK, LANES - heads), WIDE)
        sums_ref[i] = jnp.transpose(jnp.concatenate(sums + [blank], axis=1))[:8, :]


def attend(scalar, projected, places, sure):
    width = projected.shape[1] // 3
    heads = width // HD
    return pl.pallas_call(
        functools.partial(attend_kernel, places=places, heads=heads, sure=sure),
        in_specs=[scalars(), whole()],
        out_specs=(whole(), whole()),
        out_shape=(struct((width, len(places) * BLOCK), LOW), struct((len(places), 8, BLOCK), WIDE)),
        compiler_params=params(16),
        cost_estimate=cost(1),
        name="attend_forward",
    )(scalar, projected)


def attend_back_kernel(scalar_ref, *refs, chunks, rows, heads, sure):
    length = scalar_ref[1]
    core = scalar_ref[0]
    projected_ref, outs_ref, refs = refs[0], refs[1], refs[2:]
    mixed_refs, refs = refs[: len(chunks)], refs[len(chunks) :]
    sums_refs, refs = refs[: len(chunks)], refs[len(chunks) :]
    grad_refs, refs = refs[: 2 * len(chunks)], refs[2 * len(chunks) :]
    grads_ref, outs_grad_ref, whole_ref, grad_mixed, delta, logs, dq_turned = refs
    scaling = HD**-0.5
    factor = LOG2E * scaling
    width = heads * HD
    blocks = rows // BLOCK
    outs_grad = jnp.zeros(outs_ref.shape, WIDE)
    half = blocks // 2
    for number, (begin, size) in enumerate(chunks):
        for side in range(2):
            for k in range(size // BLOCK):
                local = side * size + k * BLOCK
                inside = slice(local, local + BLOCK)
                i = side * half + begin // BLOCK + k
                rows_i = slice(i * BLOCK, (i + 1) * BLOCK)
                mine = grad_refs[2 * number][k * BLOCK : (k + 1) * BLOCK, :]
                other = grad_refs[2 * number + 1][k * BLOCK : (k + 1) * BLOCK, :]

                @pl.when(core == side)
                def _():
                    whole_ref[rows_i, :] = mine

                @pl.when(core != side)
                def _():
                    whole_ref[rows_i, :] = other

                grad = whole_ref[rows_i, :]
                mixed = mixed_refs[number][:, inside]
                outs_grad = outs_grad + multiply(mixed, grad)
                turned = outer_cols(outs_ref[...], grad)
                grad_mixed[rows_i, :] = jnp.transpose(turned).astype(LOW)
                logs[:, rows_i] = sums_refs[number][local // BLOCK]
                both = turned.astype(LOW).astype(WIDE) * mixed.astype(WIDE)
                for h in range(heads):
                    delta[h : h + 1, rows_i] = jnp.sum(both[h * HD : (h + 1) * HD, :], axis=0, keepdims=True)
    outs_grad_ref[...] = jnp.transpose(outs_grad).astype(LOW)
    for j in range(blocks):
        here = slice(j * BLOCK, (j + 1) * BLOCK)
        later = slice((j + 1) * BLOCK, rows)
        dks, dvs = [], []
        for h in range(heads):
            cols = slice(h * HD, (h + 1) * HD)
            k = projected_ref[here, width + h * HD : width + (h + 1) * HD]
            v = projected_ref[here, 2 * width + h * HD : 2 * width + (h + 1) * HD]
            part = slice(j * BLOCK, rows)
            q = projected_ref[part, cols]
            g = grad_mixed[part, cols]
            scores = outer_cols(k, q)
            grad_weights = outer_cols(v, g)
            reach = jnp.abs(scores) * factor - logs[h : h + 1, part]
            key = lax.broadcasted_iota(jnp.int32, (BLOCK, 1), 0) + j * BLOCK
            row = lax.broadcasted_iota(jnp.int32, (1, BLOCK), 1) + j * BLOCK
            near = jnp.where(key <= jnp.minimum(row, length - 1), reach[:, :BLOCK], FAR)
            if part.stop > (j + 1) * BLOCK:
                past = reach[:, BLOCK:]
                if (j + 1) * BLOCK > sure:
                    past = jnp.where(key < length, past, FAR)
                near = jnp.concatenate([near, past], axis=1)
            sign = sign_of(scores)
            weights = jnp.exp2(near)
            signed = sign.astype(WIDE)
            raw = (weights * (grad_weights - signed * delta[h : h + 1, part])).astype(LOW) * (sign * sign)
            dv = multiply(weights.astype(LOW) * sign, g)
            dk = multiply(raw, q)
            more = inner_rows(k, raw)
            if j == 0:
                dq_turned[cols, part] = more
            else:
                dq_turned[cols, part] += more
            dks.append(dk * scaling)
            dvs.append(dv)
        grads_ref[:width, here] = (dq_turned[:, here] * scaling).astype(LOW)
        grads_ref[width : 2 * width, here] = jnp.transpose(jnp.concatenate(dks, axis=1)).astype(LOW)
        grads_ref[2 * width :, here] = jnp.transpose(jnp.concatenate(dvs, axis=1)).astype(LOW)


def attend_back(scalar, projected, outs, mixed, sums, grads, chunks, sure):
    rows = projected.shape[0]
    width = projected.shape[1] // 3
    depth = outs.shape[1]
    heads = width // HD
    return pl.pallas_call(
        functools.partial(attend_back_kernel, chunks=chunks, rows=rows, heads=heads, sure=sure),
        in_specs=[scalars()] + [whole()] * (2 + 4 * len(chunks)),
        out_specs=(whole(),) * 3,
        out_shape=(struct((3 * width, rows), LOW), struct((depth, width), LOW), struct((rows, depth), LOW)),
        scratch_shapes=[
            pltpu.VMEM((rows, width), LOW),
            pltpu.VMEM((8, rows), WIDE),
            pltpu.VMEM((8, rows), WIDE),
            pltpu.VMEM((width, rows), WIDE),
        ],
        compiler_params=params(24),
        cost_estimate=cost(8),
        name="attend_backward",
    )(scalar, projected, outs, *mixed, *sums, *grads)


def gelu_pair(up):
    root = 0.7978845608028654
    square = up * up
    bent = jnp.tanh(up * (root + (root * 0.044715) * square))
    half = 0.5 * bent + 0.5
    slope = half + (0.5 * up) * (1.0 - bent * bent) * (root + (3 * root * 0.044715) * square)
    return up * half, slope


def add_sums(sums_ref, ahead_ref, back, scaled, at):
    sums_ref[...] = ahead_ref[...]
    sums_ref[at : at + 1, :] += jnp.sum(back * scaled, axis=0, keepdims=True)
    sums_ref[at + 1 : at + 2, :] += jnp.sum(back, axis=0, keepdims=True)


def feed_kernel(scalar_ref, *refs, begin, size, half, keep, given):
    tokens_ref, grad_ref, m0, m1, m2, m3, o0, o1, o2, o3, up_ref, down_ref, rows_ref, ahead_ref = refs[:14]
    results = refs[14 + given : -1]
    back_ref, sums_ref, normed_ref, active_ref, upper_ref = results[:5]
    mixed_ref = refs[-1]
    place = scalar_ref[0] if keep else 1 - scalar_ref[0]
    row0 = pl.multiple_of(begin + place * half, BLOCK)
    here = pl.ds(row0, size)
    row = lax.broadcasted_iota(jnp.int32, (size, 1), 0) + row0

    @pl.when(scalar_ref[2] == 0)
    def _():
        across = inner_rows(m0[...], o0[...]) + inner_rows(m1[...], o1[...])
        mixed_ref[...] = across + inner_rows(m2[...], o2[...]) + inner_rows(m3[...], o3[...])

    @pl.when(scalar_ref[2] != 0)
    def _():
        across = inner_rows(m1[...], o1[...]) + inner_rows(m0[...], o0[...])
        mixed_ref[...] = across + inner_rows(m3[...], o3[...]) + inner_rows(m2[...], o2[...])

    hidden = tokens_ref[...].astype(WIDE) + mixed_ref[...]
    if keep:
        results[5][...] = hidden
    scaled, _ = standardize(hidden)
    normed = (scaled * rows_ref[1:2, :] + rows_ref[3:4, :]).astype(LOW)
    normed_ref[here, :] = normed
    grad = jnp.where(row < scalar_ref[1], grad_ref[...].astype(WIDE), 0.0).astype(LOW)
    back = jnp.zeros(hidden.shape, WIDE)
    units = up_ref.shape[1]
    for first in range(0, units, BLOCK):
        part = slice(first, first + BLOCK)
        active, slope = gelu_pair(multiply(normed, up_ref[:, part]))
        active_ref[here, part] = active.astype(LOW)
        upper = (multiply(grad, down_ref[:, part]) * slope).astype(LOW)
        upper_ref[here, part] = upper
        back = back + outer_cols(upper, up_ref[:, part])
    back_ref[...] = back.astype(LOW)
    add_sums(sums_ref, ahead_ref, back, scaled, 2)


def feed(scalar, tokens, out_grad, mixed, outs, up, down, rows, ahead, stored, begin, size, keep):
    count, depth = tokens.shape
    units = up.shape[1]
    width = outs[0].shape[0]
    half = count // 2

    def side(scalar_ref):
        return scalar_ref[0] if keep else 1 - scalar_ref[0]

    def placed(i, scalar_ref):
        return ((begin + side(scalar_ref) * half) // BLOCK * BLOCK, 0)

    def inside(i, scalar_ref):
        return (0, side(scalar_ref))

    rows_spec = pl.BlockSpec((pl.Element(size), pl.Element(depth)), placed)
    out_shape = (
        struct((size, depth), LOW),
        struct((8, depth), WIDE),
        struct((count, depth), LOW),
        struct((count, units), LOW),
        struct((count, units), LOW),
        (struct if begin else stored_far)((size, depth), WIDE),
    )[: 6 if keep else 5]
    return pl.pallas_call(
        functools.partial(feed_kernel, begin=begin, size=size, half=half, keep=keep, given=len(stored)),
        grid_spec=pltpu.PrefetchScalarGridSpec(
            num_scalar_prefetch=1,
            grid=(1,),
            in_specs=[rows_spec] * 2
            + [pl.BlockSpec((width, size), inside)] * 4
            + [whole()] * 8
            + [pl.BlockSpec(memory_space=pl.ANY)] * len(stored),
            out_specs=(whole(),) * len(out_shape),
            scratch_shapes=[pltpu.VMEM((size, depth), WIDE)],
        ),
        out_shape=out_shape,
        input_output_aliases={15 + k: 2 + k for k in range(len(stored))},
        compiler_params=params(20),
        cost_estimate=cost(size / 1000),
        name="feed_forward",
    )(scalar, tokens, out_grad, *mixed, *outs, up, down, rows, ahead, *stored)


def put_shards(index, outs, value, cols):
    if len(outs) == 1:
        outs[0][:, cols] = value
        return
    mine, other = outs
    rows = value.shape[0] // 8
    for place in range(8):
        piece = value[place * rows : (place + 1) * rows, :]

        @pl.when((index & 1) == place % 2)
        def _():
            mine[place // 2, :, cols] = piece

        @pl.when((index & 1) != place % 2)
        def _():
            other[place // 2, :, cols] = piece


def shard_shapes(batch, depth, cols):
    if batch != 8:
        return (stored_far((depth, cols), LOW),)
    return (struct((4, depth // 8, cols), LOW),) * 2


def weigh_kernel(scalar_ref, normed_ref, upper_ref, active_ref, grad_ref, down_ref, keep_ref, send_ref, *refs):
    outs, (up_sum, down_sum) = refs[:-2], refs[-2:]
    i = pl.program_id(0)
    units = down_ref.shape[1]
    half = grad_ref.shape[0]
    row0 = pl.multiple_of((scalar_ref[0] ^ 1 ^ i) * half, BLOCK)
    here = pl.ds(row0, half)
    row = lax.broadcasted_iota(jnp.int32, (half, 1), 0) + row0
    active = active_ref[here, :]
    branch = outer_cols(active, down_ref[...]).astype(LOW)
    grad = jnp.where(row < scalar_ref[1], grad_ref[...].astype(WIDE), 0.0).astype(LOW)
    up = inner_rows(normed_ref[here, :], upper_ref[here, :])
    down = inner_rows(grad, active)

    @pl.when(i == 0)
    def _():
        send_ref[...] = branch
        up_sum[...] = up
        down_sum[...] = down

    @pl.when(i == 1)
    def _():
        keep_ref[...] = branch
        put_shards(scalar_ref[3], outs, (up_sum[...] + up).astype(LOW), slice(0, units))
        put_shards(scalar_ref[3], outs, (down_sum[...] + down).astype(LOW), slice(units, 2 * units))


def weigh(scalar, normed, upper, active, out_grad, down, batch):
    count, depth = normed.shape
    units = down.shape[1]
    half = count // 2
    return pl.pallas_call(
        weigh_kernel,
        grid_spec=pltpu.PrefetchScalarGridSpec(
            num_scalar_prefetch=1,
            grid=(2,),
            in_specs=[whole()] * 3
            + [pl.BlockSpec((half, depth), lambda i, scalar_ref: (scalar_ref[0] ^ 1 ^ i, 0)), whole()],
            out_specs=(whole(),) * (2 + len(shard_shapes(batch, depth, 2 * units))),
            scratch_shapes=[pltpu.VMEM((depth, units), WIDE)] * 2,
        ),
        out_shape=(
            stored_far((half, depth), LOW),
            stored_far((half, depth), LOW),
            *shard_shapes(batch, depth, 2 * units),
        ),
        compiler_params=params(24),
        cost_estimate=cost(1),
        name="feed_forward_weights",
    )(scalar, normed, upper, active, out_grad, down)


def fold_kernel(scalar_ref, mine_ref, other_ref, *refs, given):
    place = scalar_ref[3] >> 1
    outs = refs[given:-1] if given else refs
    rows, cols = mine_ref.shape[1:]
    if given:
        refs[-1][...] = turned_sums(refs[0][...] + refs[1][...])
    for k, out in enumerate(outs):
        shard = place ^ k
        out[:, :cols] = (mine_ref[shard].astype(WIDE) + other_ref[shard].astype(WIDE)).astype(LOW)
        if given:
            at = pl.multiple_of((shard * 2 + (scalar_ref[3] & 1)) * rows, 32)
            out[:, cols:] = refs[-1][pl.ds(at, rows), :].astype(LOW)


def fold(scalar, mine, other, sums):
    count, rows, cols = mine.shape
    given = len(sums)
    cols += LANES if given else 0
    return pl.pallas_call(
        functools.partial(fold_kernel, given=given),
        in_specs=[scalars()] + [whole()] * (2 + given),
        out_specs=(whole(),) * count,
        out_shape=(struct((rows, cols), LOW),) * count,
        scratch_shapes=[pltpu.VMEM((sums[0].shape[1], LANES), WIDE)] if given else [],
        compiler_params=params(10),
        cost_estimate=cost(1),
        name="fold",
    )(scalar, mine, other, *sums)


def second_back_kernel(scalar_ref, mine_ref, other_ref, hidden_ref, grad_ref, rows_ref, low_ref, *, begin, half):
    size = low_ref.shape[0]
    row = lax.broadcasted_iota(jnp.int32, (size, 1), 0) + (begin + scalar_ref[0] * half)
    grad_normed = mine_ref[...].astype(WIDE) + other_ref[...].astype(WIDE)
    scaled, inverse = standardize(hidden_ref[...])
    grad = jnp.where(row < scalar_ref[1], grad_ref[...].astype(WIDE), 0.0)
    grad = grad + standardize_back(grad_normed, scaled, inverse, rows_ref[1:2, :])
    low_ref[...] = grad.astype(LOW)


def second_back(scalar, mine, other, hidden, out_grad, rows, begin, guess):
    size, depth = hidden.shape
    half = out_grad.shape[0] // 2
    placed = pl.BlockSpec(
        (pl.Element(size), pl.Element(depth)), lambda i, scalar_ref: ((begin + scalar_ref[0] * half) // BLOCK * BLOCK, 0)
    )
    return pl.pallas_call(
        functools.partial(second_back_kernel, begin=begin, half=half),
        grid_spec=pltpu.PrefetchScalarGridSpec(
            num_scalar_prefetch=1,
            grid=(1,),
            in_specs=[whole()] * 3 + [placed, whole()],
            out_specs=whole(),
        ),
        out_shape=struct((size, depth), LOW),
        compiler_params=params(14),
        cost_estimate=cost(guess),
        name="second_norm_backward",
    )(scalar, mine, other, hidden if begin else far(hidden), far(out_grad), rows)


def inward_kernel(scalar_ref, grads_ref, tokens_ref, weights_ref, ahead_ref, back_ref, sums_ref):
    width = grads_ref.shape[0]
    back = lax.dot_general(
        grads_ref[...], weights_ref[:, :width], (((0,), (1,)), ((), ())), preferred_element_type=WIDE
    )
    scaled, _ = standardize(tokens_ref[...].astype(WIDE))
    back_ref[...] = back.astype(LOW)
    add_sums(sums_ref, ahead_ref, back, scaled, 0)


def inward(scalar, grads, tokens, weights, ahead, keep):
    count, depth = tokens.shape
    width = grads.shape[0]
    half = count // 2

    def side(scalar_ref):
        return scalar_ref[0] if keep else 1 - scalar_ref[0]

    return pl.pallas_call(
        inward_kernel,
        grid_spec=pltpu.PrefetchScalarGridSpec(
            num_scalar_prefetch=1,
            grid=(1,),
            in_specs=[
                pl.BlockSpec((width, half), lambda i, scalar_ref: (0, side(scalar_ref))),
                pl.BlockSpec((half, depth), lambda i, scalar_ref: (side(scalar_ref), 0)),
                whole(),
                whole(),
            ],
            out_specs=(whole(), whole()),
        ),
        out_shape=(struct((half, depth), LOW), struct((8, depth), WIDE)),
        compiler_params=params(16),
        cost_estimate=cost(1),
        name="grad_normed",
    )(scalar, grads, tokens, weights, ahead)


def turned_sums(sums):
    blank = jnp.zeros((LANES - sums.shape[0], sums.shape[1]), WIDE)
    return jnp.transpose(jnp.concatenate([sums, blank], axis=0))


def project_back_kernel(scalar_ref, grads_ref, normed_ref, outs_ref, *refs, given):
    outs = refs[given:]
    grads = jnp.transpose(multiply(grads_ref[...], normed_ref[...])).astype(LOW)
    value = [grads, outs_ref[...]] + [turned_sums(ref[...]).astype(LOW) for ref in refs[:given]]
    value = jnp.concatenate(value, axis=1)
    put_shards(scalar_ref[3], outs, value, slice(0, value.shape[1]))


def project_back(scalar, grads, normed, outs_grad, sums, batch):
    width = grads.shape[0]
    depth = normed.shape[1]
    shapes = shard_shapes(batch, depth, width + outs_grad.shape[1] + LANES * len(sums))
    return pl.pallas_call(
        functools.partial(project_back_kernel, given=len(sums)),
        in_specs=[scalars()] + [whole()] * (3 + len(sums)),
        out_specs=(whole(),) * len(shapes),
        out_shape=shapes,
        compiler_params=params(16),
        cost_estimate=cost(1),
        name="projection_weights",
    )(scalar, grads, normed, outs_grad, *sums)


def finish_kernel(scalar_ref, mine_ref, other_ref, *refs, sizes, half):
    hidden_refs, owns, full_ref = refs[: len(sizes)], refs[len(sizes) : -1], refs[-1]
    hidden = jnp.concatenate([ref[...] for ref in hidden_refs], axis=0)
    row = lax.broadcasted_iota(jnp.int32, (half, 1), 0) + scalar_ref[0] * half
    branch = mine_ref[...].astype(WIDE) + other_ref[...].astype(WIDE)
    low = jnp.where(row < scalar_ref[1], hidden + branch, 0.0).astype(LOW)
    full_ref[...] = low
    for k, own_ref in enumerate(owns):
        own_ref[...] = low[k * STEP : (k + 1) * STEP, :]


def finish(scalar, mine, other, hiddens, count):
    half, depth = mine.shape
    sizes = tuple(hidden.shape[0] for hidden in hiddens)
    parts = half // STEP
    return pl.pallas_call(
        functools.partial(finish_kernel, sizes=sizes, half=half),
        grid_spec=pltpu.PrefetchScalarGridSpec(
            num_scalar_prefetch=1,
            grid=(1,),
            in_specs=[whole()] * (2 + len(sizes)),
            out_specs=(whole(),) * parts
            + (pl.BlockSpec((half, depth), lambda i, scalar_ref: (scalar_ref[0], 0)),),
        ),
        out_shape=(stored_far((STEP, depth), LOW),) * parts + (stored_far((count, depth), LOW),),
        compiler_params=params(16),
        cost_estimate=cost(1),
        name="layer_out",
    )(scalar, mine, other, *(far(hidden) for hidden in hiddens))


def first_back_kernel(scalar_ref, mine_ref, other_ref, tokens_ref, grad_ref, rows_ref, *refs):
    own_ref, full_ref = refs[-2:]
    grad_normed = mine_ref[...].astype(WIDE) + other_ref[...].astype(WIDE)
    scaled, inverse = standardize(tokens_ref[...].astype(WIDE))
    grad = grad_ref[...].astype(WIDE) + standardize_back(grad_normed, scaled, inverse, rows_ref[0:1, :])
    low = grad.astype(LOW)
    own_ref[...] = low
    full_ref[...] = low


def first_back(scalar, mine, other, tokens, grad, rows, number, stored):
    size, depth = mine.shape
    count = tokens.shape[0]
    blocks = count // 2 // size

    def placed(i, scalar_ref):
        return (number + scalar_ref[0] * blocks, 0)

    return pl.pallas_call(
        first_back_kernel,
        grid_spec=pltpu.PrefetchScalarGridSpec(
            num_scalar_prefetch=1,
            grid=(1,),
            in_specs=[whole(), whole()]
            + [pl.BlockSpec((size, depth), placed)] * 2
            + [whole()]
            + [pl.BlockSpec(memory_space=pl.ANY)] * len(stored),
            out_specs=(whole(), pl.BlockSpec((size, depth), placed)),
        ),
        out_shape=(stored_far((size, depth), LOW), stored_far((count, depth), LOW)),
        input_output_aliases={6: 1} if stored else {},
        compiler_params=params(12),
        cost_estimate=cost(1),
        name="first_norm_backward",
    )(scalar, mine, other, tokens, grad, rows, *stored)


def place_kernel(scalar_ref, *refs, parts):
    first_refs, second_refs = refs[:parts], refs[parts : 2 * parts]
    for k in range(parts):

        @pl.when(pl.program_id(0) == k)
        def _():
            refs[-2][...] = first_refs[k][...]
            refs[-1][...] = second_refs[k][...]


def place(scalar, first, second, targets):
    parts = len(first)
    rows, depth = first[0].shape
    placed = pl.BlockSpec((rows, depth), lambda i, scalar_ref: (i + (1 - scalar_ref[0]) * parts, 0))
    return pl.pallas_call(
        functools.partial(place_kernel, parts=parts),
        grid_spec=pltpu.PrefetchScalarGridSpec(
            num_scalar_prefetch=1,
            grid=(parts,),
            in_specs=[whole()] * (2 * parts) + [pl.BlockSpec(memory_space=pl.ANY)] * 2,
            out_specs=(placed, placed),
        ),
        out_shape=tuple(stored_far(value.shape, value.dtype) for value in targets),
        input_output_aliases={1 + 2 * parts: 0, 2 + 2 * parts: 1},
        compiler_params=params(12),
        cost_estimate=cost(1),
        name="place",
    )(scalar, *first, *second, *targets)


def total_kernel(*refs, parts, bounds, flips):
    parts_refs, outs = refs[:parts], refs[parts:]
    if parts == 1:
        pieces = [parts_refs[0][k] for k in range(parts_refs[0].shape[0])]
    else:
        pieces = [ref[...] for ref in parts_refs]
    total = pieces[0].astype(WIDE)
    for piece in pieces[1:]:
        total = total + piece.astype(WIDE)
    for out, (first, last), flip in zip(outs, bounds, flips):
        piece = total[:, first:last]
        out[...] = jnp.transpose(piece) if flip else piece


def total_parts(parts, bounds, flips, guess):
    rows = parts[0].shape[-2]
    shapes = []
    for (first, last), flip in zip(bounds, flips):
        shape = (last - first, rows) if flip else (rows, last - first)
        shapes.append(struct(shape, WIDE))
    return pl.pallas_call(
        functools.partial(total_kernel, parts=len(parts), bounds=bounds, flips=flips),
        in_specs=[whole()] * len(parts),
        out_specs=(whole(),) * len(shapes),
        out_shape=tuple(shapes),
        compiler_params=params(8),
        cost_estimate=cost(guess),
        name="total",
    )(*parts)


def exchange_far(scalar, shards, ahead=(), sums=()):
    if len(shards) == 1:
        size = lax.axis_size("batch")
        parts = shards[0].reshape(size, shards[0].shape[0] // size, shards[0].shape[1])
        return [lax.all_to_all(parts, "batch", 0, 0, tiled=True)]
    pieces = fold(scalar, after(shards[0], *ahead), shards[1], sums)
    return [pieces[0]] + [swap(piece, "batch", 2 * k) for k, piece in enumerate(pieces) if k > 0]


def exchange_near(shards):
    return shards if len(shards) == 1 else (shards[0], swap(shards[1], "batch", 1))


def per_device(tokens, lengths, w_query, w_key, w_value, w_out, w_up, w_down, norm_gain, norm_shift, out_grad):
    count, depth = tokens.shape
    batch = lax.axis_size("batch")
    if lengths.shape[0] != 1 or lax.axis_size("tensor") != 4:
        raise ValueError("unsupported mesh")
    width = w_query.shape[1]
    units = w_up.shape[1]
    tensor = lax.axis_index("tensor").astype(jnp.int32)
    core = tensor & 1
    scalar = jnp.stack([core, lengths[0], tensor >> 1, lax.axis_index("batch").astype(jnp.int32)])
    sure = 2 * count // 3
    half = count // 2
    first = half // 3 * 2
    chunks = ((0, first), (first, half - first))

    if batch == 8:
        early = pack(w_query, w_key, w_value, w_out, norm_gain, norm_shift)
    else:
        blank = jnp.zeros((w_query.shape[0], -(4 * width + 4) % LANES), LOW)
        early = jnp.concatenate([w_query, w_key, w_value, w_out.T, norm_gain.T, norm_shift.T, blank], axis=1)
    late = jnp.concatenate([w_up, w_down.T], axis=1)
    if batch == 8:
        others = gather_far(early)
        early = [early, swap(early, "batch", 1)]
        early += [others[0], swap(others[0], "batch", 1)]
        early += [others[1], swap(after(others[1], early[1], early[3]), "batch", 1)]
        early += [others[2], swap(others[2], "batch", 1)]
        late = after(late, *others, early[1], early[3], early[5])
        near = swap(late, "batch", 2)
        middle = swap(late, "batch", 4)
        beside = swap(late, "batch", 1)
    else:
        early = [lax.all_gather(early, "batch", axis=0, tiled=True)]
        late = [lax.all_gather(late, "batch", axis=0, tiled=True)]

    normed, projected, rows, weights, own_outs = project(scalar, tokens, early, width)
    across = swap(own_outs, "tensor", 2)
    outs = (own_outs, across, swap(own_outs, "tensor", 1), swap(across, "tensor", 1))
    mixed, sums, pieces = [], [], []
    if batch == 8:
        late = [late, beside, near, swap(after(near, own_outs), "batch", 1)]
    for number, (begin, size) in enumerate(chunks):
        local = tuple(range(begin // BLOCK, (begin + size) // BLOCK))
        if number == 1:
            projected = after(projected, *late[3:4])
        part, logs = attend(scalar, projected, local + tuple(k + half // BLOCK for k in local), sure)
        projected = after(projected, part)
        mixed.append(part)
        sums.append(logs)
        across = swap(part, "tensor", 2)
        pieces.append((part, across, swap(part, "tensor", 1), swap(across, "tensor", 1)))
        if number == 0 and batch == 8:
            middle = after(middle, part)
            late += [middle, swap(middle, "batch", 1)]
            last = swap(middle, "batch", 2)
    if batch == 8:
        last = after(last, part)
        late += [last, swap(last, "batch", 1)]
    late = lax.optimization_barrier((*late, *mixed))[: len(late)]
    full_up, full_down = assemble(scalar, late, units)
    rows = after(rows, *pieces[-1][1:])

    stored, sends = [], []
    twos, halves, hiddens = jnp.zeros((8, depth), WIDE), [], []
    for (begin, size), piece in zip(chunks, pieces):
        back, twos, *stored = feed(
            scalar, tokens, out_grad, piece, outs, full_up, full_down, rows, twos, stored, begin, size, False
        )
        sends.append(back)
    for (begin, size), piece, send in zip(chunks, pieces, sends):
        rows = after(rows, *(mine for mine, _ in halves))
        back, twos, *stored = feed(
            scalar, tokens, out_grad, piece, outs, full_up, full_down, rows, twos, stored, begin, size, True
        )
        hiddens.append(stored.pop())
        mine = (back.astype(WIDE) + swap(send, "tensor", 1).astype(WIDE)).astype(LOW)
        halves.append((mine, swap(mine, "tensor", 2)))
    normed_two, active, upper = stored
    normed_two = after(normed_two, *(mine for mine, _ in halves))
    branch_keep, branch_send, *feed_grads = weigh(scalar, normed_two, upper, active, out_grad, full_down, 0)
    feed_parts = exchange_far(scalar, feed_grads)

    beside = swap(branch_send, "tensor", 1)
    grads = []
    for (begin, size), (mine, other), hidden in zip(chunks, halves, hiddens):
        mine = after(mine, *feed_grads)
        low = second_back(scalar, mine, other, hidden, out_grad, rows, begin, 40000 if grads else 1)
        grads += [low, swap(low, "tensor", 1)]
    branch_mine = (branch_keep.astype(WIDE) + beside.astype(WIDE)).astype(LOW)
    branch_mine = after(branch_mine, halves[0][1])
    branch_other = swap(branch_mine, "tensor", 2)
    projected = after(projected, branch_mine)
    attend_grads, outs_grad, grad_attn = attend_back(
        scalar, projected, own_outs, mixed, sums, grads, chunks, sure
    )

    there = (1 - core) * half
    ends = []
    if batch == 8:
        project_grads = exchange_near(project_back(scalar, attend_grads, normed, outs_grad, (), batch))
        attend_grads = after(attend_grads, project_grads[0])
    for keep in (False, True):
        back, twos = inward(scalar, attend_grads, tokens, weights, twos, keep)
        ends.append(back)
    if batch == 8:
        sums = (twos, swap(twos, "batch", 1))
    else:
        project_grads = project_back(scalar, attend_grads, normed, outs_grad, (twos,), batch)
        sums = ()
    keep = after(ends[1], branch_other)
    beside = swap(ends[0], "tensor", 1)
    tails = []
    for begin in range(0, half, STEP):
        part = slice(begin, begin + STEP)
        mine = (keep[part].astype(WIDE) + beside[part].astype(WIDE)).astype(LOW)
        tails.append((mine, swap(mine, "tensor", 2)))
    *own_out, layer_out = finish(scalar, branch_mine, after(branch_other, tails[-1][0]), hiddens, count)
    project_parts = exchange_far(scalar, project_grads, own_out, sums)
    other_out = [swap(own, "tensor", 1) for own in own_out]
    stored, other_grads = [], []
    for number, (mine, other) in enumerate(tails):
        mine = after(mine, *own_out)
        own_grad, *stored = first_back(scalar, mine, other, tokens, grad_attn, rows, number, stored)
        other_grads.append(swap(own_grad, "tensor", 1))
    feed_parts[0] = after(feed_parts[0], own_grad)
    shard_up, shard_down = total_parts(feed_parts, ((0, units), (units, 2 * units)), (False, False), 1)
    last = 4 * width
    project_parts[0] = after(project_parts[0], shard_up)
    (small,) = total_parts(project_parts, ((last, last + LANES),), (True,), 40000)
    small = small[:8]
    across = swap(small, "tensor", 2)
    project_parts[0] = after(project_parts[0], small)
    shard_query, shard_key, shard_value, shard_out = total_parts(
        project_parts,
        ((0, width), (width, 2 * width), (2 * width, 3 * width), (3 * width, last)),
        (False, False, False, True),
        1,
    )
    small = small + after(across, shard_query)
    across = swap(small, "tensor", 1)
    other_grads[0] = after(other_grads[0], small)
    layer_out, grad_input = place(scalar, other_out, other_grads, (layer_out, stored[0]))
    small = small + after(across, grad_input)
    shard_gain = jnp.stack([small[0], small[2]])
    shard_shift = jnp.stack([small[1], small[3]])
    return (
        layer_out,
        grad_input,
        shard_query,
        shard_key,
        shard_value,
        shard_out,
        shard_up,
        shard_down.T,
        shard_gain,
        shard_shift,
    )


def solution(mesh):
    tall = P("batch", "tensor")
    wide = P("tensor", "batch")
    rows = P("batch", None)
    pair = P(None, "batch")
    return jax.shard_map(
        per_device,
        mesh=mesh,
        in_specs=(rows, P("batch"), tall, tall, tall, wide, tall, wide, pair, pair, rows),
        out_specs=(rows, rows, tall, tall, tall, wide, tall, wide, pair, pair),
        check_vma=False,
    )
```
